32 devices in a mesh: chain: 16 (over z, x, core), rep: 2 (over y).
Axes of the slice: x: 2, y: 2, z: 4, core: 2. Of those that a mesh axis runs over, the one named last changes fastest.
Arguments:
- spins: bfloat16 [24576, 256], P('chain'), may hold values from -1 to 1, as said below
- energies: bfloat16 [24576], P('chain'), may hold values from -150 to -70
- counts: int32 [16], P('chain'), may hold values from 1 to 1536, 12288 in all
- accepted: int32 [16, 1536], P('chain'), may hold values from 0 to 1535, each once within a row
- hidden_bias: bfloat16 [4096], P('rep'), may hold values from -3 to 3
- weights: bfloat16 [256, 4096], P(None, 'rep'), may hold values from -0.375 to 0.375
Outputs:
- update_visible: float32 [256], P('rep')
- update_hidden: float32 [4096], P('rep')
- update_weights: float32 [256, 4096], P('chain', 'rep')
The draws below stay inside these ranges and needn't reach their ends.
Inputs may be any that keep to these rules, and one draw needn't show every extreme that they name: `spins`: every entry is -1 or 1. The counts sum to 12288; at least one index of chain has 1536. Each row is a permutation of the slot numbers; its first counts entries name that index's accepted slots.
All inputs are finite; a program needn't handle non-finite values. No bound on the sum of `counts` on one device may be relied on, other than what follows from the above.
Results may differ from the reference program's by a relative error of at most 0.02.
Values may be sent and summed in bfloat16 or wider, within the bound.
A program may use at most 64 MiB of HBM per device.

```python
import math
import jax
import jax.numpy as jnp
import numpy as np
from jax import lax

N_SITES = 256
HIDDEN_SIZE = 4096
KEEP_DEV = 768
ITERS = 3
SLOTS_DEV = 1536
SLOTS_ALL = 24576
TOTAL = 12288
N_CHAIN = 16


def draw_spins(key, part):
    coin_flips = jax.random.randint(key, (SLOTS_ALL, N_SITES), 0, 2)
    return (2 * coin_flips - 1).astype(jnp.bfloat16)


def steps_of(stream_key, extent, split, smallest, largest):
    def one(dim, parts):
        steps = jax.random.uniform(jax.random.fold_in(jax.random.fold_in(stream_key, 6), dim), (parts,), jnp.float32, smallest / len(split), largest / len(split))
        return jnp.repeat(jnp.exp(steps), extent[dim] // parts).reshape((-1,) + (1,) * (len(extent) - dim - 1))

    level = one(*split[0])
    for cut in split[1:]:
        level = level * one(*cut)
    return level


def length_profile(amount, total, bound, slope):
    loads = [(1 << 20) // math.isqrt(grade ** slope) + 1 for grade in range(2, amount + 1)]
    rest, holding = total - bound - (amount - 1), [1] * (amount - 1)
    while rest > 0:
        movable = [i for i in range(amount - 1) if holding[i] < bound]
        whole, remaining = sum([loads[i] for i in movable]), rest
        for i in movable:
            more = min(bound - holding[i], max(1, remaining * loads[i] // whole), rest)
            holding[i] = holding[i] + more
            rest = rest - more
    return np.array([bound] + holding)


def uneven(stream_key, number_of, total, bound, skew):
    if number_of == 2:
        one = jax.random.randint(stream_key, (), max(1, total - bound), min(bound, total - 1) + 1)
        return jnp.stack([one, total - one])
    lengths = jnp.asarray(length_profile(number_of, total, bound, skew), jnp.int32)
    pairs = (number_of - 1) // 2
    giver, sink = lengths[1:1 + 2 * pairs:2], lengths[2:2 + 2 * pairs:2]
    room = jnp.minimum(giver - 1, bound - sink)
    passed = jax.random.randint(jax.random.fold_in(stream_key, 1), (pairs,), 0, 1 << 20) % (room + 1)
    lengths = lengths.at[1:1 + 2 * pairs:2].set(giver - passed).at[2:2 + 2 * pairs:2].set(sink + passed)
    return lengths[jax.random.permutation(jax.random.fold_in(stream_key, 2), number_of)]


def bell_draw(key, shape, deviation, most, cuts=(), held_as=jnp.bfloat16):
    gain = steps_of(key, shape, cuts, -0.22, 0.18) if cuts else 1.0
    entries = jax.random.normal(key, shape, jnp.float32) * deviation * gain
    return jnp.minimum(jnp.maximum(entries, -most), most).astype(held_as)


def setup_inputs(seed: int = 0) -> dict:
    keys = jax.random.split(jax.random.key(seed), 7)
    return {
        "spins": draw_spins(jax.random.fold_in(keys[6], 71), 0),
        "energies": jnp.clip(-150.0 + 80.0 * jax.random.uniform(keys[1], (SLOTS_ALL,), jnp.float32) ** steps_of(keys[1], (SLOTS_ALL,), ((0, 16),), -0.2, 0.2), -150.0, -70.0).astype(jnp.bfloat16),
        "counts": uneven(keys[2], N_CHAIN, TOTAL, SLOTS_DEV, 2).astype(jnp.int32),
        "accepted": jax.vmap(lambda own: jax.random.permutation(own, SLOTS_DEV))(jax.random.split(keys[3], N_CHAIN)).reshape((N_CHAIN, SLOTS_DEV)).astype(jnp.int32),
        "hidden_bias": bell_draw(keys[4], (HIDDEN_SIZE,), 0.5, 3.0, ((0, 2),)),
        "weights": bell_draw(keys[5], (N_SITES, HIDDEN_SIZE), N_SITES ** -0.5, 0.375, ((1, 2),)),
    }


PRECISE = lax.Precision.HIGHEST
DIAG_SHIFT = 0.05
EPSILON = 1e-06

def activations(block_spins, hidden_bias, weights):
    preact = hidden_bias.astype(jnp.float32) + jnp.dot(block_spins, weights, preferred_element_type=jnp.float32)
    return jnp.tanh(preact).astype(jnp.bfloat16)

def combine(base_vec, extra_vec, factor):
    return tuple((first + factor * second for first, second in zip(base_vec, extra_vec)))

def inner(first_vec, second_vec):
    return jnp.sum(first_vec[0] * second_vec[0]) + jnp.sum(first_vec[1] * second_vec[1]) + jnp.sum(first_vec[2] * second_vec[2])

def reference(spins, energies, counts, accepted, hidden_bias, weights):
    sample_total = KEEP_DEV * N_CHAIN
    counts = counts.astype(jnp.int32)
    offsets = (jnp.cumsum(counts) - counts).astype(jnp.int32)
    global_rows = jnp.arange(sample_total, dtype=jnp.int32)
    owner_chain = (lax.optimization_barrier(jnp.sum((offsets[None, :] <= global_rows[:, None]).astype(jnp.int32), axis=1)) - 1).astype(jnp.int32)
    within = global_rows - offsets[owner_chain]
    local_slot = accepted[owner_chain, within].astype(jnp.int32)
    source_slot = owner_chain * SLOTS_DEV + local_slot
    samples = spins[source_slot]
    energy = energies[source_slot].astype(jnp.float32)
    centered = energy - jnp.mean(energy)
    block_rows = math.gcd(sample_total, 512)
    block_count = sample_total // block_rows
    blocks = samples.reshape(block_count, block_rows, N_SITES)

    def pull(row_weight):
        weight_blocks = row_weight.reshape(block_count, block_rows)

        def block_sums(running, block_item):
            block_spins, weight_rows = block_item
            hidden_acts = activations(block_spins, hidden_bias, weights).astype(jnp.float32)
            spins_float = block_spins.astype(jnp.float32)
            weighted = hidden_acts * weight_rows[:, None]
            grad_vis = jnp.dot(weight_rows, spins_float, precision=PRECISE)
            grad_hid = lax.optimization_barrier(jnp.sum(weighted, axis=0))
            grad_mat = jnp.dot(spins_float.T, weighted, precision=PRECISE)
            return ((running[0] + grad_vis, running[1] + grad_hid, running[2] + grad_mat), None)
        initial = (jnp.zeros((N_SITES,), jnp.float32), jnp.zeros((HIDDEN_SIZE,), jnp.float32), jnp.zeros((N_SITES, HIDDEN_SIZE), jnp.float32))
        results, unused = lax.scan(block_sums, initial, (blocks, weight_blocks))
        return tuple((member / sample_total for member in results))

    def forward(vector):
        vis_part, hid_part, mat_part = vector

        def block_values(running, block_spins):
            hidden_acts = activations(block_spins, hidden_bias, weights).astype(jnp.float32)
            spins_float = block_spins.astype(jnp.float32)
            mixture = jnp.dot(spins_float, mat_part, precision=PRECISE)
            values = lax.optimization_barrier(jnp.sum(mixture * hidden_acts, axis=1)) + jnp.dot(hidden_acts, hid_part, precision=PRECISE) + jnp.dot(spins_float, vis_part, precision=PRECISE)
            return (running, values)
        unused, results = lax.scan(block_values, jnp.zeros((), jnp.float32), blocks)
        row_values = results.reshape(sample_total)
        return row_values - jnp.mean(row_values)
    force = pull(centered)
    solution = tuple((jnp.zeros_like(member) for member in force))
    residual = force
    direction = force
    resid_sq = inner(residual, residual)
    for iteration in range(ITERS):
        image = combine(pull(forward(direction)), direction, DIAG_SHIFT)
        step_size = resid_sq / inner(direction, image)
        solution = combine(solution, direction, step_size)
        residual = combine(residual, image, -step_size)
        if iteration + 1 < ITERS:
            resid_next = inner(residual, residual)
            direction = combine(residual, direction, resid_next / resid_sq)
            resid_sq = resid_next
    param_total = N_SITES * HIDDEN_SIZE + HIDDEN_SIZE + N_SITES
    scale = 1.0 / jnp.sqrt(inner(solution, solution) / param_total + EPSILON)
    return (solution[0] * scale, solution[1] * scale, solution[2] * scale)
```

```python
import functools

import jax
import jax.numpy as jnp
from jax import lax
from jax.experimental import pallas as pl
from jax.experimental.pallas import tpu as pltpu
from jax.sharding import PartitionSpec as P

N_SITES = 256
HIDDEN_SIZE = 4096
KEEP_DEV = 768
ITERS = 3

DIAG_SHIFT = 0.05
EPSILON = 1e-06
LANES = 128
MAX_STRANDS = 4
MIN_ROWS = 16
MESH = pl.DeviceIdType.MESH
F32 = jnp.float32
BF16 = jnp.bfloat16


def to_row(column):
    return jnp.transpose(jnp.broadcast_to(column, (LANES, LANES)))[:1, :]


def to_column(row):
    return jnp.transpose(jnp.broadcast_to(row, (LANES, LANES)))[:, :1]


def bit_order(strand, bits):
    rest = list(range(1, bits - 1))
    turn = strand % len(rest)
    return [0] + rest[turn:] + rest[:turn] + [bits - 1]


def total(values):
    return jnp.sum(values, axis=1, keepdims=True)


def wide_kernel(
    n_chain, n_rep, s_ref, st_ref, wt_ref, bias_ref, energy_ref, live_ref,
    mat_ref, vec_ref, acts, acc, outbox, inbox, pulled, vecs, vec_in, rowsum, rows, gathered,
    mat_send, mat_recv, back_send, back_recv, vec_send, vec_recv, row_send, row_recv,
    tell_send, tell_recv,
):
    slots, sites = s_ref.shape
    hidden = wt_ref.shape[0]
    visible = sites // n_rep
    sample_total = float(KEEP_DEV * n_chain)
    bits = n_chain.bit_length() - 1
    strands = min(MAX_STRANDS, hidden // 256)
    tile = min(256, hidden // (2 * strands))
    chunks = tile // LANES
    vis_row = hidden // LANES
    me = lax.axis_index("chain")
    rep = lax.axis_index("rep")
    lane = lax.broadcasted_iota(jnp.int32, (1, LANES), 1)

    barrier = pltpu.get_barrier_semaphore()

    @pl.loop(1, n_chain)
    def _(k):
        pl.semaphore_signal(
            barrier, inc=1, device_id={"chain": lax.rem(me + k, n_chain)}, device_id_type=MESH
        )

    for k in range(1, n_rep):
        pl.semaphore_signal(
            barrier, inc=1, device_id={"rep": lax.rem(rep + k, n_rep)}, device_id_type=MESH
        )
    pl.semaphore_wait(barrier, n_chain - 1 + n_rep - 1)

    def tell_copy(sync, source, target):
        return pltpu.make_async_remote_copy(
            src_ref=gathered.at[sync, source],
            dst_ref=gathered.at[sync, source],
            send_sem=tell_send.at[sync, target],
            recv_sem=tell_recv.at[sync, source],
            device_id={"chain": target},
            device_id_type=MESH,
        )

    def tell(sync, values):
        packed = jnp.zeros((1, LANES), F32)
        for j, value in enumerate(values):
            packed = jnp.where(lane == j, value, packed)
        weight = jnp.broadcast_to(values[0], (1, LANES))
        middle = jnp.broadcast_to(values[1], (1, LANES))
        blank = jnp.zeros((5, LANES), F32)
        gathered[sync, me] = jnp.concatenate([packed, weight, middle, blank], axis=0)

        @pl.loop(1, n_chain)
        def _(k):
            tell_copy(sync, me, lax.rem(me + k, n_chain)).start()

    def hear(sync, count):
        @pl.loop(1, n_chain)
        def _(k):
            tell_copy(sync, lax.rem(me + k, n_chain), lax.rem(me + k, n_chain)).wait_recv()

        @pl.loop(1, n_chain)
        def _(k):
            tell_copy(sync, me, lax.rem(me + k, n_chain)).wait_send()

        everyone = [gathered[sync, j] for j in range(n_chain)]
        packed = everyone[0][0:1]
        weighted = everyone[0][1:2] * everyone[0][2:3]
        for one in everyone[1:]:
            packed = packed + one[0:1]
            weighted = weighted + one[1:2] * one[2:3]
        mean = weighted / sample_total
        spread = jnp.zeros((1, LANES), F32)
        for one in everyone:
            spread = spread + one[1:2] * (one[2:3] - mean) * (one[2:3] - mean)
        found = [total(jnp.where(lane == j, packed, 0.0)) for j in range(count)]
        return mean[:, :1], spread[:, :1], found

    vecs[...] = jnp.zeros_like(vecs)
    live = live_ref[...]
    own_count = total(live)
    energy = energy_ref[...]
    tell(0, [own_count, total(energy * live) / own_count])

    @pl.loop(0, hidden // tile)
    def _(i):
        part = pl.ds(pl.multiple_of(i * tile, tile), tile)
        preact = jnp.dot(wt_ref[part, :], st_ref[...], preferred_element_type=F32)
        bias = [to_column(bias_ref[pl.ds(i * chunks + r, 1), :]) for r in range(chunks)]
        acts[part, :] = jnp.tanh(preact + jnp.concatenate(bias, axis=0)).astype(BF16)

    mean_energy, _, _ = hear(0, 0)
    centered = (energy - mean_energy) * live

    own_visible = pl.ds(pl.multiple_of(rep * visible, visible), visible)

    def pull_tiles(k, first, count, row_weight):
        @pl.loop(0, count)
        def _(i):
            begin = first + i * tile
            part = pl.ds(pl.multiple_of(begin, tile), tile)
            weighted = acts[part, :].astype(F32) * row_weight
            sums = jnp.sum(weighted, axis=1, keepdims=True)
            for r in range(chunks):
                row = to_row(sums[r * LANES : (r + 1) * LANES])
                vecs[k, pl.ds(begin // LANES + r, 1), :] = row
            acc[part, :] = jnp.dot(
                weighted.astype(BF16), s_ref[...], preferred_element_type=F32
            )

    def peer(b):
        digit = lax.rem(me // (2**b), 2)
        return digit, me + (1 - 2 * digit) * (2**b)

    def push_tiles(k, first, count):
        @pl.loop(0, count)
        def _(i):
            begin = first + i * tile
            part = pl.ds(pl.multiple_of(begin, tile), tile)
            mixture = jnp.dot(pulled[k, part, :], st_ref[...], preferred_element_type=F32)
            shift = [to_column(vecs[k, pl.ds(begin // LANES + r, 1), :]) for r in range(chunks)]
            mixture = mixture + jnp.concatenate(shift, axis=0)
            product = mixture * acts[part, :].astype(F32)
            rowsum[...] += jnp.sum(product.reshape(tile // 8, 8, slots), axis=0)

    def apply(k, row_weight):
        row_weight = row_weight / sample_total
        sums = jnp.sum(st_ref[own_visible, :].astype(F32) * row_weight, axis=1, keepdims=True)
        if visible < LANES:
            sums = jnp.concatenate([sums, jnp.zeros((LANES - visible, 1), F32)], axis=0)
        vecs[k, vis_row : vis_row + 1, :] = to_row(sums)

        rowsum[...] = jnp.zeros_like(rowsum)

        def mat_copy(source, target, sends, recvs, slot, partner):
            return pltpu.make_async_remote_copy(
                src_ref=source,
                dst_ref=target,
                send_sem=sends.at[k, slot],
                recv_sem=recvs.at[k, slot],
                device_id={"chain": partner},
                device_id_type=MESH,
            )

        def strand(c, order):
            size = hidden // strands
            start, place = c * size, c * (size + MIN_ROWS * bits)
            steps = []
            for b in order:
                digit, partner = peer(b)
                split = size // 2 >= MIN_ROWS
                moved = size // 2 if split else size
                away = start + (1 - digit) * moved if split else start
                keep = start + digit * moved if split else start
                away = pl.multiple_of(away, moved)
                keep = pl.multiple_of(keep, moved)
                if b == order[0]:
                    pull_tiles(k, away, moved // tile, row_weight)
                outbox[pl.ds(place, moved), :] = acc[pl.ds(away, moved), :].astype(BF16)
                box = pl.ds(place, moved)
                send = mat_copy(
                    outbox.at[box], inbox.at[box], mat_send, mat_recv, c * bits + b, partner
                )
                send.start()
                yield
                if b == order[0]:
                    pull_tiles(k, keep, moved // tile, row_weight)
                send.wait()
                own = acc[pl.ds(keep, moved), :]
                if not split:
                    own = own.astype(BF16).astype(F32)
                acc[pl.ds(keep, moved), :] = own + inbox[box, :].astype(F32)
                place += moved
                start, size = keep, moved
                steps.append((b, partner, split, keep, moved))
            pulled[k, pl.ds(start, size), :] = acc[pl.ds(start, size), :].astype(BF16)
            for b, partner, split, keep, moved in reversed(steps):
                if not split:
                    continue
                part = pulled.at[k, pl.ds(pl.multiple_of(keep, moved), moved)]
                send = mat_copy(part, part, back_send, back_recv, c * bits + b, partner)
                send.start()
                yield
                if b == order[0]:
                    push_tiles(k, keep, moved // tile)
                    yield
                send.wait()
                if b == order[0]:
                    other = 2 * c * (hidden // strands) + hidden // strands - moved - keep
                    push_tiles(k, other, moved // tile)

        def vec_strand():
            yield
            for b in range(bits):
                spread = pltpu.make_async_remote_copy(
                    src_ref=vecs.at[k],
                    dst_ref=vec_in.at[k, b],
                    send_sem=vec_send.at[k, b],
                    recv_sem=vec_recv.at[k, b],
                    device_id={"chain": peer(b)[1]},
                    device_id_type=MESH,
                )
                spread.start()
                yield
                spread.wait()
                vecs[k] = vecs[k] + vec_in[k, b]

        active = [strand(c, bit_order(c, bits)) for c in range(strands)] + [vec_strand()]
        while active:
            active = [one for one in active if next(one, active) is not active]
        seen = jnp.sum(rowsum[...], axis=0, keepdims=True)
        effect = to_column(vecs[k, vis_row : vis_row + 1, :])[:visible]
        seen = seen + jnp.sum(st_ref[own_visible, :].astype(F32) * effect, axis=0, keepdims=True)
        rows[k, rep, 0:1, :] = seen

        def row_copy(source, target):
            return pltpu.make_async_remote_copy(
                src_ref=rows.at[k, source, pl.ds(0, 1)],
                dst_ref=rows.at[k, source, pl.ds(0, 1)],
                send_sem=row_send.at[k, target],
                recv_sem=row_recv.at[k, source],
                device_id={"rep": target},
                device_id_type=MESH,
            )

        others = [lax.rem(rep + d, n_rep) for d in range(1, n_rep)]
        for other in others:
            row_copy(rep, other).start()
        for other in others:
            row_copy(other, other).wait_recv()
        for other in others:
            row_copy(rep, other).wait_send()
        whole = rows[k, 0, 0:1, :]
        for j in range(1, n_rep):
            whole = whole + rows[k, j, 0:1, :]
        return whole * live

    raw = apply(0, centered)
    middle = total(raw) / own_count
    local = (raw - middle) * live
    tell(1, [own_count, middle, total(local * local), total(raw * centered)])
    mean, spread, found = hear(1, 4)
    image = (raw - mean) * live
    dir_dir = found[2] + spread
    dir_wgt = found[3]
    resid_sq = dir_wgt
    dir_w, dir_o, dir_c = centered, image, [1.0, 0.0, 0.0]
    res_w, res_o, res_c = centered, image, [1.0, 0.0, 0.0]
    step = resid_sq / (dir_dir + DIAG_SHIFT * dir_wgt)
    ans_w, ans_o = step * dir_w, step * dir_o
    ans_c = [step * x for x in dir_c]
    norm = None
    for i in range(1, ITERS):
        raw = apply(i, dir_o)
        unit = [1.0 if j == i else 0.0 for j in range(ITERS)]
        res_w = res_w - step * (dir_o + DIAG_SHIFT * dir_w)
        res_c = [r - step * (u + DIAG_SHIFT * d) for r, u, d in zip(res_c, unit, dir_c)]
        fresh = res_o - step * (raw + DIAG_SHIFT * dir_o)
        middle = total(fresh * live) / own_count
        local = (fresh - middle) * live
        tell(i + 1, [
            own_count, middle, total(local * local), total(fresh * dir_o), total(fresh * res_w),
            total(fresh * dir_w), total(dir_o * res_w), total(fresh * ans_w),
            total(dir_o * ans_w), total(ans_o * ans_w),
        ])
        mean, spread, found = hear(i + 1, 10)
        res_o = (fresh - mean) * live
        _, _, res_res, res_dir, resid_next, res_dirw, dir_resw, res_ans, dir_ans, ans_ans = found
        res_res = res_res + spread
        ratio = resid_next / resid_sq
        new_dir = res_res + 2.0 * ratio * res_dir + ratio * ratio * dir_dir
        new_wgt = resid_next + ratio * (res_dirw + dir_resw) + ratio * ratio * dir_wgt
        mixed = res_ans + ratio * dir_ans
        dir_w = res_w + ratio * dir_w
        dir_o = res_o + ratio * dir_o
        dir_c = [r + ratio * d for r, d in zip(res_c, dir_c)]
        dir_dir, dir_wgt, resid_sq = new_dir, new_wgt, resid_next
        step = resid_sq / (dir_dir + DIAG_SHIFT * dir_wgt)
        norm = (ans_ans + 2.0 * step * mixed + step * step * dir_wgt) / sample_total
        ans_w, ans_o = ans_w + step * dir_w, ans_o + step * dir_o
        ans_c = [a + step * d for a, d in zip(ans_c, dir_c)]
    params = N_SITES * HIDDEN_SIZE + HIDDEN_SIZE + N_SITES
    scale = lax.rsqrt(norm / params + EPSILON)
    own_rows = mat_ref.shape[0]
    picks = lax.broadcasted_iota(jnp.int32, (MIN_ROWS, sites), 0) + me * own_rows
    picks = (picks == lax.broadcasted_iota(jnp.int32, (MIN_ROWS, sites), 1)).astype(BF16)
    for i in range(hidden // tile):
        part = slice(i * tile, (i + 1) * tile)
        out = 0.0
        for k in range(ITERS):
            piece = lax.dot_general(
                picks, pulled[k, part, :], (((1,), (1,)), ((), ())), preferred_element_type=F32
            )
            out = out + (ans_c[k] * scale) * piece
        mat_ref[:, part] = out[:own_rows]
    vec = 0.0
    for k in range(ITERS):
        vec = vec + (ans_c[k] * scale) * vecs[k]
    vec_ref[...] = vec


def wide_device(spins, energies, counts, accepted, hidden_bias, weights):
    n_chain = lax.axis_size("chain")
    n_rep = lax.axis_size("rep")
    slots, sites = spins.shape
    hidden = weights.shape[1]
    visible = sites // n_rep
    bits = n_chain.bit_length() - 1
    strands = min(MAX_STRANDS, hidden // 256)
    vec_rows = -(-(hidden // LANES + 1) // 8) * 8
    order = jnp.arange(slots, dtype=jnp.int32)
    names = jnp.where(order < counts[0], accepted[0], -1)
    live = jnp.any(order[:, None] == names[None, :], axis=1).astype(F32)
    vmem = pl.BlockSpec(memory_space=pltpu.VMEM)
    dma = pltpu.SemaphoreType.DMA
    mat, vec = pl.pallas_call(
        functools.partial(wide_kernel, n_chain, n_rep),
        out_shape=(
            jax.ShapeDtypeStruct((sites // n_chain, hidden), F32),
            jax.ShapeDtypeStruct((vec_rows, LANES), F32),
        ),
        in_specs=[vmem] * 6,
        out_specs=(vmem, vmem),
        scratch_shapes=[
            pltpu.VMEM((hidden, slots), BF16),
            pltpu.VMEM((hidden, sites), F32),
            pltpu.VMEM((hidden + strands * MIN_ROWS * bits, sites), BF16),
            pltpu.VMEM((hidden + strands * MIN_ROWS * bits, sites), BF16),
            pltpu.VMEM((ITERS, hidden, sites), BF16),
            pltpu.VMEM((ITERS, vec_rows, LANES), F32),
            pltpu.VMEM((ITERS, bits, vec_rows, LANES), F32),
            pltpu.VMEM((8, slots), F32),
            pltpu.VMEM((ITERS, n_rep, 8, slots), F32),
            pltpu.VMEM((ITERS + 1, n_chain, 8, LANES), F32),
            dma((ITERS, strands * bits)),
            dma((ITERS, strands * bits)),
            dma((ITERS, strands * bits)),
            dma((ITERS, strands * bits)),
            dma((ITERS, bits)),
            dma((ITERS, bits)),
            dma((ITERS, n_rep)),
            dma((ITERS, n_rep)),
            dma((ITERS + 1, n_chain)),
            dma((ITERS + 1, n_chain)),
        ],
        compiler_params=pltpu.CompilerParams(
            collective_id=0, has_side_effects=True, vmem_limit_bytes=60 * 1024 * 1024
        ),
    )(
        spins,
        spins.T,
        weights.T,
        hidden_bias.astype(F32).reshape(hidden // LANES, LANES),
        energies.astype(F32)[None],
        live[None],
    )
    flat = vec.reshape(-1)
    return flat[hidden : hidden + visible], flat[:hidden], mat


VMEM_LIMIT = 60 * 1024 * 1024
TAIL = 16
CORES = 2
PAIR = 2
LAG = 2


def line_kernel(
    n_chain, s_ref, w_ref, aux_ref, names_ref, count_ref,
    mat_ref, hid_ref, vis_ref,
    samples, spins_t, acts, acc, hid_acc, bias_col, shift_col, w_t,
    outbox, inbox, tail_out, tail_in, push_mat, row_weight, partial, part_in, full, energies, tail_sum, flipped, final_in,
    line_send, line_recv, rep_send, rep_recv, sib_send, sib_recv, own_send, own_recv,
    en_send, en_recv, mat_send, mat_recv, tail_send, tail_recv, part_send, part_recv, full_send, full_recv,
    fin_send, fin_recv,
):
    slots, sites = s_ref.shape
    hidden = w_ref.shape[1]
    line = n_chain // (CORES * PAIR)
    blocks = line * CORES
    width = hidden // blocks
    tall = width + TAIL
    half = slots // 2
    half_rows = half // LANES
    tiles = slots // LANES
    piece = min(256, half)
    pieces = half // piece
    members = 2 * blocks
    line_rows = members * 8
    own_sites = mat_ref.shape[0]
    chunks = width // LANES
    sample_total = float(KEEP_DEV * n_chain)
    steps = line - 1
    arrivals = steps * pieces

    me = lax.axis_index("chain")
    rep = lax.axis_index("rep")
    core = lax.rem(me, CORES)
    side = lax.rem(me // CORES, PAIR)
    z = me // (CORES * PAIR)
    block = z * CORES + core
    member = block * 2 + rep
    own_tile = side * members + member

    def chain_of(z_, side_, core_):
        return (z_ * PAIR + side_) * CORES + core_

    def device_of(tile):
        m = lax.rem(tile, members)
        b = m // 2
        return {
            "chain": chain_of(b // CORES, tile // members, lax.rem(b, CORES)),
            "rep": lax.rem(m, 2),
        }

    everyone = PAIR * members
    barrier = pltpu.get_barrier_semaphore()

    @pl.loop(1, everyone)
    def _(k):
        pl.semaphore_signal(
            barrier, inc=1, device_id=device_of(lax.rem(own_tile + k, everyone)), device_id_type=MESH
        )

    samples[block] = s_ref[...]
    names = names_ref[...]
    order = lax.broadcasted_iota(jnp.int32, (1, slots), 1)
    names = jnp.where(order < count_ref[0], names, -1)
    tile_no = names // LANES
    row_no = jnp.where(names < 0, -1, tile_no + jnp.where(tile_no >= half_rows, 8 - half_rows, 0))
    row_hot = (lax.broadcasted_iota(jnp.int32, (16, slots), 0) == row_no).astype(F32).astype(BF16)
    low = names - tile_no * LANES
    lane_hot = (lax.broadcasted_iota(jnp.int32, (LANES, slots), 0) == low).astype(F32).astype(BF16)
    live_own = lax.dot_general(
        row_hot, lane_hot, (((1,), (1,)), ((), ())), preferred_element_type=F32
    )
    slot_no = side * blocks + block
    energies[slot_no] = (aux_ref[0:16, :] * live_own).astype(BF16)
    pl.semaphore_wait(barrier, everyone - 1)

    def part_rows(r, p):
        return pl.ds(pl.multiple_of(r * half + p * piece, piece), piece)

    def line_copy(d, s, p, from_z, to_z):
        place = samples.at[from_z * CORES + core, part_rows(rep, p)]
        return pltpu.make_async_remote_copy(
            src_ref=place,
            dst_ref=place,
            send_sem=line_send.at[d, s, p],
            recv_sem=line_recv.at[d, s, p],
            device_id={"chain": chain_of(to_z, side, core)},
            device_id_type=MESH,
        )

    def own_copy(b):
        return pltpu.make_async_remote_copy(
            src_ref=samples.at[b],
            dst_ref=samples.at[b],
            send_sem=own_send,
            recv_sem=own_recv,
            device_id={"chain": chain_of(z, side, 1 - core)},
            device_id_type=MESH,
        )

    def rep_copy(it, from_z, r, p):
        place = samples.at[from_z * CORES + core, part_rows(r, p)]
        return pltpu.make_async_remote_copy(
            src_ref=place,
            dst_ref=place,
            send_sem=rep_send.at[it],
            recv_sem=rep_recv.at[it],
            device_id={"rep": 1 - rep},
            device_id_type=MESH,
        )

    def sib_copy(kind, it, from_z, c, r, p):
        place = samples.at[from_z * CORES + c, part_rows(r, p)]
        return pltpu.make_async_remote_copy(
            src_ref=place,
            dst_ref=place,
            send_sem=sib_send.at[kind, it],
            recv_sem=sib_recv.at[kind, it],
            device_id={"chain": chain_of(z, side, 1 - core)},
            device_id_type=MESH,
        )

    def en_copy(source, target):
        place = energies.at[source]
        return pltpu.make_async_remote_copy(
            src_ref=place,
            dst_ref=place,
            send_sem=en_send.at[target],
            recv_sem=en_recv.at[source],
            device_id={
                "chain": chain_of(
                    lax.rem(target, blocks) // CORES, target // blocks, lax.rem(target, CORES)
                )
            },
            device_id_type=MESH,
        )

    @pl.loop(1, n_chain)
    def _(k):
        en_copy(slot_no, lax.rem(slot_no + k, n_chain)).start()

    for p in range(pieces):
        @pl.when(z + 1 < line)
        def _():
            line_copy(0, 0, p, z, z + 1).start()

        @pl.when(z > 0)
        def _():
            line_copy(1, 0, p, z, z - 1).start()
    own_copy(block).start()

    w_t[...] = jnp.transpose(w_ref[:, pl.ds(pl.multiple_of(block * width, width), width)])
    for r in range(chunks):
        bias = to_column(aux_ref[pl.ds(16 + block * chunks + r, 1), :])
        bias_col[r * LANES : (r + 1) * LANES, :] = jnp.broadcast_to(bias, (LANES, LANES))
    partial[...] = jnp.zeros_like(partial)
    tail = lax.broadcasted_iota(jnp.int32, (TAIL, slots), 0)
    ones = (tail == 0).astype(F32).astype(BF16)

    @pl.loop(0, blocks)
    def _(j):
        acts[j, width:, :] = ones

    @pl.loop(1, n_chain)
    def _(k):
        en_copy(lax.rem(slot_no + k, n_chain), lax.rem(slot_no + k, n_chain)).wait_recv()

    energy = energies[...].astype(F32).reshape(PAIR * line_rows, LANES)
    live = (energy != 0.0).astype(F32)

    def sum_all(values):
        return total(jnp.sum(values, axis=0, keepdims=True))

    centered = (energy - sum_all(energy) / sample_total) * live

    row_weight[...] = centered / sample_total
    acc[...] = jnp.zeros_like(acc)
    hid_acc[...] = jnp.zeros_like(hid_acc)
    tail_lane = lax.broadcasted_iota(jnp.int32, (TAIL, LANES), 0)
    tail_row = lax.broadcasted_iota(jnp.int32, (TAIL, sites), 0)

    def weigh(held, b, r, p, sums):
        parts = []
        for e in range(piece // LANES):
            row = side * line_rows + b * 16 + r * 8 + p * (piece // LANES) + e
            scale = row_weight[pl.ds(row, 1), :]
            scaled = held[:, e * LANES : (e + 1) * LANES].astype(F32) * scale
            sums = sums + scaled
            high = scale.astype(BF16).astype(F32)
            ends = jnp.where(tail_lane == 0, high, jnp.where(tail_lane == 1, scale - high, 0.0))
            parts.append(jnp.concatenate([scaled, ends], axis=0).astype(BF16))
        return parts, sums

    def process(b, r, p):
        got = jnp.transpose(samples[b, part_rows(r, p), :])
        lanes = pl.ds(pl.multiple_of(r * half + p * piece, piece), piece)
        spins_t[b, :, lanes] = got
        preact = jnp.dot(w_t[...], got, preferred_element_type=F32)
        bias = bias_col[...]
        bias = jnp.concatenate([bias] * (piece // LANES), axis=1)
        found = jnp.tanh(preact + bias).astype(BF16)
        acts[b, 0:width, lanes] = found
        parts, sums = weigh(found, b, r, p, hid_acc[...])
        hid_acc[...] = sums
        acc[...] += jnp.dot(
            jnp.concatenate(parts, axis=1),
            samples[b, part_rows(r, p), :],
            preferred_element_type=F32,
        )

    @pl.loop(0, 2 * pieces)
    def _(i):
        process(block, i // pieces, lax.rem(i, pieces))

    other = z * CORES + 1 - core
    own_copy(other).wait_recv()

    @pl.loop(0, 2 * pieces)
    def _(i):
        process(other, i // pieces, lax.rem(i, pieces))

    def nearest(n):
        below, above = z, line - 1 - z
        near = jnp.minimum(below, above)
        paired = n < 2 * near
        dist = jnp.where(paired, n // 2 + 1, n - near + 1)
        upward = jnp.where(paired, lax.rem(n, 2) == 0, below > above)
        return upward, dist, jnp.where(upward, z - dist, z + dist)

    def arrival(it):
        upward, dist, from_z = nearest(it // pieces)
        return jnp.where(upward, 0, 1), dist - 1, lax.rem(it, pieces), from_z

    @pl.loop(0, arrivals + LAG + 1)
    def _(it):
        @pl.when(it < arrivals)
        def _():
            d, s, p, from_z = arrival(it)
            line_copy(d, s, p, from_z, z).wait_recv()
            to_z = z + 1 - 2 * d

            @pl.when(jnp.logical_and(to_z >= 0, to_z < line))
            def _():
                line_copy(d, s + 1, p, from_z, to_z).start()

            rep_copy(it, from_z, rep, p).start()
            sib_copy(0, it, from_z, core, rep, p).start()

        @pl.when(jnp.logical_and(it >= LAG, it < arrivals + LAG))
        def _():
            last = it - LAG
            _, _, p, from_z = arrival(last)
            rep_copy(last, from_z, 1 - rep, p).wait_recv()
            sib_copy(1, last, from_z, core, 1 - rep, p).start()

        @pl.when(jnp.logical_and(it >= 1, it <= arrivals))
        def _():
            last = it - 1
            _, _, p, from_z = arrival(last)
            process(from_z * CORES + core, rep, p)
            sib_copy(0, last, from_z, 1 - core, rep, p).wait_recv()
            process(from_z * CORES + 1 - core, rep, p)

        @pl.when(jnp.logical_and(it >= LAG, it < arrivals + LAG))
        def _():
            last = it - LAG
            _, _, p, from_z = arrival(last)
            process(from_z * CORES + core, 1 - rep, p)

        @pl.when(it >= LAG + 1)
        def _():
            last = it - LAG - 1
            _, _, p, from_z = arrival(last)
            sib_copy(1, last, from_z, 1 - core, 1 - rep, p).wait_recv()
            process(from_z * CORES + 1 - core, 1 - rep, p)

    def mat_copy(k):
        return pltpu.make_async_remote_copy(
            src_ref=outbox.at[k],
            dst_ref=inbox.at[k],
            send_sem=mat_send.at[k],
            recv_sem=mat_recv.at[k],
            device_id={"chain": chain_of(z, 1 - side, core)},
            device_id_type=MESH,
        )

    def tail_copy(k):
        return pltpu.make_async_remote_copy(
            src_ref=tail_out.at[k],
            dst_ref=tail_in.at[k],
            send_sem=tail_send.at[k],
            recv_sem=tail_recv.at[k],
            device_id={"chain": chain_of(z, 1 - side, core)},
            device_id_type=MESH,
        )

    def part_copy(k, source, target):
        return pltpu.make_async_remote_copy(
            src_ref=partial.at[k, target],
            dst_ref=part_in.at[k, source],
            send_sem=part_send.at[k, target],
            recv_sem=part_recv.at[k, source],
            device_id=device_of(side * members + target),
            device_id_type=MESH,
        )

    def full_copy(k, source, target):
        return pltpu.make_async_remote_copy(
            src_ref=full.at[k, source],
            dst_ref=full.at[k, source],
            send_sem=full_send.at[k, target],
            recv_sem=full_recv.at[k, source],
            device_id=device_of(target),
            device_id_type=MESH,
        )

    def final_copy(k, source, target):
        begin = chain_of(target // CORES, side, lax.rem(target, CORES)) * own_sites
        return pltpu.make_async_remote_copy(
            src_ref=flipped.at[k, pl.ds(pl.multiple_of(begin, own_sites), own_sites)],
            dst_ref=final_in.at[k, source],
            send_sem=fin_send.at[k, target],
            recv_sem=fin_recv.at[k, source],
            device_id={"chain": chain_of(target // CORES, side, lax.rem(target, CORES))},
            device_id_type=MESH,
        )

    def pull(k, weight):
        row_weight[...] = weight / sample_total
        acc[...] = jnp.zeros_like(acc)
        hid_acc[...] = jnp.zeros_like(hid_acc)

        @pl.loop(0, blocks)
        def _(j):
            parts = []
            sums = hid_acc[...]
            for r in range(2):
                for p in range(pieces):
                    begin = r * half + p * piece
                    more, sums = weigh(acts[j, 0:width, begin : begin + piece], j, r, p, sums)
                    parts += more
            hid_acc[...] = sums
            acc[...] += jnp.dot(
                jnp.concatenate(parts, axis=1), samples[j], preferred_element_type=F32
            )

    def apply(k, meanwhile):
        sums = jnp.sum(hid_acc[...], axis=1, keepdims=True)
        hid_row = jnp.concatenate(
            [to_row(sums[r * LANES : (r + 1) * LANES]) for r in range(chunks)], axis=1
        )
        if width < sites:
            hid_row = jnp.concatenate([hid_row, jnp.zeros((1, sites - width), F32)], axis=1)
        vis_row = acc[width : width + 1, :] + acc[width + 1 : width + 2, :]
        outbox[k] = acc[0:width, :].astype(BF16)
        tail_out[k] = jnp.concatenate([vis_row, hid_row, jnp.zeros((6, sites), F32)], axis=0)
        mat_copy(k).start()
        tail_copy(k).start()
        meanwhile()
        mat_copy(k).wait()
        tail_copy(k).wait()
        whole = outbox[k].astype(F32) + inbox[k].astype(F32)
        rest = tail_out[k] + tail_in[k]
        tail_sum[k] = rest
        flipped[k] = jnp.transpose(whole).astype(BF16)

        @pl.loop(1, blocks)
        def _(d):
            final_copy(k, block, lax.rem(block + d, blocks)).start()

        own_begin = pl.multiple_of(me * own_sites, own_sites)
        final_in[k, block] = flipped[k, pl.ds(own_begin, own_sites), :]
        push_mat[0:width, :] = whole.astype(BF16)
        rest = jnp.concatenate([rest, jnp.zeros((TAIL - 8, sites), F32)], axis=0)
        push_mat[width:, :] = jnp.where(tail_row == 0, rest / members, 0.0).astype(BF16)
        for r in range(chunks):
            shift = to_column(rest[1:2, r * LANES : (r + 1) * LANES])
            shift_col[r * LANES : (r + 1) * LANES, :] = jnp.broadcast_to(shift, (LANES, LANES))
        shift_col[width:, :] = jnp.zeros((TAIL, LANES), F32)

        @pl.loop(0, members)
        def _(i):
            turn = lax.rem(i, 4)
            _, _, far_z = nearest(jnp.maximum(line - 2 - i // 4, 0))
            at_z = jnp.where(i // 4 == line - 1, z, far_z)
            at_core = lax.rem(core + jnp.where(lax.rem(turn, 2) == 0, 1, 0), CORES)
            at_rep = lax.rem(rep + jnp.where(turn < 2, 1, 0), 2)
            j = at_z * CORES + at_core
            target = j * 2 + at_rep
            shift = shift_col[...]
            for p in range(pieces):
                begin = at_rep * half + p * piece
                mixture = jnp.dot(
                    push_mat[...],
                    spins_t[j, :, pl.ds(pl.multiple_of(begin, piece), piece)],
                    preferred_element_type=F32,
                )
                for e in range(piece // LANES):
                    lanes = pl.ds(pl.multiple_of(begin + e * LANES, LANES), LANES)
                    mix = mixture[:, e * LANES : (e + 1) * LANES] + shift
                    mix = mix * acts[j, :, lanes].astype(F32)
                    row = p * (piece // LANES) + e
                    partial[k, target, row : row + 1, :] = jnp.sum(mix, axis=0, keepdims=True)

            @pl.when(i < members - 1)
            def _():
                part_copy(k, member, target).start()

        part_in[k, member] = partial[k, member]

        @pl.loop(1, members)
        def _(d):
            part_copy(k, lax.rem(member + d, members), lax.rem(member + d, members)).wait_recv()

        full[k, own_tile] = jnp.sum(part_in[k], axis=0)
        for r in range(chunks):
            full[k, own_tile, half_rows + r : half_rows + r + 1, :] = tail_sum[
                k, 1:2, r * LANES : (r + 1) * LANES
            ]

        @pl.loop(1, everyone)
        def _(d):
            full_copy(k, own_tile, lax.rem(own_tile + d, everyone)).start()

        @pl.loop(1, everyone)
        def _(d):
            other = lax.rem(own_tile + d, everyone)
            full_copy(k, other, other).wait_recv()

        return full[k].reshape(PAIR * line_rows, LANES)

    def center(values):
        return (values - sum_all(values * live) / sample_total) * live

    state = {}

    def nothing():
        pass

    def first():
        resid_sq = sum_all(image * centered)
        state["resid_sq"] = resid_sq
        state["dir"] = centered, image, [1.0, 0.0, 0.0]
        state["res"] = centered, image, [1.0, 0.0, 0.0]
        advance(sum_all(image * image), resid_sq, None)

    def advance(dir_dir, dir_wgt, before):
        step = state["resid_sq"] / (dir_dir + DIAG_SHIFT * dir_wgt)
        dir_w, dir_o, dir_c = state["dir"]
        if before is None:
            ans = step * dir_w, step * dir_o, [step * x for x in dir_c]
        else:
            ans_w, ans_o, ans_c = before
            ans = (
                ans_w + step * dir_w,
                ans_o + step * dir_o,
                [a + step * d for a, d in zip(ans_c, dir_c)],
            )
        state["step"], state["ans"] = step, ans

    def follow():
        dir_w, dir_o, _ = state["dir"]
        advance(sum_all(dir_o * dir_o), sum_all(dir_w * dir_o), state["ans"])

    def turn_to(i, raw):
        step = state["step"]
        dir_w, dir_o, dir_c = state["dir"]
        res_w, res_o, res_c = state["res"]
        unit = [1.0 if j == i else 0.0 for j in range(ITERS)]
        res_w = res_w - step * (dir_o + DIAG_SHIFT * dir_w)
        res_c = [r - step * (u + DIAG_SHIFT * d) for r, u, d in zip(res_c, unit, dir_c)]
        res_o = center(res_o - step * (raw + DIAG_SHIFT * dir_o))
        resid_next = sum_all(res_w * res_o)
        ratio = resid_next / state["resid_sq"]
        state["resid_sq"] = resid_next
        state["res"] = res_w, res_o, res_c
        state["dir"] = (
            res_w + ratio * dir_w,
            res_o + ratio * dir_o,
            [r + ratio * d for r, d in zip(res_c, dir_c)],
        )

    image = center(apply(0, nothing))
    pull(1, image)
    raw = apply(1, first)
    for i in range(1, ITERS):
        turn_to(i, raw)
        if i + 1 < ITERS:
            pull(i + 1, state["dir"][1])
            raw = apply(i + 1, follow)
        else:
            follow()
    ans_w, ans_o, ans_c = state["ans"]
    norm = sum_all(ans_w * ans_o) / sample_total
    params = N_SITES * HIDDEN_SIZE + HIDDEN_SIZE + N_SITES
    scale = lax.rsqrt(norm / params + EPSILON)
    mix_c = [c * scale for c in ans_c]

    @pl.loop(0, ITERS)
    def _(k):
        @pl.loop(1, blocks)
        def _(d):
            other = lax.rem(block + d, blocks)
            final_copy(k, other, other).wait_recv()

    answer = 0.0
    for k in range(ITERS):
        answer = answer + mix_c[k] * tail_sum[k]
    for b in range(blocks):
        out = 0.0
        for k in range(ITERS):
            out = out + mix_c[k] * final_in[k, b].astype(F32)
        mat_ref[:, b * width : (b + 1) * width] = out
        out = 0.0
        for k in range(ITERS):
            out = out + mix_c[k] * full[k, side * members + 2 * b + rep]
        hid_ref[b * chunks : (b + 1) * chunks, :] = out[half_rows : half_rows + chunks]
    visible = sites // 2
    vis_row = answer[0:1, :]
    vis_ref[...] = jnp.where(rep == 0, vis_row[:, :visible], vis_row[:, visible:])

    @pl.loop(0, arrivals)
    def _(it):
        _, _, p, from_z = arrival(it)
        rep_copy(it, from_z, rep, p).wait_send()
        sib_copy(0, it, from_z, core, rep, p).wait_send()
        sib_copy(1, it, from_z, core, 1 - rep, p).wait_send()

    for s in range(steps):
        for p in range(pieces):
            @pl.when(jnp.logical_and(z + 1 < line, z - s >= 0))
            def _():
                line_copy(0, s, p, z - s, z + 1).wait_send()

            @pl.when(jnp.logical_and(z > 0, z + s < line))
            def _():
                line_copy(1, s, p, z + s, z - 1).wait_send()
    own_copy(block).wait_send()

    @pl.loop(1, n_chain)
    def _(k):
        en_copy(slot_no, lax.rem(slot_no + k, n_chain)).wait_send()

    @pl.loop(0, ITERS)
    def _(k):
        @pl.loop(1, blocks)
        def _(d):
            final_copy(k, block, lax.rem(block + d, blocks)).wait_send()

        @pl.loop(1, members)
        def _(d):
            part_copy(k, member, lax.rem(member + d, members)).wait_send()

        @pl.loop(1, everyone)
        def _(d):
            full_copy(k, own_tile, lax.rem(own_tile + d, everyone)).wait_send()


def line_fits(n_chain, n_rep, slots, sites, hidden):
    blocks = n_chain // PAIR
    if n_rep != 2 or n_chain % (CORES * PAIR) or n_chain < 2 * CORES * PAIR:
        return False
    if hidden % (blocks * LANES) or sites != 2 * LANES or hidden // blocks > sites:
        return False
    half = slots // 2
    if slots % (2 * LANES) or half % min(256, half) or sites % (16 * n_chain):
        return False
    if half // LANES + hidden // blocks // LANES > 8:
        return False
    held = 2 * blocks * slots * (2 * sites + hidden // blocks + TAIL)
    return 2 * held < VMEM_LIMIT


def per_device(spins, energies, counts, accepted, hidden_bias, weights):
    n_chain = lax.axis_size("chain")
    n_rep = lax.axis_size("rep")
    slots, sites = spins.shape
    hidden = weights.shape[1]
    if not line_fits(n_chain, n_rep, slots, sites, hidden):
        return wide_device(spins, energies, counts, accepted, hidden_bias, weights)
    blocks = n_chain // PAIR
    line = blocks // CORES
    width = hidden // blocks
    tall = width + TAIL
    half = slots // 2
    pieces = half // min(256, half)
    arrivals = (line - 1) * pieces
    members = 2 * blocks
    rows = PAIR * members
    own_sites = sites // n_chain
    energy = energies.astype(F32).reshape(2, half // LANES, LANES)
    energy = jnp.pad(energy, ((0, 0), (0, 8 - half // LANES), (0, 0))).reshape(16, LANES)
    aux = jnp.concatenate([energy, hidden_bias.astype(F32).reshape(hidden // LANES, LANES)], axis=0)
    vmem = pl.BlockSpec(memory_space=pltpu.VMEM)
    dma = pltpu.SemaphoreType.DMA
    mat, hid, vis = pl.pallas_call(
        functools.partial(line_kernel, n_chain),
        out_shape=(
            jax.ShapeDtypeStruct((own_sites, hidden), F32),
            jax.ShapeDtypeStruct((hidden // LANES, LANES), F32),
            jax.ShapeDtypeStruct((1, sites // 2), F32),
        ),
        in_specs=[vmem] * 4 + [pl.BlockSpec(memory_space=pltpu.SMEM)],
        out_specs=(vmem, vmem, vmem),
        scratch_shapes=[
            pltpu.VMEM((blocks, slots, sites), BF16),
            pltpu.VMEM((blocks, sites, slots), BF16),
            pltpu.VMEM((blocks, tall, slots), BF16),
            pltpu.VMEM((tall, sites), F32),
            pltpu.VMEM((width, LANES), F32),
            pltpu.VMEM((width, LANES), F32),
            pltpu.VMEM((tall, LANES), F32),
            pltpu.VMEM((width, sites), BF16),
            pltpu.VMEM((ITERS, width, sites), BF16),
            pltpu.VMEM((ITERS, width, sites), BF16),
            pltpu.VMEM((ITERS, 8, sites), F32),
            pltpu.VMEM((ITERS, 8, sites), F32),
            pltpu.VMEM((tall, sites), BF16),
            pltpu.VMEM((rows * 8, LANES), F32),
            pltpu.VMEM((ITERS, members, 8, LANES), F32),
            pltpu.VMEM((ITERS, members, 8, LANES), F32),
            pltpu.VMEM((ITERS, rows, 8, LANES), F32),
            pltpu.VMEM((n_chain, 16, LANES), BF16),
            pltpu.VMEM((ITERS, 8, sites), F32),
            pltpu.VMEM((ITERS, sites, width), BF16),
            pltpu.VMEM((ITERS, blocks, own_sites, width), BF16),
            dma((2, line - 1, pieces)),
            dma((2, line - 1, pieces)),
            dma((arrivals,)),
            dma((arrivals,)),
            dma((2, arrivals)),
            dma((2, arrivals)),
            dma,
            dma,
            dma((n_chain,)),
            dma((n_chain,)),
            dma((ITERS,)),
            dma((ITERS,)),
            dma((ITERS,)),
            dma((ITERS,)),
            dma((ITERS, members)),
            dma((ITERS, members)),
            dma((ITERS, rows)),
            dma((ITERS, rows)),
            dma((ITERS, blocks)),
            dma((ITERS, blocks)),
        ],
        compiler_params=pltpu.CompilerParams(
            collective_id=0, has_side_effects=True, vmem_limit_bytes=VMEM_LIMIT
        ),
    )(spins, weights, aux, accepted, counts)
    return vis.reshape(-1), hid.reshape(-1), mat


def solution(mesh):
    in_specs = (
        P("chain", None),
        P("chain"),
        P("chain"),
        P("chain", None),
        P("rep"),
        P(None, "rep"),
    )
    out_specs = (P("rep"), P("rep"), P("chain", "rep"))
    return jax.shard_map(
        per_device, mesh=mesh, in_specs=in_specs, out_specs=out_specs, check_vma=False
    )
```

```python
import functools

import jax
import jax.numpy as jnp
from jax import lax
from jax.experimental import pallas as pl
from jax.experimental.pallas import tpu as pltpu
from jax.sharding import PartitionSpec as P

N_SITES = 256
HIDDEN_SIZE = 4096
KEEP_DEV = 768
ITERS = 3

DIAG_SHIFT = 0.05
EPSILON = 1e-06
LANES = 128
MAX_STRANDS = 4
MIN_ROWS = 16
MESH = pl.DeviceIdType.MESH
F32 = jnp.float32
BF16 = jnp.bfloat16


def to_row(column):
    return jnp.transpose(jnp.broadcast_to(column, (LANES, LANES)))[:1, :]


def to_column(row):
    return jnp.transpose(jnp.broadcast_to(row, (LANES, LANES)))[:, :1]


def bit_order(strand, bits):
    rest = list(range(1, bits - 1))
    turn = strand % len(rest)
    return [0] + rest[turn:] + rest[:turn] + [bits - 1]


def total(values):
    return jnp.sum(values, axis=1, keepdims=True)


def wide_kernel(
    n_chain, n_rep, s_ref, st_ref, wt_ref, bias_ref, energy_ref, live_ref,
    mat_ref, vec_ref, acts, acc, outbox, inbox, pulled, vecs, vec_in, rowsum, rows, gathered,
    mat_send, mat_recv, back_send, back_recv, vec_send, vec_recv, row_send, row_recv,
    tell_send, tell_recv,
):
    slots, sites = s_ref.shape
    hidden = wt_ref.shape[0]
    visible = sites // n_rep
    sample_total = float(KEEP_DEV * n_chain)
    bits = n_chain.bit_length() - 1
    strands = min(MAX_STRANDS, hidden // 256)
    tile = min(256, hidden // (2 * strands))
    chunks = tile // LANES
    vis_row = hidden // LANES
    me = lax.axis_index("chain")
    rep = lax.axis_index("rep")
    lane = lax.broadcasted_iota(jnp.int32, (1, LANES), 1)

    barrier = pltpu.get_barrier_semaphore()

    @pl.loop(1, n_chain)
    def _(k):
        pl.semaphore_signal(
            barrier, inc=1, device_id={"chain": lax.rem(me + k, n_chain)}, device_id_type=MESH
        )

    for k in range(1, n_rep):
        pl.semaphore_signal(
            barrier, inc=1, device_id={"rep": lax.rem(rep + k, n_rep)}, device_id_type=MESH
        )
    pl.semaphore_wait(barrier, n_chain - 1 + n_rep - 1)

    def tell_copy(sync, source, target):
        return pltpu.make_async_remote_copy(
            src_ref=gathered.at[sync, source],
            dst_ref=gathered.at[sync, source],
            send_sem=tell_send.at[sync, target],
            recv_sem=tell_recv.at[sync, source],
            device_id={"chain": target},
            device_id_type=MESH,
        )

    def tell(sync, values):
        packed = jnp.zeros((1, LANES), F32)
        for j, value in enumerate(values):
            packed = jnp.where(lane == j, value, packed)
        weight = jnp.broadcast_to(values[0], (1, LANES))
        middle = jnp.broadcast_to(values[1], (1, LANES))
        blank = jnp.zeros((5, LANES), F32)
        gathered[sync, me] = jnp.concatenate([packed, weight, middle, blank], axis=0)

        @pl.loop(1, n_chain)
        def _(k):
            tell_copy(sync, me, lax.rem(me + k, n_chain)).start()

    def hear(sync, count):
        @pl.loop(1, n_chain)
        def _(k):
            tell_copy(sync, lax.rem(me + k, n_chain), lax.rem(me + k, n_chain)).wait_recv()

        @pl.loop(1, n_chain)
        def _(k):
            tell_copy(sync, me, lax.rem(me + k, n_chain)).wait_send()

        everyone = [gathered[sync, j] for j in range(n_chain)]
        packed = everyone[0][0:1]
        weighted = everyone[0][1:2] * everyone[0][2:3]
        for one in everyone[1:]:
            packed = packed + one[0:1]
            weighted = weighted + one[1:2] * one[2:3]
        mean = weighted / sample_total
        spread = jnp.zeros((1, LANES), F32)
        for one in everyone:
            spread = spread + one[1:2] * (one[2:3] - mean) * (one[2:3] - mean)
        found = [total(jnp.where(lane == j, packed, 0.0)) for j in range(count)]
        return mean[:, :1], spread[:, :1], found

    vecs[...] = jnp.zeros_like(vecs)
    live = live_ref[...]
    own_count = total(live)
    energy = energy_ref[...]
    tell(0, [own_count, total(energy * live) / own_count])

    @pl.loop(0, hidden // tile)
    def _(i):
        part = pl.ds(pl.multiple_of(i * tile, tile), tile)
        preact = jnp.dot(wt_ref[part, :], st_ref[...], preferred_element_type=F32)
        bias = [to_column(bias_ref[pl.ds(i * chunks + r, 1), :]) for r in range(chunks)]
        acts[part, :] = jnp.tanh(preact + jnp.concatenate(bias, axis=0)).astype(BF16)

    mean_energy, _, _ = hear(0, 0)
    centered = (energy - mean_energy) * live

    own_visible = pl.ds(pl.multiple_of(rep * visible, visible), visible)

    def pull_tiles(k, first, count, row_weight):
        @pl.loop(0, count)
        def _(i):
            begin = first + i * tile
            part = pl.ds(pl.multiple_of(begin, tile), tile)
            weighted = acts[part, :].astype(F32) * row_weight
            sums = jnp.sum(weighted, axis=1, keepdims=True)
            for r in range(chunks):
                row = to_row(sums[r * LANES : (r + 1) * LANES])
                vecs[k, pl.ds(begin // LANES + r, 1), :] = row
            acc[part, :] = jnp.dot(
                weighted.astype(BF16), s_ref[...], preferred_element_type=F32
            )

    def peer(b):
        digit = lax.rem(me // (2**b), 2)
        return digit, me + (1 - 2 * digit) * (2**b)

    def push_tiles(k, first, count):
        @pl.loop(0, count)
        def _(i):
            begin = first + i * tile
            part = pl.ds(pl.multiple_of(begin, tile), tile)
            mixture = jnp.dot(pulled[k, part, :], st_ref[...], preferred_element_type=F32)
            shift = [to_column(vecs[k, pl.ds(begin // LANES + r, 1), :]) for r in range(chunks)]
            mixture = mixture + jnp.concatenate(shift, axis=0)
            product = mixture * acts[part, :].astype(F32)
            rowsum[...] += jnp.sum(product.reshape(tile // 8, 8, slots), axis=0)

    def apply(k, row_weight):
        row_weight = row_weight / sample_total
        sums = jnp.sum(st_ref[own_visible, :].astype(F32) * row_weight, axis=1, keepdims=True)
        if visible < LANES:
            sums = jnp.concatenate([sums, jnp.zeros((LANES - visible, 1), F32)], axis=0)
        vecs[k, vis_row : vis_row + 1, :] = to_row(sums)

        rowsum[...] = jnp.zeros_like(rowsum)

        def mat_copy(source, target, sends, recvs, slot, partner):
            return pltpu.make_async_remote_copy(
                src_ref=source,
                dst_ref=target,
                send_sem=sends.at[k, slot],
                recv_sem=recvs.at[k, slot],
                device_id={"chain": partner},
                device_id_type=MESH,
            )

        def strand(c, order):
            size = hidden // strands
            start, place = c * size, c * (size + MIN_ROWS * bits)
            steps = []
            for b in order:
                digit, partner = peer(b)
                split = size // 2 >= MIN_ROWS
                moved = size // 2 if split else size
                away = start + (1 - digit) * moved if split else start
                keep = start + digit * moved if split else start
                away = pl.multiple_of(away, moved)
                keep = pl.multiple_of(keep, moved)
                if b == order[0]:
                    pull_tiles(k, away, moved // tile, row_weight)
                outbox[pl.ds(place, moved), :] = acc[pl.ds(away, moved), :].astype(BF16)
                box = pl.ds(place, moved)
                send = mat_copy(
                    outbox.at[box], inbox.at[box], mat_send, mat_recv, c * bits + b, partner
                )
                send.start()
                yield
                if b == order[0]:
                    pull_tiles(k, keep, moved // tile, row_weight)
                send.wait()
                own = acc[pl.ds(keep, moved), :]
                if not split:
                    own = own.astype(BF16).astype(F32)
                acc[pl.ds(keep, moved), :] = own + inbox[box, :].astype(F32)
                place += moved
                start, size = keep, moved
                steps.append((b, partner, split, keep, moved))
            pulled[k, pl.ds(start, size), :] = acc[pl.ds(start, size), :].astype(BF16)
            for b, partner, split, keep, moved in reversed(steps):
                if not split:
                    continue
                part = pulled.at[k, pl.ds(pl.multiple_of(keep, moved), moved)]
                send = mat_copy(part, part, back_send, back_recv, c * bits + b, partner)
                send.start()
                yield
                if b == order[0]:
                    push_tiles(k, keep, moved // tile)
                    yield
                send.wait()
                if b == order[0]:
                    other = 2 * c * (hidden // strands) + hidden // strands - moved - keep
                    push_tiles(k, other, moved // tile)

        def vec_strand():
            yield
            for b in range(bits):
                spread = pltpu.make_async_remote_copy(
                    src_ref=vecs.at[k],
                    dst_ref=vec_in.at[k, b],
                    send_sem=vec_send.at[k, b],
                    recv_sem=vec_recv.at[k, b],
                    device_id={"chain": peer(b)[1]},
                    device_id_type=MESH,
                )
                spread.start()
                yield
                spread.wait()
                vecs[k] = vecs[k] + vec_in[k, b]

        active = [strand(c, bit_order(c, bits)) for c in range(strands)] + [vec_strand()]
        while active:
            active = [one for one in active if next(one, active) is not active]
        seen = jnp.sum(rowsum[...], axis=0, keepdims=True)
        effect = to_column(vecs[k, vis_row : vis_row + 1, :])[:visible]
        seen = seen + jnp.sum(st_ref[own_visible, :].astype(F32) * effect, axis=0, keepdims=True)
        rows[k, rep, 0:1, :] = seen

        def row_copy(source, target):
            return pltpu.make_async_remote_copy(
                src_ref=rows.at[k, source, pl.ds(0, 1)],
                dst_ref=rows.at[k, source, pl.ds(0, 1)],
                send_sem=row_send.at[k, target],
                recv_sem=row_recv.at[k, source],
                device_id={"rep": target},
                device_id_type=MESH,
            )

        others = [lax.rem(rep + d, n_rep) for d in range(1, n_rep)]
        for other in others:
            row_copy(rep, other).start()
        for other in others:
            row_copy(other, other).wait_recv()
        for other in others:
            row_copy(rep, other).wait_send()
        whole = rows[k, 0, 0:1, :]
        for j in range(1, n_rep):
            whole = whole + rows[k, j, 0:1, :]
        return whole * live

    raw = apply(0, centered)
    middle = total(raw) / own_count
    local = (raw - middle) * live
    tell(1, [own_count, middle, total(local * local), total(raw * centered)])
    mean, spread, found = hear(1, 4)
    image = (raw - mean) * live
    dir_dir = found[2] + spread
    dir_wgt = found[3]
    resid_sq = dir_wgt
    dir_w, dir_o, dir_c = centered, image, [1.0, 0.0, 0.0]
    res_w, res_o, res_c = centered, image, [1.0, 0.0, 0.0]
    step = resid_sq / (dir_dir + DIAG_SHIFT * dir_wgt)
    ans_w, ans_o = step * dir_w, step * dir_o
    ans_c = [step * x for x in dir_c]
    norm = None
    for i in range(1, ITERS):
        raw = apply(i, dir_o)
        unit = [1.0 if j == i else 0.0 for j in range(ITERS)]
        res_w = res_w - step * (dir_o + DIAG_SHIFT * dir_w)
        res_c = [r - step * (u + DIAG_SHIFT * d) for r, u, d in zip(res_c, unit, dir_c)]
        fresh = res_o - step * (raw + DIAG_SHIFT * dir_o)
        middle = total(fresh * live) / own_count
        local = (fresh - middle) * live
        tell(i + 1, [
            own_count, middle, total(local * local), total(fresh * dir_o), total(fresh * res_w),
            total(fresh * dir_w), total(dir_o * res_w), total(fresh * ans_w),
            total(dir_o * ans_w), total(ans_o * ans_w),
        ])
        mean, spread, found = hear(i + 1, 10)
        res_o = (fresh - mean) * live
        _, _, res_res, res_dir, resid_next, res_dirw, dir_resw, res_ans, dir_ans, ans_ans = found
        res_res = res_res + spread
        ratio = resid_next / resid_sq
        new_dir = res_res + 2.0 * ratio * res_dir + ratio * ratio * dir_dir
        new_wgt = resid_next + ratio * (res_dirw + dir_resw) + ratio * ratio * dir_wgt
        mixed = res_ans + ratio * dir_ans
        dir_w = res_w + ratio * dir_w
        dir_o = res_o + ratio * dir_o
        dir_c = [r + ratio * d for r, d in zip(res_c, dir_c)]
        dir_dir, dir_wgt, resid_sq = new_dir, new_wgt, resid_next
        step = resid_sq / (dir_dir + DIAG_SHIFT * dir_wgt)
        norm = (ans_ans + 2.0 * step * mixed + step * step * dir_wgt) / sample_total
        ans_w, ans_o = ans_w + step * dir_w, ans_o + step * dir_o
        ans_c = [a + step * d for a, d in zip(ans_c, dir_c)]
    params = N_SITES * HIDDEN_SIZE + HIDDEN_SIZE + N_SITES
    scale = lax.rsqrt(norm / params + EPSILON)
    own_rows = mat_ref.shape[0]
    picks = lax.broadcasted_iota(jnp.int32, (MIN_ROWS, sites), 0) + me * own_rows
    picks = (picks == lax.broadcasted_iota(jnp.int32, (MIN_ROWS, sites), 1)).astype(BF16)
    for i in range(hidden // tile):
        part = slice(i * tile, (i + 1) * tile)
        out = 0.0
        for k in range(ITERS):
            piece = lax.dot_general(
                picks, pulled[k, part, :], (((1,), (1,)), ((), ())), preferred_element_type=F32
            )
            out = out + (ans_c[k] * scale) * piece
        mat_ref[:, part] = out[:own_rows]
    vec = 0.0
    for k in range(ITERS):
        vec = vec + (ans_c[k] * scale) * vecs[k]
    vec_ref[...] = vec


def wide_device(spins, energies, counts, accepted, hidden_bias, weights):
    n_chain = lax.axis_size("chain")
    n_rep = lax.axis_size("rep")
    slots, sites = spins.shape
    hidden = weights.shape[1]
    visible = sites // n_rep
    bits = n_chain.bit_length() - 1
    strands = min(MAX_STRANDS, hidden // 256)
    vec_rows = -(-(hidden // LANES + 1) // 8) * 8
    order = jnp.arange(slots, dtype=jnp.int32)
    names = jnp.where(order < counts[0], accepted[0], -1)
    live = jnp.any(order[:, None] == names[None, :], axis=1).astype(F32)
    vmem = pl.BlockSpec(memory_space=pltpu.VMEM)
    dma = pltpu.SemaphoreType.DMA
    mat, vec = pl.pallas_call(
        functools.partial(wide_kernel, n_chain, n_rep),
        out_shape=(
            jax.ShapeDtypeStruct((sites // n_chain, hidden), F32),
            jax.ShapeDtypeStruct((vec_rows, LANES), F32),
        ),
        in_specs=[vmem] * 6,
        out_specs=(vmem, vmem),
        scratch_shapes=[
            pltpu.VMEM((hidden, slots), BF16),
            pltpu.VMEM((hidden, sites), F32),
            pltpu.VMEM((hidden + strands * MIN_ROWS * bits, sites), BF16),
            pltpu.VMEM((hidden + strands * MIN_ROWS * bits, sites), BF16),
            pltpu.VMEM((ITERS, hidden, sites), BF16),
            pltpu.VMEM((ITERS, vec_rows, LANES), F32),
            pltpu.VMEM((ITERS, bits, vec_rows, LANES), F32),
            pltpu.VMEM((8, slots), F32),
            pltpu.VMEM((ITERS, n_rep, 8, slots), F32),
            pltpu.VMEM((ITERS + 1, n_chain, 8, LANES), F32),
            dma((ITERS, strands * bits)),
            dma((ITERS, strands * bits)),
            dma((ITERS, strands * bits)),
            dma((ITERS, strands * bits)),
            dma((ITERS, bits)),
            dma((ITERS, bits)),
            dma((ITERS, n_rep)),
            dma((ITERS, n_rep)),
            dma((ITERS + 1, n_chain)),
            dma((ITERS + 1, n_chain)),
        ],
        compiler_params=pltpu.CompilerParams(
            collective_id=0, has_side_effects=True, vmem_limit_bytes=60 * 1024 * 1024
        ),
    )(
        spins,
        spins.T,
        weights.T,
        hidden_bias.astype(F32).reshape(hidden // LANES, LANES),
        energies.astype(F32)[None],
        live[None],
    )
    flat = vec.reshape(-1)
    return flat[hidden : hidden + visible], flat[:hidden], mat


VMEM_LIMIT = 60 * 1024 * 1024
TAIL = 16
CORES = 2
PAIR = 2


def line_kernel(
    n_chain, s_ref, w_ref, aux_ref, names_ref, count_ref,
    mat_ref, hid_ref, vis_ref,
    samples, spins_t, acts, acc, hid_acc, bias_col, shift_col, w_t, w_in,
    outbox, inbox, tail_out, tail_in, push_mat, row_weight, partial, part_in, full, energies, tail_sum, flipped, final_in,
    line_send, line_recv, rep_send, rep_recv, sib_send, sib_recv, own_send, own_recv,
    en_send, en_recv, mat_send, mat_recv, tail_send, tail_recv, part_send, part_recv, full_send, full_recv,
    fin_send, fin_recv, load_sem, load_w_sem,
):
    slots, sites = s_ref.shape
    hidden = w_ref.shape[1]
    line = n_chain // (CORES * PAIR)
    blocks = line * CORES
    width = hidden // blocks
    tall = width + TAIL
    half = slots // 2
    half_rows = half // LANES
    tiles = slots // LANES
    piece = min(256, half)
    pieces = half // piece
    members = 2 * blocks
    line_rows = members * 8
    own_sites = mat_ref.shape[0]
    chunks = width // LANES
    sample_total = float(KEEP_DEV * n_chain)
    steps = line - 1
    arrivals = steps * pieces
    lag = pieces - 1

    me = lax.axis_index("chain")
    rep = lax.axis_index("rep")
    core = lax.rem(me, CORES)
    side = lax.rem(me // CORES, PAIR)
    z = me // (CORES * PAIR)
    block = z * CORES + core
    member = block * 2 + rep
    own_tile = side * members + member

    def chain_of(z_, side_, core_):
        return (z_ * PAIR + side_) * CORES + core_

    def device_of(tile):
        m = lax.rem(tile, members)
        b = m // 2
        return {
            "chain": chain_of(b // CORES, tile // members, lax.rem(b, CORES)),
            "rep": lax.rem(m, 2),
        }

    everyone = PAIR * members
    load = pltpu.make_async_copy(s_ref, samples.at[block], load_sem)
    load.start()
    columns = pl.ds(pl.multiple_of(block * width, width), width)
    load_w = pltpu.make_async_copy(w_ref.at[:, columns], w_in, load_w_sem)
    load_w.start()
    barrier = pltpu.get_barrier_semaphore()

    def nearest(n):
        below, above = z, line - 1 - z
        near = jnp.minimum(below, above)
        paired = n < 2 * near
        dist = jnp.where(paired, n // 2 + 1, n - near + 1)
        upward = jnp.where(paired, lax.rem(n, 2) == 0, below > above)
        return upward, dist, jnp.where(upward, z - dist, z + dist)

    def far_first(i):
        _, _, far_z = nearest(jnp.maximum(line - 2 - i // 8, 0))
        at_z = jnp.where(i // 8 == line - 1, z, far_z)
        turn = lax.rem(i, 8)
        at_side = lax.rem(side + jnp.where(turn < 4, 1, 0), PAIR)
        at_rep = lax.rem(rep + jnp.where(lax.rem(turn, 4) < 2, 1, 0), 2)
        at_core = lax.rem(core + jnp.where(lax.rem(turn, 2) == 0, 1, 0), CORES)
        return at_side * members + (at_z * CORES + at_core) * 2 + at_rep

    @pl.loop(0, everyone - 1)
    def _(i):
        pl.semaphore_signal(
            barrier, inc=1, device_id=device_of(far_first(i)), device_id_type=MESH
        )

    names = names_ref[...]
    order = lax.broadcasted_iota(jnp.int32, (1, slots), 1)
    names = jnp.where(order < count_ref[0], names, -1)
    tile_no = names // LANES
    row_no = jnp.where(names < 0, -1, tile_no + jnp.where(tile_no >= half_rows, 8 - half_rows, 0))
    row_hot = (lax.broadcasted_iota(jnp.int32, (16, slots), 0) == row_no).astype(F32).astype(BF16)
    low = names - tile_no * LANES
    lane_hot = (lax.broadcasted_iota(jnp.int32, (LANES, slots), 0) == low).astype(F32).astype(BF16)
    live_own = lax.dot_general(
        row_hot, lane_hot, (((1,), (1,)), ((), ())), preferred_element_type=F32
    )
    slot_no = side * blocks + block
    energies[slot_no] = (aux_ref[0:16, :] * live_own).astype(BF16)
    load.wait()
    load_w.wait()
    pl.semaphore_wait(barrier, everyone - 1)

    def batch(place, send, recv):
        return pltpu.make_async_remote_copy(
            src_ref=place,
            dst_ref=place,
            send_sem=send,
            recv_sem=recv,
            device_id={"chain": chain_of(z, side, 1 - core)},
            device_id_type=MESH,
        )

    def part_rows(r, p):
        return pl.ds(pl.multiple_of(r * half + p * piece, piece), piece)

    def line_copy(d, s, p, from_z, to_z):
        place = samples.at[from_z * CORES + core, part_rows(rep, p)]
        return pltpu.make_async_remote_copy(
            src_ref=place,
            dst_ref=place,
            send_sem=line_send.at[d, s, p],
            recv_sem=line_recv.at[d, s, p],
            device_id={"chain": chain_of(to_z, side, core)},
            device_id_type=MESH,
        )

    def own_copy(b):
        return pltpu.make_async_remote_copy(
            src_ref=samples.at[b],
            dst_ref=samples.at[b],
            send_sem=own_send,
            recv_sem=own_recv,
            device_id={"chain": chain_of(z, side, 1 - core)},
            device_id_type=MESH,
        )

    def rep_copy(it, from_z, r, p):
        place = samples.at[from_z * CORES + core, part_rows(r, p)]
        return pltpu.make_async_remote_copy(
            src_ref=place,
            dst_ref=place,
            send_sem=rep_send.at[it],
            recv_sem=rep_recv.at[it],
            device_id={"rep": 1 - rep},
            device_id_type=MESH,
        )

    def sib_copy(kind, it, from_z, c, r, p):
        place = samples.at[from_z * CORES + c, part_rows(r, p)]
        return pltpu.make_async_remote_copy(
            src_ref=place,
            dst_ref=place,
            send_sem=sib_send.at[kind, it],
            recv_sem=sib_recv.at[kind, it],
            device_id={"chain": chain_of(z, side, 1 - core)},
            device_id_type=MESH,
        )

    def en_copy(source, target):
        place = energies.at[source]
        return pltpu.make_async_remote_copy(
            src_ref=place,
            dst_ref=place,
            send_sem=en_send,
            recv_sem=en_recv,
            device_id={
                "chain": chain_of(
                    lax.rem(target, blocks) // CORES, target // blocks, lax.rem(target, CORES)
                )
            },
            device_id_type=MESH,
        )

    @pl.loop(1, n_chain)
    def _(k):
        en_copy(slot_no, lax.rem(slot_no + k, n_chain)).start()

    for p in range(pieces):
        @pl.when(z + 1 < line)
        def _():
            line_copy(0, 0, p, z, z + 1).start()

        @pl.when(z > 0)
        def _():
            line_copy(1, 0, p, z, z - 1).start()
    own_copy(block).start()

    w_t[...] = jnp.transpose(w_in[...])
    for r in range(chunks):
        bias = to_column(aux_ref[pl.ds(16 + block * chunks + r, 1), :])
        bias_col[r * LANES : (r + 1) * LANES, :] = jnp.broadcast_to(bias, (LANES, LANES))
    partial[...] = jnp.zeros_like(partial)
    tail = lax.broadcasted_iota(jnp.int32, (TAIL, slots), 0)
    ones = (tail == 0).astype(F32).astype(BF16)

    @pl.loop(0, blocks)
    def _(j):
        acts[j, width:, :] = ones

    batch(energies.at[pl.ds(0, n_chain - 1)], en_send, en_recv).wait_recv()

    energy = energies[...].astype(F32).reshape(PAIR * line_rows, LANES)
    live = (energy != 0.0).astype(F32)

    def sum_all(values):
        return total(jnp.sum(values, axis=0, keepdims=True))

    centered = (energy - sum_all(energy) / sample_total) * live

    row_weight[...] = centered / sample_total
    acc[...] = jnp.zeros_like(acc)
    hid_acc[...] = jnp.zeros_like(hid_acc)
    tail_lane = lax.broadcasted_iota(jnp.int32, (TAIL, LANES), 0)
    tail_row = lax.broadcasted_iota(jnp.int32, (TAIL, sites), 0)

    def weigh(held, b, r, p, sums):
        parts = []
        for e in range(piece // LANES):
            row = side * line_rows + b * 16 + r * 8 + p * (piece // LANES) + e
            scale = row_weight[pl.ds(row, 1), :]
            scaled = held[:, e * LANES : (e + 1) * LANES].astype(F32) * scale
            sums = sums + scaled
            high = scale.astype(BF16).astype(F32)
            ends = jnp.where(tail_lane == 0, high, jnp.where(tail_lane == 1, scale - high, 0.0))
            parts.append(jnp.concatenate([scaled, ends], axis=0).astype(BF16))
        return parts, sums

    def process(places):
        rows = [samples[b, part_rows(r, p), :] for b, r, p in places]
        got = [jnp.transpose(part) for part in rows]
        bias = jnp.concatenate([bias_col[...]] * (piece // LANES), axis=1)
        found = [
            jnp.tanh(jnp.dot(w_t[...], part, preferred_element_type=F32) + bias).astype(BF16)
            for part in got
        ]
        parts, sums = [], hid_acc[...]
        for (b, r, p), part in zip(places, found):
            more, sums = weigh(part, b, r, p, sums)
            parts += more
        pulled = jnp.dot(
            jnp.concatenate(parts, axis=1),
            jnp.concatenate(rows, axis=0),
            preferred_element_type=F32,
        )
        hid_acc[...] = sums
        acc[...] += pulled
        for (b, r, p), flip, act in zip(places, got, found):
            lanes = pl.ds(pl.multiple_of(r * half + p * piece, piece), piece)
            spins_t[b, :, lanes] = flip
            acts[b, 0:width, lanes] = act

    other = z * CORES + 1 - core
    own_copy(other).wait_recv()

    def arrival(it):
        both = it // pieces < 2 * jnp.minimum(z, line - 1 - z)
        spot = lax.rem(it, 2 * pieces)
        n = jnp.where(both, it // (2 * pieces) * 2 + lax.rem(spot, 2), it // pieces)
        p = jnp.where(both, spot // 2, lax.rem(it, pieces))
        upward, dist, from_z = nearest(n)
        return jnp.where(upward, 0, 1), dist - 1, p, from_z

    @pl.loop(0, arrivals + lag + 1)
    def _(it):
        @pl.when(it < arrivals)
        def _():
            d, s, p, from_z = arrival(it)
            line_copy(d, s, p, from_z, z).wait_recv()
            to_z = z + 1 - 2 * d

            @pl.when(jnp.logical_and(to_z >= 0, to_z < line))
            def _():
                line_copy(d, s + 1, p, from_z, to_z).start()

            rep_copy(it, from_z, rep, p).start()
            sib_copy(0, it, from_z, core, rep, p).start()

        @pl.when(jnp.logical_and(it >= lag, it < arrivals + lag))
        def _():
            last = it - lag
            _, _, p, from_z = arrival(last)
            rep_copy(last, from_z, 1 - rep, p).wait_recv()
            sib_copy(1, last, from_z, core, 1 - rep, p).start()

        last = jnp.maximum(it - pieces, 0)
        _, _, last_p, last_z = arrival(last)
        p = jnp.where(it < pieces, it, last_p)
        at_z = jnp.where(it < pieces, z, last_z)
        b = at_z * CORES + core
        other = at_z * CORES + 1 - core

        @pl.when(it >= pieces)
        def _():
            sib_copy(0, last, last_z, 1 - core, rep, p).wait_recv()
            sib_copy(1, last, last_z, 1 - core, 1 - rep, p).wait_recv()

        process([(b, rep, p), (other, rep, p), (b, 1 - rep, p), (other, 1 - rep, p)])

    def mat_copy(k):
        return pltpu.make_async_remote_copy(
            src_ref=outbox.at[k],
            dst_ref=inbox.at[k],
            send_sem=mat_send.at[k],
            recv_sem=mat_recv.at[k],
            device_id={"chain": chain_of(z, 1 - side, core)},
            device_id_type=MESH,
        )

    def tail_copy(k):
        return pltpu.make_async_remote_copy(
            src_ref=tail_out.at[k],
            dst_ref=tail_in.at[k],
            send_sem=tail_send.at[k],
            recv_sem=tail_recv.at[k],
            device_id={"chain": chain_of(z, 1 - side, core)},
            device_id_type=MESH,
        )

    def part_copy(k, source, target):
        return pltpu.make_async_remote_copy(
            src_ref=partial.at[k, target],
            dst_ref=part_in.at[k, source],
            send_sem=part_send.at[k],
            recv_sem=part_recv.at[k],
            device_id=device_of(side * members + target),
            device_id_type=MESH,
        )

    def part_batch(k):
        return batch(part_in.at[k, pl.ds(0, members - 1)], part_send.at[k], part_recv.at[k])

    def full_batch(k):
        return batch(full.at[k, pl.ds(0, everyone - 1)], full_send.at[k], full_recv.at[k])

    def final_batch(k):
        return batch(final_in.at[k, pl.ds(0, blocks - 1)], fin_send.at[k], fin_recv.at[k])

    def final_copy(k, source, target):
        begin = chain_of(target // CORES, side, lax.rem(target, CORES)) * own_sites
        return pltpu.make_async_remote_copy(
            src_ref=flipped.at[k, pl.ds(pl.multiple_of(begin, own_sites), own_sites)],
            dst_ref=final_in.at[k, source],
            send_sem=fin_send.at[k],
            recv_sem=fin_recv.at[k],
            device_id={"chain": chain_of(target // CORES, side, lax.rem(target, CORES))},
            device_id_type=MESH,
        )

    def pull(k, weight):
        row_weight[...] = weight / sample_total
        acc[...] = jnp.zeros_like(acc)
        hid_acc[...] = jnp.zeros_like(hid_acc)

        @pl.loop(0, blocks)
        def _(j):
            parts = []
            sums = hid_acc[...]
            for r in range(2):
                for p in range(pieces):
                    begin = r * half + p * piece
                    more, sums = weigh(acts[j, 0:width, begin : begin + piece], j, r, p, sums)
                    parts += more
            hid_acc[...] = sums
            acc[...] += jnp.dot(
                jnp.concatenate(parts, axis=1), samples[j], preferred_element_type=F32
            )

    def apply(k, meanwhile):
        sums = jnp.sum(hid_acc[...], axis=1, keepdims=True)
        hid_row = jnp.concatenate(
            [to_row(sums[r * LANES : (r + 1) * LANES]) for r in range(chunks)], axis=1
        )
        if width < sites:
            hid_row = jnp.concatenate([hid_row, jnp.zeros((1, sites - width), F32)], axis=1)
        vis_row = acc[width : width + 1, :] + acc[width + 1 : width + 2, :]
        outbox[k] = acc[0:width, :].astype(BF16)
        tail_out[k] = jnp.concatenate([vis_row, hid_row, jnp.zeros((6, sites), F32)], axis=0)
        tail_copy(k).start()
        mat_copy(k).start()
        meanwhile()
        mat_copy(k).wait()
        tail_copy(k).wait()
        whole = outbox[k].astype(F32) + inbox[k].astype(F32)
        rest = tail_out[k] + tail_in[k]
        tail_sum[k] = rest
        push_mat[0:width, :] = whole.astype(BF16)
        rest = jnp.concatenate([rest, jnp.zeros((TAIL - 8, sites), F32)], axis=0)
        push_mat[width:, :] = jnp.where(tail_row == 0, rest / members, 0.0).astype(BF16)
        for r in range(chunks):
            shift = to_column(rest[1:2, r * LANES : (r + 1) * LANES])
            shift_col[r * LANES : (r + 1) * LANES, :] = jnp.broadcast_to(shift, (LANES, LANES))
        shift_col[width:, :] = jnp.zeros((TAIL, LANES), F32)

        @pl.loop(0, members)
        def _(i):
            turn = lax.rem(i, 4)
            _, _, far_z = nearest(jnp.maximum(line - 2 - i // 4, 0))
            at_z = jnp.where(i // 4 == line - 1, z, far_z)
            at_core = lax.rem(core + jnp.where(lax.rem(turn, 2) == 0, 1, 0), CORES)
            at_rep = lax.rem(rep + jnp.where(turn < 2, 1, 0), 2)
            j = at_z * CORES + at_core
            target = j * 2 + at_rep
            shift = shift_col[...]
            for p in range(pieces):
                begin = at_rep * half + p * piece
                mixture = jnp.dot(
                    push_mat[...],
                    spins_t[j, :, pl.ds(pl.multiple_of(begin, piece), piece)],
                    preferred_element_type=F32,
                )
                for e in range(piece // LANES):
                    lanes = pl.ds(pl.multiple_of(begin + e * LANES, LANES), LANES)
                    mix = mixture[:, e * LANES : (e + 1) * LANES] + shift
                    mix = mix * acts[j, :, lanes].astype(F32)
                    row = p * (piece // LANES) + e
                    partial[k, target, row : row + 1, :] = jnp.sum(mix, axis=0, keepdims=True)

            @pl.when(i < members - 1)
            def _():
                part_copy(k, member, target).start()

        flipped[k] = jnp.transpose(push_mat[0:width, :])

        @pl.loop(1, blocks)
        def _(d):
            final_copy(k, block, lax.rem(block + d, blocks)).start()

        own_begin = pl.multiple_of(me * own_sites, own_sites)
        final_in[k, block] = flipped[k, pl.ds(own_begin, own_sites), :]
        part_in[k, member] = partial[k, member]

        part_batch(k).wait_recv()

        full[k, own_tile] = jnp.sum(part_in[k], axis=0)
        for r in range(chunks):
            full[k, own_tile, half_rows + r : half_rows + r + 1, :] = tail_sum[
                k, 1:2, r * LANES : (r + 1) * LANES
            ]

        for n in range(line):
            at_z = z if n == line - 1 else nearest(line - 2 - n)[2]
            for turn in range(8):
                flips = turn < 4, turn % 2 == 0, turn % 4 < 2
                if n == line - 1 and not any(flips):
                    continue
                at_side = 1 - side if flips[0] else side
                at_core = 1 - core if flips[1] else core
                at_rep = 1 - rep if flips[2] else rep
                pltpu.make_async_remote_copy(
                    src_ref=full.at[k, own_tile],
                    dst_ref=full.at[k, own_tile],
                    send_sem=full_send.at[k],
                    recv_sem=full_recv.at[k],
                    device_id={"chain": chain_of(at_z, at_side, at_core), "rep": at_rep},
                    device_id_type=MESH,
                ).start()

        full_batch(k).wait_recv()
        return full[k].reshape(PAIR * line_rows, LANES)

    def center(values):
        return (values - sum_all(values * live) / sample_total) * live

    state = {}

    def nothing():
        pass

    def first():
        resid_sq = sum_all(image * centered)
        state["resid_sq"] = resid_sq
        state["dir"] = centered, image, [1.0, 0.0, 0.0]
        state["res"] = centered, image, [1.0, 0.0, 0.0]
        advance(sum_all(image * image), resid_sq, None)

    def advance(dir_dir, dir_wgt, before):
        step = state["resid_sq"] / (dir_dir + DIAG_SHIFT * dir_wgt)
        dir_w, dir_o, dir_c = state["dir"]
        if before is None:
            ans = step * dir_w, step * dir_o, [step * x for x in dir_c]
        else:
            ans_w, ans_o, ans_c = before
            ans = (
                ans_w + step * dir_w,
                ans_o + step * dir_o,
                [a + step * d for a, d in zip(ans_c, dir_c)],
            )
        state["step"], state["ans"] = step, ans

    def follow():
        dir_w, dir_o, _ = state["dir"]
        advance(sum_all(dir_o * dir_o), sum_all(dir_w * dir_o), state["ans"])

    def turn_to(i, raw):
        step = state["step"]
        dir_w, dir_o, dir_c = state["dir"]
        res_w, res_o, res_c = state["res"]
        unit = [1.0 if j == i else 0.0 for j in range(ITERS)]
        res_w = res_w - step * (dir_o + DIAG_SHIFT * dir_w)
        res_c = [r - step * (u + DIAG_SHIFT * d) for r, u, d in zip(res_c, unit, dir_c)]
        res_o = center(res_o - step * (raw + DIAG_SHIFT * dir_o))
        resid_next = sum_all(res_w * res_o)
        ratio = resid_next / state["resid_sq"]
        state["resid_sq"] = resid_next
        state["res"] = res_w, res_o, res_c
        state["dir"] = (
            res_w + ratio * dir_w,
            res_o + ratio * dir_o,
            [r + ratio * d for r, d in zip(res_c, dir_c)],
        )

    image = center(apply(0, nothing))
    pull(1, image)
    raw = apply(1, first)
    for i in range(1, ITERS):
        turn_to(i, raw)
        if i + 1 < ITERS:
            pull(i + 1, state["dir"][1])
            raw = apply(i + 1, follow)
        else:
            follow()
    ans_w, ans_o, ans_c = state["ans"]
    norm = sum_all(ans_w * ans_o) / sample_total
    params = N_SITES * HIDDEN_SIZE + HIDDEN_SIZE + N_SITES
    scale = lax.rsqrt(norm / params + EPSILON)
    mix_c = [c * scale for c in ans_c]

    for k in range(ITERS):
        final_batch(k).wait_recv()

    answer = 0.0
    for k in range(ITERS):
        answer = answer + mix_c[k] * tail_sum[k]
    for b in range(blocks):
        out = 0.0
        for k in range(ITERS):
            out = out + mix_c[k] * final_in[k, b].astype(F32)
        mat_ref[:, b * width : (b + 1) * width] = out
        out = 0.0
        for k in range(ITERS):
            out = out + mix_c[k] * full[k, side * members + 2 * b + rep]
        hid_ref[b * chunks : (b + 1) * chunks, :] = out[half_rows : half_rows + chunks]
    visible = sites // 2
    vis_row = answer[0:1, :]
    vis_ref[...] = jnp.where(rep == 0, vis_row[:, :visible], vis_row[:, visible:])

    @pl.loop(0, arrivals)
    def _(it):
        _, _, p, from_z = arrival(it)
        rep_copy(it, from_z, rep, p).wait_send()
        sib_copy(0, it, from_z, core, rep, p).wait_send()
        sib_copy(1, it, from_z, core, 1 - rep, p).wait_send()

    for s in range(steps):
        for p in range(pieces):
            @pl.when(jnp.logical_and(z + 1 < line, z - s >= 0))
            def _():
                line_copy(0, s, p, z - s, z + 1).wait_send()

            @pl.when(jnp.logical_and(z > 0, z + s < line))
            def _():
                line_copy(1, s, p, z + s, z - 1).wait_send()
    own_copy(block).wait_send()

    batch(energies.at[pl.ds(0, n_chain - 1)], en_send, en_recv).wait_send()
    for k in range(ITERS):
        final_batch(k).wait_send()
        part_batch(k).wait_send()
        full_batch(k).wait_send()


def line_fits(n_chain, n_rep, slots, sites, hidden):
    blocks = n_chain // PAIR
    if n_rep != 2 or n_chain % (CORES * PAIR) or n_chain < 2 * CORES * PAIR:
        return False
    if hidden % (blocks * LANES) or sites != 2 * LANES or hidden // blocks > sites:
        return False
    half = slots // 2
    if slots % (2 * LANES) or half % min(256, half) or sites % (16 * n_chain):
        return False
    if half // LANES + hidden // blocks // LANES > 8:
        return False
    held = 2 * blocks * slots * (2 * sites + hidden // blocks + TAIL)
    return 2 * held < VMEM_LIMIT


def per_device(spins, energies, counts, accepted, hidden_bias, weights):
    n_chain = lax.axis_size("chain")
    n_rep = lax.axis_size("rep")
    slots, sites = spins.shape
    hidden = weights.shape[1]
    if not line_fits(n_chain, n_rep, slots, sites, hidden):
        return wide_device(spins, energies, counts, accepted, hidden_bias, weights)
    blocks = n_chain // PAIR
    line = blocks // CORES
    width = hidden // blocks
    tall = width + TAIL
    half = slots // 2
    pieces = half // min(256, half)
    arrivals = (line - 1) * pieces
    members = 2 * blocks
    rows = PAIR * members
    own_sites = sites // n_chain
    energy = energies.astype(F32).reshape(2, half // LANES, LANES)
    energy = jnp.pad(energy, ((0, 0), (0, 8 - half // LANES), (0, 0))).reshape(16, LANES)
    aux = jnp.concatenate([energy, hidden_bias.astype(F32).reshape(hidden // LANES, LANES)], axis=0)
    vmem = pl.BlockSpec(memory_space=pltpu.VMEM)
    dma = pltpu.SemaphoreType.DMA
    mat, hid, vis = pl.pallas_call(
        functools.partial(line_kernel, n_chain),
        out_shape=(
            jax.ShapeDtypeStruct((own_sites, hidden), F32),
            jax.ShapeDtypeStruct((hidden // LANES, LANES), F32),
            jax.ShapeDtypeStruct((1, sites // 2), F32),
        ),
        in_specs=[pl.BlockSpec(memory_space=pl.ANY)] * 2 + [vmem] * 2 + [pl.BlockSpec(memory_space=pltpu.SMEM)],
        out_specs=(vmem, vmem, vmem),
        scratch_shapes=[
            pltpu.VMEM((blocks, slots, sites), BF16),
            pltpu.VMEM((blocks, sites, slots), BF16),
            pltpu.VMEM((blocks, tall, slots), BF16),
            pltpu.VMEM((tall, sites), F32),
            pltpu.VMEM((width, LANES), F32),
            pltpu.VMEM((width, LANES), F32),
            pltpu.VMEM((tall, LANES), F32),
            pltpu.VMEM((width, sites), BF16),
            pltpu.VMEM((sites, width), BF16),
            pltpu.VMEM((ITERS, width, sites), BF16),
            pltpu.VMEM((ITERS, width, sites), BF16),
            pltpu.VMEM((ITERS, 8, sites), F32),
            pltpu.VMEM((ITERS, 8, sites), F32),
            pltpu.VMEM((tall, sites), BF16),
            pltpu.VMEM((rows * 8, LANES), F32),
            pltpu.VMEM((ITERS, members, 8, LANES), F32),
            pltpu.VMEM((ITERS, members, 8, LANES), F32),
            pltpu.VMEM((ITERS, rows, 8, LANES), F32),
            pltpu.VMEM((n_chain, 16, LANES), BF16),
            pltpu.VMEM((ITERS, 8, sites), F32),
            pltpu.VMEM((ITERS, sites, width), BF16),
            pltpu.VMEM((ITERS, blocks, own_sites, width), BF16),
            dma((2, line - 1, pieces)),
            dma((2, line - 1, pieces)),
            dma((arrivals,)),
            dma((arrivals,)),
            dma((2, arrivals)),
            dma((2, arrivals)),
            dma,
            dma,
            dma,
            dma,
            dma((ITERS,)),
            dma((ITERS,)),
            dma((ITERS,)),
            dma((ITERS,)),
            dma((ITERS,)),
            dma((ITERS,)),
            dma((ITERS,)),
            dma((ITERS,)),
            dma((ITERS,)),
            dma((ITERS,)),
            dma,
            dma,
        ],
        compiler_params=pltpu.CompilerParams(
            collective_id=0, has_side_effects=True, vmem_limit_bytes=VMEM_LIMIT
        ),
    )(spins, weights, aux, accepted, counts)
    return vis.reshape(-1), hid.reshape(-1), mat


def solution(mesh):
    in_specs = (
        P("chain", None),
        P("chain"),
        P("chain"),
        P("chain", None),
        P("rep"),
        P(None, "rep"),
    )
    out_specs = (P("rep"), P("rep"), P("chain", "rep"))
    return jax.shard_map(
        per_device, mesh=mesh, in_specs=in_specs, out_specs=out_specs, check_vma=False
    )
```

```python
import functools

import jax
import jax.numpy as jnp
from jax import lax
from jax.experimental import pallas as pl
from jax.experimental.pallas import tpu as pltpu
from jax.sharding import PartitionSpec as P

N_SITES = 256
HIDDEN_SIZE = 4096
KEEP_DEV = 768
ITERS = 3

DIAG_SHIFT = 0.05
EPSILON = 1e-06
LANES = 128
MAX_STRANDS = 4
MIN_ROWS = 16
MESH = pl.DeviceIdType.MESH
F32 = jnp.float32
BF16 = jnp.bfloat16


def to_row(column):
    return jnp.transpose(jnp.broadcast_to(column, (LANES, LANES)))[:1, :]


def to_column(row):
    return jnp.transpose(jnp.broadcast_to(row, (LANES, LANES)))[:, :1]


def bit_order(strand, bits):
    rest = list(range(1, bits - 1))
    turn = strand % len(rest)
    return [0] + rest[turn:] + rest[:turn] + [bits - 1]


def total(values):
    return jnp.sum(values, axis=1, keepdims=True)


def wide_kernel(
    n_chain, n_rep, s_ref, st_ref, wt_ref, bias_ref, energy_ref, live_ref,
    mat_ref, vec_ref, acts, acc, outbox, inbox, pulled, vecs, vec_in, rowsum, rows, gathered,
    mat_send, mat_recv, back_send, back_recv, vec_send, vec_recv, row_send, row_recv,
    tell_send, tell_recv,
):
    slots, sites = s_ref.shape
    hidden = wt_ref.shape[0]
    visible = sites // n_rep
    sample_total = float(KEEP_DEV * n_chain)
    bits = n_chain.bit_length() - 1
    strands = min(MAX_STRANDS, hidden // 256)
    tile = min(256, hidden // (2 * strands))
    chunks = tile // LANES
    vis_row = hidden // LANES
    me = lax.axis_index("chain")
    rep = lax.axis_index("rep")
    lane = lax.broadcasted_iota(jnp.int32, (1, LANES), 1)

    barrier = pltpu.get_barrier_semaphore()

    @pl.loop(1, n_chain)
    def _(k):
        pl.semaphore_signal(
            barrier, inc=1, device_id={"chain": lax.rem(me + k, n_chain)}, device_id_type=MESH
        )

    for k in range(1, n_rep):
        pl.semaphore_signal(
            barrier, inc=1, device_id={"rep": lax.rem(rep + k, n_rep)}, device_id_type=MESH
        )
    pl.semaphore_wait(barrier, n_chain - 1 + n_rep - 1)

    def tell_copy(sync, source, target):
        return pltpu.make_async_remote_copy(
            src_ref=gathered.at[sync, source],
            dst_ref=gathered.at[sync, source],
            send_sem=tell_send.at[sync, target],
            recv_sem=tell_recv.at[sync, source],
            device_id={"chain": target},
            device_id_type=MESH,
        )

    def tell(sync, values):
        packed = jnp.zeros((1, LANES), F32)
        for j, value in enumerate(values):
            packed = jnp.where(lane == j, value, packed)
        weight = jnp.broadcast_to(values[0], (1, LANES))
        middle = jnp.broadcast_to(values[1], (1, LANES))
        blank = jnp.zeros((5, LANES), F32)
        gathered[sync, me] = jnp.concatenate([packed, weight, middle, blank], axis=0)

        @pl.loop(1, n_chain)
        def _(k):
            tell_copy(sync, me, lax.rem(me + k, n_chain)).start()

    def hear(sync, count):
        @pl.loop(1, n_chain)
        def _(k):
            tell_copy(sync, lax.rem(me + k, n_chain), lax.rem(me + k, n_chain)).wait_recv()

        @pl.loop(1, n_chain)
        def _(k):
            tell_copy(sync, me, lax.rem(me + k, n_chain)).wait_send()

        everyone = [gathered[sync, j] for j in range(n_chain)]
        packed = everyone[0][0:1]
        weighted = everyone[0][1:2] * everyone[0][2:3]
        for one in everyone[1:]:
            packed = packed + one[0:1]
            weighted = weighted + one[1:2] * one[2:3]
        mean = weighted / sample_total
        spread = jnp.zeros((1, LANES), F32)
        for one in everyone:
            spread = spread + one[1:2] * (one[2:3] - mean) * (one[2:3] - mean)
        found = [total(jnp.where(lane == j, packed, 0.0)) for j in range(count)]
        return mean[:, :1], spread[:, :1], found

    vecs[...] = jnp.zeros_like(vecs)
    live = live_ref[...]
    own_count = total(live)
    energy = energy_ref[...]
    tell(0, [own_count, total(energy * live) / own_count])

    @pl.loop(0, hidden // tile)
    def _(i):
        part = pl.ds(pl.multiple_of(i * tile, tile), tile)
        preact = jnp.dot(wt_ref[part, :], st_ref[...], preferred_element_type=F32)
        bias = [to_column(bias_ref[pl.ds(i * chunks + r, 1), :]) for r in range(chunks)]
        acts[part, :] = jnp.tanh(preact + jnp.concatenate(bias, axis=0)).astype(BF16)

    mean_energy, _, _ = hear(0, 0)
    centered = (energy - mean_energy) * live

    own_visible = pl.ds(pl.multiple_of(rep * visible, visible), visible)

    def pull_tiles(k, first, count, row_weight):
        @pl.loop(0, count)
        def _(i):
            begin = first + i * tile
            part = pl.ds(pl.multiple_of(begin, tile), tile)
            weighted = acts[part, :].astype(F32) * row_weight
            sums = jnp.sum(weighted, axis=1, keepdims=True)
            for r in range(chunks):
                row = to_row(sums[r * LANES : (r + 1) * LANES])
                vecs[k, pl.ds(begin // LANES + r, 1), :] = row
            acc[part, :] = jnp.dot(
                weighted.astype(BF16), s_ref[...], preferred_element_type=F32
            )

    def peer(b):
        digit = lax.rem(me // (2**b), 2)
        return digit, me + (1 - 2 * digit) * (2**b)

    def push_tiles(k, first, count):
        @pl.loop(0, count)
        def _(i):
            begin = first + i * tile
            part = pl.ds(pl.multiple_of(begin, tile), tile)
            mixture = jnp.dot(pulled[k, part, :], st_ref[...], preferred_element_type=F32)
            shift = [to_column(vecs[k, pl.ds(begin // LANES + r, 1), :]) for r in range(chunks)]
            mixture = mixture + jnp.concatenate(shift, axis=0)
            product = mixture * acts[part, :].astype(F32)
            rowsum[...] += jnp.sum(product.reshape(tile // 8, 8, slots), axis=0)

    def apply(k, row_weight):
        row_weight = row_weight / sample_total
        sums = jnp.sum(st_ref[own_visible, :].astype(F32) * row_weight, axis=1, keepdims=True)
        if visible < LANES:
            sums = jnp.concatenate([sums, jnp.zeros((LANES - visible, 1), F32)], axis=0)
        vecs[k, vis_row : vis_row + 1, :] = to_row(sums)

        rowsum[...] = jnp.zeros_like(rowsum)

        def mat_copy(source, target, sends, recvs, slot, partner):
            return pltpu.make_async_remote_copy(
                src_ref=source,
                dst_ref=target,
                send_sem=sends.at[k, slot],
                recv_sem=recvs.at[k, slot],
                device_id={"chain": partner},
                device_id_type=MESH,
            )

        def strand(c, order):
            size = hidden // strands
            start, place = c * size, c * (size + MIN_ROWS * bits)
            steps = []
            for b in order:
                digit, partner = peer(b)
                split = size // 2 >= MIN_ROWS
                moved = size // 2 if split else size
                away = start + (1 - digit) * moved if split else start
                keep = start + digit * moved if split else start
                away = pl.multiple_of(away, moved)
                keep = pl.multiple_of(keep, moved)
                if b == order[0]:
                    pull_tiles(k, away, moved // tile, row_weight)
                outbox[pl.ds(place, moved), :] = acc[pl.ds(away, moved), :].astype(BF16)
                box = pl.ds(place, moved)
                send = mat_copy(
                    outbox.at[box], inbox.at[box], mat_send, mat_recv, c * bits + b, partner
                )
                send.start()
                yield
                if b == order[0]:
                    pull_tiles(k, keep, moved // tile, row_weight)
                send.wait()
                own = acc[pl.ds(keep, moved), :]
                if not split:
                    own = own.astype(BF16).astype(F32)
                acc[pl.ds(keep, moved), :] = own + inbox[box, :].astype(F32)
                place += moved
                start, size = keep, moved
                steps.append((b, partner, split, keep, moved))
            pulled[k, pl.ds(start, size), :] = acc[pl.ds(start, size), :].astype(BF16)
            for b, partner, split, keep, moved in reversed(steps):
                if not split:
                    continue
                part = pulled.at[k, pl.ds(pl.multiple_of(keep, moved), moved)]
                send = mat_copy(part, part, back_send, back_recv, c * bits + b, partner)
                send.start()
                yield
                if b == order[0]:
                    push_tiles(k, keep, moved // tile)
                    yield
                send.wait()
                if b == order[0]:
                    other = 2 * c * (hidden // strands) + hidden // strands - moved - keep
                    push_tiles(k, other, moved // tile)

        def vec_strand():
            yield
            for b in range(bits):
                spread = pltpu.make_async_remote_copy(
                    src_ref=vecs.at[k],
                    dst_ref=vec_in.at[k, b],
                    send_sem=vec_send.at[k, b],
                    recv_sem=vec_recv.at[k, b],
                    device_id={"chain": peer(b)[1]},
                    device_id_type=MESH,
                )
                spread.start()
                yield
                spread.wait()
                vecs[k] = vecs[k] + vec_in[k, b]

        active = [strand(c, bit_order(c, bits)) for c in range(strands)] + [vec_strand()]
        while active:
            active = [one for one in active if next(one, active) is not active]
        seen = jnp.sum(rowsum[...], axis=0, keepdims=True)
        effect = to_column(vecs[k, vis_row : vis_row + 1, :])[:visible]
        seen = seen + jnp.sum(st_ref[own_visible, :].astype(F32) * effect, axis=0, keepdims=True)
        rows[k, rep, 0:1, :] = seen

        def row_copy(source, target):
            return pltpu.make_async_remote_copy(
                src_ref=rows.at[k, source, pl.ds(0, 1)],
                dst_ref=rows.at[k, source, pl.ds(0, 1)],
                send_sem=row_send.at[k, target],
                recv_sem=row_recv.at[k, source],
                device_id={"rep": target},
                device_id_type=MESH,
            )

        others = [lax.rem(rep + d, n_rep) for d in range(1, n_rep)]
        for other in others:
            row_copy(rep, other).start()
        for other in others:
            row_copy(other, other).wait_recv()
        for other in others:
            row_copy(rep, other).wait_send()
        whole = rows[k, 0, 0:1, :]
        for j in range(1, n_rep):
            whole = whole + rows[k, j, 0:1, :]
        return whole * live

    raw = apply(0, centered)
    middle = total(raw) / own_count
    local = (raw - middle) * live
    tell(1, [own_count, middle, total(local * local), total(raw * centered)])
    mean, spread, found = hear(1, 4)
    image = (raw - mean) * live
    dir_dir = found[2] + spread
    dir_wgt = found[3]
    resid_sq = dir_wgt
    dir_w, dir_o, dir_c = centered, image, [1.0, 0.0, 0.0]
    res_w, res_o, res_c = centered, image, [1.0, 0.0, 0.0]
    step = resid_sq / (dir_dir + DIAG_SHIFT * dir_wgt)
    ans_w, ans_o = step * dir_w, step * dir_o
    ans_c = [step * x for x in dir_c]
    norm = None
    for i in range(1, ITERS):
        raw = apply(i, dir_o)
        unit = [1.0 if j == i else 0.0 for j in range(ITERS)]
        res_w = res_w - step * (dir_o + DIAG_SHIFT * dir_w)
        res_c = [r - step * (u + DIAG_SHIFT * d) for r, u, d in zip(res_c, unit, dir_c)]
        fresh = res_o - step * (raw + DIAG_SHIFT * dir_o)
        middle = total(fresh * live) / own_count
        local = (fresh - middle) * live
        tell(i + 1, [
            own_count, middle, total(local * local), total(fresh * dir_o), total(fresh * res_w),
            total(fresh * dir_w), total(dir_o * res_w), total(fresh * ans_w),
            total(dir_o * ans_w), total(ans_o * ans_w),
        ])
        mean, spread, found = hear(i + 1, 10)
        res_o = (fresh - mean) * live
        _, _, res_res, res_dir, resid_next, res_dirw, dir_resw, res_ans, dir_ans, ans_ans = found
        res_res = res_res + spread
        ratio = resid_next / resid_sq
        new_dir = res_res + 2.0 * ratio * res_dir + ratio * ratio * dir_dir
        new_wgt = resid_next + ratio * (res_dirw + dir_resw) + ratio * ratio * dir_wgt
        mixed = res_ans + ratio * dir_ans
        dir_w = res_w + ratio * dir_w
        dir_o = res_o + ratio * dir_o
        dir_c = [r + ratio * d for r, d in zip(res_c, dir_c)]
        dir_dir, dir_wgt, resid_sq = new_dir, new_wgt, resid_next
        step = resid_sq / (dir_dir + DIAG_SHIFT * dir_wgt)
        norm = (ans_ans + 2.0 * step * mixed + step * step * dir_wgt) / sample_total
        ans_w, ans_o = ans_w + step * dir_w, ans_o + step * dir_o
        ans_c = [a + step * d for a, d in zip(ans_c, dir_c)]
    params = N_SITES * HIDDEN_SIZE + HIDDEN_SIZE + N_SITES
    scale = lax.rsqrt(norm / params + EPSILON)
    own_rows = mat_ref.shape[0]
    picks = lax.broadcasted_iota(jnp.int32, (MIN_ROWS, sites), 0) + me * own_rows
    picks = (picks == lax.broadcasted_iota(jnp.int32, (MIN_ROWS, sites), 1)).astype(BF16)
    for i in range(hidden // tile):
        part = slice(i * tile, (i + 1) * tile)
        out = 0.0
        for k in range(ITERS):
            piece = lax.dot_general(
                picks, pulled[k, part, :], (((1,), (1,)), ((), ())), preferred_element_type=F32
            )
            out = out + (ans_c[k] * scale) * piece
        mat_ref[:, part] = out[:own_rows]
    vec = 0.0
    for k in range(ITERS):
        vec = vec + (ans_c[k] * scale) * vecs[k]
    vec_ref[...] = vec


def wide_device(spins, energies, counts, accepted, hidden_bias, weights):
    n_chain = lax.axis_size("chain")
    n_rep = lax.axis_size("rep")
    slots, sites = spins.shape
    hidden = weights.shape[1]
    visible = sites // n_rep
    bits = n_chain.bit_length() - 1
    strands = min(MAX_STRANDS, hidden // 256)
    vec_rows = -(-(hidden // LANES + 1) // 8) * 8
    order = jnp.arange(slots, dtype=jnp.int32)
    names = jnp.where(order < counts[0], accepted[0], -1)
    live = jnp.any(order[:, None] == names[None, :], axis=1).astype(F32)
    vmem = pl.BlockSpec(memory_space=pltpu.VMEM)
    dma = pltpu.SemaphoreType.DMA
    mat, vec = pl.pallas_call(
        functools.partial(wide_kernel, n_chain, n_rep),
        out_shape=(
            jax.ShapeDtypeStruct((sites // n_chain, hidden), F32),
            jax.ShapeDtypeStruct((vec_rows, LANES), F32),
        ),
        in_specs=[vmem] * 6,
        out_specs=(vmem, vmem),
        scratch_shapes=[
            pltpu.VMEM((hidden, slots), BF16),
            pltpu.VMEM((hidden, sites), F32),
            pltpu.VMEM((hidden + strands * MIN_ROWS * bits, sites), BF16),
            pltpu.VMEM((hidden + strands * MIN_ROWS * bits, sites), BF16),
            pltpu.VMEM((ITERS, hidden, sites), BF16),
            pltpu.VMEM((ITERS, vec_rows, LANES), F32),
            pltpu.VMEM((ITERS, bits, vec_rows, LANES), F32),
            pltpu.VMEM((8, slots), F32),
            pltpu.VMEM((ITERS, n_rep, 8, slots), F32),
            pltpu.VMEM((ITERS + 1, n_chain, 8, LANES), F32),
            dma((ITERS, strands * bits)),
            dma((ITERS, strands * bits)),
            dma((ITERS, strands * bits)),
            dma((ITERS, strands * bits)),
            dma((ITERS, bits)),
            dma((ITERS, bits)),
            dma((ITERS, n_rep)),
            dma((ITERS, n_rep)),
            dma((ITERS + 1, n_chain)),
            dma((ITERS + 1, n_chain)),
        ],
        compiler_params=pltpu.CompilerParams(
            collective_id=0, has_side_effects=True, vmem_limit_bytes=60 * 1024 * 1024
        ),
    )(
        spins,
        spins.T,
        weights.T,
        hidden_bias.astype(F32).reshape(hidden // LANES, LANES),
        energies.astype(F32)[None],
        live[None],
    )
    flat = vec.reshape(-1)
    return flat[hidden : hidden + visible], flat[:hidden], mat


VMEM_LIMIT = 60 * 1024 * 1024
TAIL = 16
CORES = 2
PAIR = 2


def line_kernel(
    n_chain, s_ref, w_ref, aux_ref, names_ref, count_ref,
    mat_ref, hid_ref, vis_ref,
    samples, spins_t, acts, acc, hid_acc, bias_col, shift_col, w_t, w_in,
    outbox, inbox, tail_out, tail_in, push_mat, row_weight, partial, part_in, full, energies, tail_sum, flipped, final_in,
    line_send, line_recv, rep_send, rep_recv, sib_send, sib_recv, own_send, own_recv,
    en_send, en_recv, mat_send, mat_recv, tail_send, tail_recv, part_send, part_recv, full_send, full_recv,
    fin_send, fin_recv, load_sem, load_w_sem,
):
    slots, sites = s_ref.shape
    hidden = w_ref.shape[1]
    line = n_chain // (CORES * PAIR)
    blocks = line * CORES
    width = hidden // blocks
    tall = width + TAIL
    half = slots // 2
    half_rows = half // LANES
    tiles = slots // LANES
    piece = min(256, half)
    pieces = half // piece
    members = 2 * blocks
    line_rows = members * 8
    own_sites = mat_ref.shape[0]
    chunks = width // LANES
    sample_total = float(KEEP_DEV * n_chain)
    steps = line - 1
    arrivals = steps * pieces
    long_lag = 2 * pieces - 1

    me = lax.axis_index("chain")
    rep = lax.axis_index("rep")
    core = lax.rem(me, CORES)
    side = lax.rem(me // CORES, PAIR)
    z = me // (CORES * PAIR)
    block = z * CORES + core
    member = block * 2 + rep
    own_tile = side * members + member

    def chain_of(z_, side_, core_):
        return (z_ * PAIR + side_) * CORES + core_

    def device_of(m):
        b = m // 2
        return {"chain": chain_of(b // CORES, side, lax.rem(b, CORES)), "rep": lax.rem(m, 2)}

    everyone = PAIR * members
    load = pltpu.make_async_copy(s_ref, samples.at[block], load_sem)
    load.start()
    columns = pl.ds(pl.multiple_of(block * width, width), width)
    load_w = pltpu.make_async_copy(w_ref.at[:, columns], w_in, load_w_sem)
    load_w.start()
    barrier = pltpu.get_barrier_semaphore()

    def nearest(n):
        below, above = z, line - 1 - z
        near = jnp.minimum(below, above)
        paired = n < 2 * near
        dist = jnp.where(paired, n // 2 + 1, n - near + 1)
        upward = jnp.where(paired, lax.rem(n, 2) == 0, below > above)
        return upward, dist, jnp.where(upward, z - dist, z + dist)

    far_z = [nearest(line - 2 - n)[2] for n in range(line - 1)] + [z]

    def peers():
        for n in range(line):
            for turn in range(8):
                sides, cores, reps = turn < 4, turn % 2 == 0, turn % 4 < 2
                if n == line - 1 and not (sides or cores or reps):
                    continue
                yield (
                    far_z[n],
                    1 - side if sides else side,
                    1 - core if cores else core,
                    1 - rep if reps else rep,
                )

    for at_z, at_side, at_core, at_rep in peers():
        target = {"chain": chain_of(at_z, at_side, at_core), "rep": at_rep}
        pl.semaphore_signal(barrier, inc=1, device_id=target, device_id_type=MESH)

    names = names_ref[...]
    order = lax.broadcasted_iota(jnp.int32, (1, slots), 1)
    names = jnp.where(order < count_ref[0], names, -1)
    tile_no = names // LANES
    row_no = jnp.where(names < 0, -1, tile_no + jnp.where(tile_no >= half_rows, 8 - half_rows, 0))
    row_hot = (lax.broadcasted_iota(jnp.int32, (16, slots), 0) == row_no).astype(F32).astype(BF16)
    low = names - tile_no * LANES
    lane_hot = (lax.broadcasted_iota(jnp.int32, (LANES, slots), 0) == low).astype(F32).astype(BF16)
    live_own = lax.dot_general(
        row_hot, lane_hot, (((1,), (1,)), ((), ())), preferred_element_type=F32
    )
    slot_no = side * blocks + block
    energies[slot_no] = (aux_ref[0:16, :] * live_own).astype(BF16)
    load.wait()
    load_w.wait()
    pl.semaphore_wait(barrier, everyone - 1)

    def batch(place, send, recv):
        return pltpu.make_async_remote_copy(
            src_ref=place,
            dst_ref=place,
            send_sem=send,
            recv_sem=recv,
            device_id={"chain": chain_of(z, side, 1 - core)},
            device_id_type=MESH,
        )

    def part_rows(r, p):
        return pl.ds(pl.multiple_of(r * half + p * piece, piece), piece)

    def line_copy(d, s, p, from_z, to_z):
        place = samples.at[from_z * CORES + core, part_rows(rep, p)]
        return pltpu.make_async_remote_copy(
            src_ref=place,
            dst_ref=place,
            send_sem=line_send.at[d, s, p],
            recv_sem=line_recv.at[d, s, p],
            device_id={"chain": chain_of(to_z, side, core)},
            device_id_type=MESH,
        )

    def own_copy(b):
        return pltpu.make_async_remote_copy(
            src_ref=samples.at[b],
            dst_ref=samples.at[b],
            send_sem=own_send,
            recv_sem=own_recv,
            device_id={"chain": chain_of(z, side, 1 - core)},
            device_id_type=MESH,
        )

    def rep_copy(it, from_z, r, p):
        place = samples.at[from_z * CORES + core, part_rows(r, p)]
        return pltpu.make_async_remote_copy(
            src_ref=place,
            dst_ref=place,
            send_sem=rep_send.at[it],
            recv_sem=rep_recv.at[it],
            device_id={"rep": 1 - rep},
            device_id_type=MESH,
        )

    def sib_copy(kind, it, from_z, c, r, p):
        place = samples.at[from_z * CORES + c, part_rows(r, p)]
        return pltpu.make_async_remote_copy(
            src_ref=place,
            dst_ref=place,
            send_sem=sib_send.at[kind, it],
            recv_sem=sib_recv.at[kind, it],
            device_id={"chain": chain_of(z, side, 1 - core)},
            device_id_type=MESH,
        )

    for at_z, at_side, at_core, at_rep in peers():
        if at_rep is rep:
            pltpu.make_async_remote_copy(
                src_ref=energies.at[slot_no],
                dst_ref=energies.at[slot_no],
                send_sem=en_send,
                recv_sem=en_recv,
                device_id={"chain": chain_of(at_z, at_side, at_core)},
                device_id_type=MESH,
            ).start()

    for p in range(pieces):
        @pl.when(z + 1 < line)
        def _():
            line_copy(0, 0, p, z, z + 1).start()

        @pl.when(z > 0)
        def _():
            line_copy(1, 0, p, z, z - 1).start()
    own_copy(block).start()

    w_t[...] = jnp.transpose(w_in[...])
    for r in range(chunks):
        bias = to_column(aux_ref[pl.ds(16 + block * chunks + r, 1), :])
        bias_col[r * LANES : (r + 1) * LANES, :] = jnp.broadcast_to(bias, (LANES, LANES))
    partial[...] = jnp.zeros_like(partial)
    tail = lax.broadcasted_iota(jnp.int32, (TAIL, slots), 0)
    ones = (tail == 0).astype(F32).astype(BF16)

    @pl.loop(0, blocks)
    def _(j):
        acts[j, width:, :] = ones

    batch(energies.at[pl.ds(0, n_chain - 1)], en_send, en_recv).wait_recv()

    energy = energies[...].astype(F32).reshape(PAIR * line_rows, LANES)
    live = (energy != 0.0).astype(F32)

    def sum_all(values):
        return total(jnp.sum(values, axis=0, keepdims=True))

    centered = (energy - sum_all(energy) / sample_total) * live

    row_weight[...] = centered / sample_total
    acc[...] = jnp.zeros_like(acc)
    hid_acc[...] = jnp.zeros_like(hid_acc)
    tail_lane = lax.broadcasted_iota(jnp.int32, (TAIL, LANES), 0)
    tail_row = lax.broadcasted_iota(jnp.int32, (TAIL, sites), 0)

    def weigh(held, b, r, p, sums):
        parts = []
        for e in range(piece // LANES):
            row = side * line_rows + b * 16 + r * 8 + p * (piece // LANES) + e
            scale = row_weight[pl.ds(row, 1), :]
            scaled = held[:, e * LANES : (e + 1) * LANES].astype(F32) * scale
            sums = sums + scaled
            high = scale.astype(BF16).astype(F32)
            ends = jnp.where(tail_lane == 0, high, jnp.where(tail_lane == 1, scale - high, 0.0))
            parts.append(jnp.concatenate([scaled, ends], axis=0).astype(BF16))
        return parts, sums

    def process(places):
        rows = [samples[b, part_rows(r, p), :] for b, r, p in places]
        got = [jnp.transpose(part) for part in rows]
        bias = jnp.concatenate([bias_col[...]] * (piece // LANES), axis=1)
        found = [
            jnp.tanh(jnp.dot(w_t[...], part, preferred_element_type=F32) + bias).astype(BF16)
            for part in got
        ]
        parts, sums = [], hid_acc[...]
        for (b, r, p), part in zip(places, found):
            more, sums = weigh(part, b, r, p, sums)
            parts += more
        pulled = jnp.dot(
            jnp.concatenate(parts, axis=1),
            jnp.concatenate(rows, axis=0),
            preferred_element_type=F32,
        )
        hid_acc[...] = sums
        acc[...] += pulled
        for (b, r, p), flip, act in zip(places, got, found):
            lanes = pl.ds(pl.multiple_of(r * half + p * piece, piece), piece)
            spins_t[b, :, lanes] = flip
            acts[b, 0:width, lanes] = act

    other = z * CORES + 1 - core
    own_copy(other).wait_recv()

    def arrival(it):
        both = it // pieces < 2 * jnp.minimum(z, line - 1 - z)
        spot = lax.rem(it, 2 * pieces)
        n = jnp.where(both, it // (2 * pieces) * 2 + lax.rem(spot, 2), it // pieces)
        p = jnp.where(both, spot // 2, lax.rem(it, pieces))
        upward, dist, from_z = nearest(n)
        return jnp.where(upward, 0, 1), dist - 1, p, from_z

    lag = jnp.where(jnp.minimum(z, line - 1 - z) > 0, long_lag, pieces - 1)

    @pl.loop(0, arrivals + long_lag + 1)
    def _(it):
        @pl.when(it < arrivals)
        def _():
            d, s, p, from_z = arrival(it)
            line_copy(d, s, p, from_z, z).wait_recv()
            to_z = z + 1 - 2 * d

            @pl.when(jnp.logical_and(to_z >= 0, to_z < line))
            def _():
                line_copy(d, s + 1, p, from_z, to_z).start()

            rep_copy(it, from_z, rep, p).start()
            sib_copy(0, it, from_z, core, rep, p).start()

        @pl.when(jnp.logical_and(it >= lag, it < arrivals + lag))
        def _():
            last = it - lag
            _, _, p, from_z = arrival(last)
            rep_copy(last, from_z, 1 - rep, p).wait_recv()
            sib_copy(1, last, from_z, core, 1 - rep, p).start()

        fresh = it < pieces
        ripe = jnp.logical_and(it > lag, it <= arrivals + lag)
        last = jnp.clip(it - lag - 1, 0, arrivals - 1)
        _, _, last_p, last_z = arrival(last)
        p = jnp.where(fresh, it, last_p)
        at_z = jnp.where(fresh, z, last_z)
        b = at_z * CORES + core
        other = at_z * CORES + 1 - core

        @pl.when(ripe)
        def _():
            sib_copy(0, last, last_z, 1 - core, rep, p).wait_recv()
            sib_copy(1, last, last_z, 1 - core, 1 - rep, p).wait_recv()

        @pl.when(jnp.logical_or(fresh, ripe))
        def _():
            process([(b, rep, p), (other, rep, p), (b, 1 - rep, p), (other, 1 - rep, p)])

    def mat_copy(k):
        return pltpu.make_async_remote_copy(
            src_ref=outbox.at[k],
            dst_ref=inbox.at[k],
            send_sem=mat_send.at[k],
            recv_sem=mat_recv.at[k],
            device_id={"chain": chain_of(z, 1 - side, core)},
            device_id_type=MESH,
        )

    def tail_copy(k):
        return pltpu.make_async_remote_copy(
            src_ref=tail_out.at[k],
            dst_ref=tail_in.at[k],
            send_sem=tail_send.at[k],
            recv_sem=tail_recv.at[k],
            device_id={"chain": chain_of(z, 1 - side, core)},
            device_id_type=MESH,
        )

    def part_copy(k, source, target):
        return pltpu.make_async_remote_copy(
            src_ref=partial.at[k, target],
            dst_ref=part_in.at[k, source],
            send_sem=part_send.at[k],
            recv_sem=part_recv.at[k],
            device_id=device_of(target),
            device_id_type=MESH,
        )

    def part_batch(k):
        return batch(part_in.at[k, pl.ds(0, members - 1)], part_send.at[k], part_recv.at[k])

    def full_batch(k):
        return batch(full.at[k, pl.ds(0, everyone - 1)], full_send.at[k], full_recv.at[k])

    def final_batch(k):
        return batch(final_in.at[k, pl.ds(0, blocks - 1)], fin_send.at[k], fin_recv.at[k])

    def final_start(k):
        for at_z, at_side, at_core, at_rep in peers():
            if at_rep is rep and at_side is side:
                target = chain_of(at_z, side, at_core)
                begin = pl.multiple_of(target * own_sites, own_sites)
                pltpu.make_async_remote_copy(
                    src_ref=flipped.at[k, pl.ds(begin, own_sites)],
                    dst_ref=final_in.at[k, block],
                    send_sem=fin_send.at[k],
                    recv_sem=fin_recv.at[k],
                    device_id={"chain": target},
                    device_id_type=MESH,
                ).start()

    def pull(k, weight):
        row_weight[...] = weight / sample_total
        acc[...] = jnp.zeros_like(acc)
        hid_acc[...] = jnp.zeros_like(hid_acc)

        @pl.loop(0, blocks)
        def _(j):
            parts = []
            sums = hid_acc[...]
            for r in range(2):
                for p in range(pieces):
                    begin = r * half + p * piece
                    more, sums = weigh(acts[j, 0:width, begin : begin + piece], j, r, p, sums)
                    parts += more
            hid_acc[...] = sums
            acc[...] += jnp.dot(
                jnp.concatenate(parts, axis=1), samples[j], preferred_element_type=F32
            )

    def apply(k, meanwhile):
        sums = jnp.sum(hid_acc[...], axis=1, keepdims=True)
        hid_row = jnp.concatenate(
            [to_row(sums[r * LANES : (r + 1) * LANES]) for r in range(chunks)], axis=1
        )
        if width < sites:
            hid_row = jnp.concatenate([hid_row, jnp.zeros((1, sites - width), F32)], axis=1)
        vis_row = acc[width : width + 1, :] + acc[width + 1 : width + 2, :]
        outbox[k] = acc[0:width, :].astype(BF16)
        tail_out[k] = jnp.concatenate([vis_row, hid_row, jnp.zeros((6, sites), F32)], axis=0)
        tail_copy(k).start()
        mat_copy(k).start()
        meanwhile()
        mat_copy(k).wait()
        tail_copy(k).wait()
        whole = outbox[k].astype(F32) + inbox[k].astype(F32)
        rest = tail_out[k] + tail_in[k]
        tail_sum[k] = rest
        push_mat[0:width, :] = whole.astype(BF16)
        rest = jnp.concatenate([rest, jnp.zeros((TAIL - 8, sites), F32)], axis=0)
        push_mat[width:, :] = jnp.where(tail_row == 0, rest / members, 0.0).astype(BF16)
        for r in range(chunks):
            shift = to_column(rest[1:2, r * LANES : (r + 1) * LANES])
            shift_col[r * LANES : (r + 1) * LANES, :] = jnp.broadcast_to(shift, (LANES, LANES))
        shift_col[width:, :] = jnp.zeros((TAIL, LANES), F32)

        @pl.loop(0, members)
        def _(i):
            turn = lax.rem(i, 4)
            _, _, far_z = nearest(jnp.maximum(line - 2 - i // 4, 0))
            at_z = jnp.where(i // 4 == line - 1, z, far_z)
            at_core = lax.rem(core + jnp.where(lax.rem(turn, 2) == 0, 1, 0), CORES)
            at_rep = lax.rem(rep + jnp.where(turn < 2, 1, 0), 2)
            j = at_z * CORES + at_core
            target = j * 2 + at_rep
            shift = shift_col[...]
            for p in range(pieces):
                begin = at_rep * half + p * piece
                mixture = jnp.dot(
                    push_mat[...],
                    spins_t[j, :, pl.ds(pl.multiple_of(begin, piece), piece)],
                    preferred_element_type=F32,
                )
                for e in range(piece // LANES):
                    lanes = pl.ds(pl.multiple_of(begin + e * LANES, LANES), LANES)
                    mix = mixture[:, e * LANES : (e + 1) * LANES] + shift
                    mix = mix * acts[j, :, lanes].astype(F32)
                    row = p * (piece // LANES) + e
                    partial[k, target, row : row + 1, :] = jnp.sum(mix, axis=0, keepdims=True)

            @pl.when(i < members - 1)
            def _():
                part_copy(k, member, target).start()

        flipped[k] = jnp.transpose(push_mat[0:width, :])

        final_start(k)
        own_begin = pl.multiple_of(me * own_sites, own_sites)
        final_in[k, block] = flipped[k, pl.ds(own_begin, own_sites), :]
        part_in[k, member] = partial[k, member]

        part_batch(k).wait_recv()

        full[k, own_tile] = jnp.sum(part_in[k], axis=0)
        for r in range(chunks):
            full[k, own_tile, half_rows + r : half_rows + r + 1, :] = tail_sum[
                k, 1:2, r * LANES : (r + 1) * LANES
            ]

        for at_z, at_side, at_core, at_rep in peers():
            pltpu.make_async_remote_copy(
                src_ref=full.at[k, own_tile],
                dst_ref=full.at[k, own_tile],
                send_sem=full_send.at[k],
                recv_sem=full_recv.at[k],
                device_id={"chain": chain_of(at_z, at_side, at_core), "rep": at_rep},
                device_id_type=MESH,
            ).start()

        full_batch(k).wait_recv()
        return full[k].reshape(PAIR * line_rows, LANES)

    def center(values):
        return (values - sum_all(values * live) / sample_total) * live

    state = {}

    def nothing():
        pass

    def first():
        resid_sq = sum_all(image * centered)
        state["resid_sq"] = resid_sq
        state["dir"] = centered, image, [1.0, 0.0, 0.0]
        state["res"] = centered, image, [1.0, 0.0, 0.0]
        advance(sum_all(image * image), resid_sq, None)

    def advance(dir_dir, dir_wgt, before):
        step = state["resid_sq"] / (dir_dir + DIAG_SHIFT * dir_wgt)
        dir_w, dir_o, dir_c = state["dir"]
        if before is None:
            ans = step * dir_w, step * dir_o, [step * x for x in dir_c]
        else:
            ans_w, ans_o, ans_c = before
            ans = (
                ans_w + step * dir_w,
                ans_o + step * dir_o,
                [a + step * d for a, d in zip(ans_c, dir_c)],
            )
        state["step"], state["ans"] = step, ans

    def follow():
        dir_w, dir_o, _ = state["dir"]
        advance(sum_all(dir_o * dir_o), sum_all(dir_w * dir_o), state["ans"])

    def turn_to(i, raw):
        step = state["step"]
        dir_w, dir_o, dir_c = state["dir"]
        res_w, res_o, res_c = state["res"]
        unit = [1.0 if j == i else 0.0 for j in range(ITERS)]
        res_w = res_w - step * (dir_o + DIAG_SHIFT * dir_w)
        res_c = [r - step * (u + DIAG_SHIFT * d) for r, u, d in zip(res_c, unit, dir_c)]
        res_o = center(res_o - step * (raw + DIAG_SHIFT * dir_o))
        resid_next = sum_all(res_w * res_o)
        ratio = resid_next / state["resid_sq"]
        state["resid_sq"] = resid_next
        state["res"] = res_w, res_o, res_c
        state["dir"] = (
            res_w + ratio * dir_w,
            res_o + ratio * dir_o,
            [r + ratio * d for r, d in zip(res_c, dir_c)],
        )

    image = center(apply(0, nothing))
    pull(1, image)
    raw = apply(1, first)
    for i in range(1, ITERS):
        turn_to(i, raw)
        if i + 1 < ITERS:
            pull(i + 1, state["dir"][1])
            raw = apply(i + 1, follow)
        else:
            follow()
    ans_w, ans_o, ans_c = state["ans"]
    norm = sum_all(ans_w * ans_o) / sample_total
    params = N_SITES * HIDDEN_SIZE + HIDDEN_SIZE + N_SITES
    scale = lax.rsqrt(norm / params + EPSILON)
    mix_c = [c * scale for c in ans_c]

    for k in range(ITERS):
        final_batch(k).wait_recv()

    answer = 0.0
    for k in range(ITERS):
        answer = answer + mix_c[k] * tail_sum[k]
    for b in range(blocks):
        out = 0.0
        for k in range(ITERS):
            out = out + mix_c[k] * final_in[k, b].astype(F32)
        mat_ref[:, b * width : (b + 1) * width] = out
        out = 0.0
        for k in range(ITERS):
            out = out + mix_c[k] * full[k, side * members + 2 * b + rep]
        hid_ref[b * chunks : (b + 1) * chunks, :] = out[half_rows : half_rows + chunks]
    visible = sites // 2
    vis_row = answer[0:1, :]
    vis_ref[...] = jnp.where(rep == 0, vis_row[:, :visible], vis_row[:, visible:])

    @pl.loop(0, arrivals)
    def _(it):
        _, _, p, from_z = arrival(it)
        rep_copy(it, from_z, rep, p).wait_send()
        sib_copy(0, it, from_z, core, rep, p).wait_send()
        sib_copy(1, it, from_z, core, 1 - rep, p).wait_send()

    for s in range(steps):
        for p in range(pieces):
            @pl.when(jnp.logical_and(z + 1 < line, z - s >= 0))
            def _():
                line_copy(0, s, p, z - s, z + 1).wait_send()

            @pl.when(jnp.logical_and(z > 0, z + s < line))
            def _():
                line_copy(1, s, p, z + s, z - 1).wait_send()
    own_copy(block).wait_send()

    batch(energies.at[pl.ds(0, n_chain - 1)], en_send, en_recv).wait_send()
    for k in range(ITERS):
        final_batch(k).wait_send()
        part_batch(k).wait_send()
        full_batch(k).wait_send()


def line_fits(n_chain, n_rep, slots, sites, hidden):
    blocks = n_chain // PAIR
    if n_rep != 2 or n_chain % (CORES * PAIR) or n_chain < 2 * CORES * PAIR:
        return False
    if hidden % (blocks * LANES) or sites != 2 * LANES or hidden // blocks > sites:
        return False
    half = slots // 2
    if slots % (2 * LANES) or half % min(256, half) or sites % (16 * n_chain):
        return False
    if half // LANES + hidden // blocks // LANES > 8:
        return False
    held = 2 * blocks * slots * (2 * sites + hidden // blocks + TAIL)
    return 2 * held < VMEM_LIMIT


def per_device(spins, energies, counts, accepted, hidden_bias, weights):
    n_chain = lax.axis_size("chain")
    n_rep = lax.axis_size("rep")
    slots, sites = spins.shape
    hidden = weights.shape[1]
    if not line_fits(n_chain, n_rep, slots, sites, hidden):
        return wide_device(spins, energies, counts, accepted, hidden_bias, weights)
    blocks = n_chain // PAIR
    line = blocks // CORES
    width = hidden // blocks
    tall = width + TAIL
    half = slots // 2
    pieces = half // min(256, half)
    arrivals = (line - 1) * pieces
    members = 2 * blocks
    rows = PAIR * members
    own_sites = sites // n_chain
    energy = energies.astype(F32).reshape(2, half // LANES, LANES)
    energy = jnp.pad(energy, ((0, 0), (0, 8 - half // LANES), (0, 0))).reshape(16, LANES)
    aux = jnp.concatenate([energy, hidden_bias.astype(F32).reshape(hidden // LANES, LANES)], axis=0)
    vmem = pl.BlockSpec(memory_space=pltpu.VMEM)
    dma = pltpu.SemaphoreType.DMA
    mat, hid, vis = pl.pallas_call(
        functools.partial(line_kernel, n_chain),
        out_shape=(
            jax.ShapeDtypeStruct((own_sites, hidden), F32),
            jax.ShapeDtypeStruct((hidden // LANES, LANES), F32),
            jax.ShapeDtypeStruct((1, sites // 2), F32),
        ),
        in_specs=[pl.BlockSpec(memory_space=pl.ANY)] * 2 + [vmem] * 2 + [pl.BlockSpec(memory_space=pltpu.SMEM)],
        out_specs=(vmem, vmem, vmem),
        scratch_shapes=[
            pltpu.VMEM((blocks, slots, sites), BF16),
            pltpu.VMEM((blocks, sites, slots), BF16),
            pltpu.VMEM((blocks, tall, slots), BF16),
            pltpu.VMEM((tall, sites), F32),
            pltpu.VMEM((width, LANES), F32),
            pltpu.VMEM((width, LANES), F32),
            pltpu.VMEM((tall, LANES), F32),
            pltpu.VMEM((width, sites), BF16),
            pltpu.VMEM((sites, width), BF16),
            pltpu.VMEM((ITERS, width, sites), BF16),
            pltpu.VMEM((ITERS, width, sites), BF16),
            pltpu.VMEM((ITERS, 8, sites), F32),
            pltpu.VMEM((ITERS, 8, sites), F32),
            pltpu.VMEM((tall, sites), BF16),
            pltpu.VMEM((rows * 8, LANES), F32),
            pltpu.VMEM((ITERS, members, 8, LANES), F32),
            pltpu.VMEM((ITERS, members, 8, LANES), F32),
            pltpu.VMEM((ITERS, rows, 8, LANES), F32),
            pltpu.VMEM((n_chain, 16, LANES), BF16),
            pltpu.VMEM((ITERS, 8, sites), F32),
            pltpu.VMEM((ITERS, sites, width), BF16),
            pltpu.VMEM((ITERS, blocks, own_sites, width), BF16),
            dma((2, line - 1, pieces)),
            dma((2, line - 1, pieces)),
            dma((arrivals,)),
            dma((arrivals,)),
            dma((2, arrivals)),
            dma((2, arrivals)),
            dma,
            dma,
            dma,
            dma,
            dma((ITERS,)),
            dma((ITERS,)),
            dma((ITERS,)),
            dma((ITERS,)),
            dma((ITERS,)),
            dma((ITERS,)),
            dma((ITERS,)),
            dma((ITERS,)),
            dma((ITERS,)),
            dma((ITERS,)),
            dma,
            dma,
        ],
        compiler_params=pltpu.CompilerParams(
            collective_id=0, has_side_effects=True, vmem_limit_bytes=VMEM_LIMIT
        ),
    )(spins, weights, aux, accepted, counts)
    return vis.reshape(-1), hid.reshape(-1), mat


def solution(mesh):
    in_specs = (
        P("chain", None),
        P("chain"),
        P("chain"),
        P("chain", None),
        P("rep"),
        P(None, "rep"),
    )
    out_specs = (P("rep"), P("rep"), P("chain", "rep"))
    return jax.shard_map(
        per_device, mesh=mesh, in_specs=in_specs, out_specs=out_specs, check_vma=False
    )
```

```python
import functools

import jax
import jax.numpy as jnp
from jax import lax
from jax.experimental import pallas as pl
from jax.experimental.pallas import tpu as pltpu
from jax.sharding import PartitionSpec as P

N_SITES = 256
HIDDEN_SIZE = 4096
KEEP_DEV = 768
ITERS = 3

DIAG_SHIFT = 0.05
EPSILON = 1e-06
LANES = 128
MAX_STRANDS = 4
MIN_ROWS = 16
MESH = pl.DeviceIdType.MESH
F32 = jnp.float32
BF16 = jnp.bfloat16


def to_row(column):
    return jnp.transpose(jnp.broadcast_to(column, (LANES, LANES)))[:1, :]


def to_column(row):
    return jnp.transpose(jnp.broadcast_to(row, (LANES, LANES)))[:, :1]


def bit_order(strand, bits):
    rest = list(range(1, bits - 1))
    turn = strand % len(rest)
    return [0] + rest[turn:] + rest[:turn] + [bits - 1]


def total(values):
    return jnp.sum(values, axis=1, keepdims=True)


def wide_kernel(
    n_chain, n_rep, s_ref, st_ref, wt_ref, bias_ref, energy_ref, live_ref,
    mat_ref, vec_ref, acts, acc, outbox, inbox, pulled, vecs, vec_in, rowsum, rows, gathered,
    mat_send, mat_recv, back_send, back_recv, vec_send, vec_recv, row_send, row_recv,
    tell_send, tell_recv,
):
    slots, sites = s_ref.shape
    hidden = wt_ref.shape[0]
    visible = sites // n_rep
    sample_total = float(KEEP_DEV * n_chain)
    bits = n_chain.bit_length() - 1
    strands = min(MAX_STRANDS, hidden // 256)
    tile = min(256, hidden // (2 * strands))
    chunks = tile // LANES
    vis_row = hidden // LANES
    me = lax.axis_index("chain")
    rep = lax.axis_index("rep")
    lane = lax.broadcasted_iota(jnp.int32, (1, LANES), 1)

    barrier = pltpu.get_barrier_semaphore()

    @pl.loop(1, n_chain)
    def _(k):
        pl.semaphore_signal(
            barrier, inc=1, device_id={"chain": lax.rem(me + k, n_chain)}, device_id_type=MESH
        )

    for k in range(1, n_rep):
        pl.semaphore_signal(
            barrier, inc=1, device_id={"rep": lax.rem(rep + k, n_rep)}, device_id_type=MESH
        )
    pl.semaphore_wait(barrier, n_chain - 1 + n_rep - 1)

    def tell_copy(sync, source, target):
        return pltpu.make_async_remote_copy(
            src_ref=gathered.at[sync, source],
            dst_ref=gathered.at[sync, source],
            send_sem=tell_send.at[sync, target],
            recv_sem=tell_recv.at[sync, source],
            device_id={"chain": target},
            device_id_type=MESH,
        )

    def tell(sync, values):
        packed = jnp.zeros((1, LANES), F32)
        for j, value in enumerate(values):
            packed = jnp.where(lane == j, value, packed)
        weight = jnp.broadcast_to(values[0], (1, LANES))
        middle = jnp.broadcast_to(values[1], (1, LANES))
        blank = jnp.zeros((5, LANES), F32)
        gathered[sync, me] = jnp.concatenate([packed, weight, middle, blank], axis=0)

        @pl.loop(1, n_chain)
        def _(k):
            tell_copy(sync, me, lax.rem(me + k, n_chain)).start()

    def hear(sync, count):
        @pl.loop(1, n_chain)
        def _(k):
            tell_copy(sync, lax.rem(me + k, n_chain), lax.rem(me + k, n_chain)).wait_recv()

        @pl.loop(1, n_chain)
        def _(k):
            tell_copy(sync, me, lax.rem(me + k, n_chain)).wait_send()

        everyone = [gathered[sync, j] for j in range(n_chain)]
        packed = everyone[0][0:1]
        weighted = everyone[0][1:2] * everyone[0][2:3]
        for one in everyone[1:]:
            packed = packed + one[0:1]
            weighted = weighted + one[1:2] * one[2:3]
        mean = weighted / sample_total
        spread = jnp.zeros((1, LANES), F32)
        for one in everyone:
            spread = spread + one[1:2] * (one[2:3] - mean) * (one[2:3] - mean)
        found = [total(jnp.where(lane == j, packed, 0.0)) for j in range(count)]
        return mean[:, :1], spread[:, :1], found

    vecs[...] = jnp.zeros_like(vecs)
    live = live_ref[...]
    own_count = total(live)
    energy = energy_ref[...]
    tell(0, [own_count, total(energy * live) / own_count])

    @pl.loop(0, hidden // tile)
    def _(i):
        part = pl.ds(pl.multiple_of(i * tile, tile), tile)
        preact = jnp.dot(wt_ref[part, :], st_ref[...], preferred_element_type=F32)
        bias = [to_column(bias_ref[pl.ds(i * chunks + r, 1), :]) for r in range(chunks)]
        acts[part, :] = jnp.tanh(preact + jnp.concatenate(bias, axis=0)).astype(BF16)

    mean_energy, _, _ = hear(0, 0)
    centered = (energy - mean_energy) * live

    own_visible = pl.ds(pl.multiple_of(rep * visible, visible), visible)

    def pull_tiles(k, first, count, row_weight):
        @pl.loop(0, count)
        def _(i):
            begin = first + i * tile
            part = pl.ds(pl.multiple_of(begin, tile), tile)
            weighted = acts[part, :].astype(F32) * row_weight
            sums = jnp.sum(weighted, axis=1, keepdims=True)
            for r in range(chunks):
                row = to_row(sums[r * LANES : (r + 1) * LANES])
                vecs[k, pl.ds(begin // LANES + r, 1), :] = row
            acc[part, :] = jnp.dot(
                weighted.astype(BF16), s_ref[...], preferred_element_type=F32
            )

    def peer(b):
        digit = lax.rem(me // (2**b), 2)
        return digit, me + (1 - 2 * digit) * (2**b)

    def push_tiles(k, first, count):
        @pl.loop(0, count)
        def _(i):
            begin = first + i * tile
            part = pl.ds(pl.multiple_of(begin, tile), tile)
            mixture = jnp.dot(pulled[k, part, :], st_ref[...], preferred_element_type=F32)
            shift = [to_column(vecs[k, pl.ds(begin // LANES + r, 1), :]) for r in range(chunks)]
            mixture = mixture + jnp.concatenate(shift, axis=0)
            product = mixture * acts[part, :].astype(F32)
            rowsum[...] += jnp.sum(product.reshape(tile // 8, 8, slots), axis=0)

    def apply(k, row_weight):
        row_weight = row_weight / sample_total
        sums = jnp.sum(st_ref[own_visible, :].astype(F32) * row_weight, axis=1, keepdims=True)
        if visible < LANES:
            sums = jnp.concatenate([sums, jnp.zeros((LANES - visible, 1), F32)], axis=0)
        vecs[k, vis_row : vis_row + 1, :] = to_row(sums)

        rowsum[...] = jnp.zeros_like(rowsum)

        def mat_copy(source, target, sends, recvs, slot, partner):
            return pltpu.make_async_remote_copy(
                src_ref=source,
                dst_ref=target,
                send_sem=sends.at[k, slot],
                recv_sem=recvs.at[k, slot],
                device_id={"chain": partner},
                device_id_type=MESH,
            )

        def strand(c, order):
            size = hidden // strands
            start, place = c * size, c * (size + MIN_ROWS * bits)
            steps = []
            for b in order:
                digit, partner = peer(b)
                split = size // 2 >= MIN_ROWS
                moved = size // 2 if split else size
                away = start + (1 - digit) * moved if split else start
                keep = start + digit * moved if split else start
                away = pl.multiple_of(away, moved)
                keep = pl.multiple_of(keep, moved)
                if b == order[0]:
                    pull_tiles(k, away, moved // tile, row_weight)
                outbox[pl.ds(place, moved), :] = acc[pl.ds(away, moved), :].astype(BF16)
                box = pl.ds(place, moved)
                send = mat_copy(
                    outbox.at[box], inbox.at[box], mat_send, mat_recv, c * bits + b, partner
                )
                send.start()
                yield
                if b == order[0]:
                    pull_tiles(k, keep, moved // tile, row_weight)
                send.wait()
                own = acc[pl.ds(keep, moved), :]
                if not split:
                    own = own.astype(BF16).astype(F32)
                acc[pl.ds(keep, moved), :] = own + inbox[box, :].astype(F32)
                place += moved
                start, size = keep, moved
                steps.append((b, partner, split, keep, moved))
            pulled[k, pl.ds(start, size), :] = acc[pl.ds(start, size), :].astype(BF16)
            for b, partner, split, keep, moved in reversed(steps):
                if not split:
                    continue
                part = pulled.at[k, pl.ds(pl.multiple_of(keep, moved), moved)]
                send = mat_copy(part, part, back_send, back_recv, c * bits + b, partner)
                send.start()
                yield
                if b == order[0]:
                    push_tiles(k, keep, moved // tile)
                    yield
                send.wait()
                if b == order[0]:
                    other = 2 * c * (hidden // strands) + hidden // strands - moved - keep
                    push_tiles(k, other, moved // tile)

        def vec_strand():
            yield
            for b in range(bits):
                spread = pltpu.make_async_remote_copy(
                    src_ref=vecs.at[k],
                    dst_ref=vec_in.at[k, b],
                    send_sem=vec_send.at[k, b],
                    recv_sem=vec_recv.at[k, b],
                    device_id={"chain": peer(b)[1]},
                    device_id_type=MESH,
                )
                spread.start()
                yield
                spread.wait()
                vecs[k] = vecs[k] + vec_in[k, b]

        active = [strand(c, bit_order(c, bits)) for c in range(strands)] + [vec_strand()]
        while active:
            active = [one for one in active if next(one, active) is not active]
        seen = jnp.sum(rowsum[...], axis=0, keepdims=True)
        effect = to_column(vecs[k, vis_row : vis_row + 1, :])[:visible]
        seen = seen + jnp.sum(st_ref[own_visible, :].astype(F32) * effect, axis=0, keepdims=True)
        rows[k, rep, 0:1, :] = seen

        def row_copy(source, target):
            return pltpu.make_async_remote_copy(
                src_ref=rows.at[k, source, pl.ds(0, 1)],
                dst_ref=rows.at[k, source, pl.ds(0, 1)],
                send_sem=row_send.at[k, target],
                recv_sem=row_recv.at[k, source],
                device_id={"rep": target},
                device_id_type=MESH,
            )

        others = [lax.rem(rep + d, n_rep) for d in range(1, n_rep)]
        for other in others:
            row_copy(rep, other).start()
        for other in others:
            row_copy(other, other).wait_recv()
        for other in others:
            row_copy(rep, other).wait_send()
        whole = rows[k, 0, 0:1, :]
        for j in range(1, n_rep):
            whole = whole + rows[k, j, 0:1, :]
        return whole * live

    raw = apply(0, centered)
    middle = total(raw) / own_count
    local = (raw - middle) * live
    tell(1, [own_count, middle, total(local * local), total(raw * centered)])
    mean, spread, found = hear(1, 4)
    image = (raw - mean) * live
    dir_dir = found[2] + spread
    dir_wgt = found[3]
    resid_sq = dir_wgt
    dir_w, dir_o, dir_c = centered, image, [1.0, 0.0, 0.0]
    res_w, res_o, res_c = centered, image, [1.0, 0.0, 0.0]
    step = resid_sq / (dir_dir + DIAG_SHIFT * dir_wgt)
    ans_w, ans_o = step * dir_w, step * dir_o
    ans_c = [step * x for x in dir_c]
    norm = None
    for i in range(1, ITERS):
        raw = apply(i, dir_o)
        unit = [1.0 if j == i else 0.0 for j in range(ITERS)]
        res_w = res_w - step * (dir_o + DIAG_SHIFT * dir_w)
        res_c = [r - step * (u + DIAG_SHIFT * d) for r, u, d in zip(res_c, unit, dir_c)]
        fresh = res_o - step * (raw + DIAG_SHIFT * dir_o)
        middle = total(fresh * live) / own_count
        local = (fresh - middle) * live
        tell(i + 1, [
            own_count, middle, total(local * local), total(fresh * dir_o), total(fresh * res_w),
            total(fresh * dir_w), total(dir_o * res_w), total(fresh * ans_w),
            total(dir_o * ans_w), total(ans_o * ans_w),
        ])
        mean, spread, found = hear(i + 1, 10)
        res_o = (fresh - mean) * live
        _, _, res_res, res_dir, resid_next, res_dirw, dir_resw, res_ans, dir_ans, ans_ans = found
        res_res = res_res + spread
        ratio = resid_next / resid_sq
        new_dir = res_res + 2.0 * ratio * res_dir + ratio * ratio * dir_dir
        new_wgt = resid_next + ratio * (res_dirw + dir_resw) + ratio * ratio * dir_wgt
        mixed = res_ans + ratio * dir_ans
        dir_w = res_w + ratio * dir_w
        dir_o = res_o + ratio * dir_o
        dir_c = [r + ratio * d for r, d in zip(res_c, dir_c)]
        dir_dir, dir_wgt, resid_sq = new_dir, new_wgt, resid_next
        step = resid_sq / (dir_dir + DIAG_SHIFT * dir_wgt)
        norm = (ans_ans + 2.0 * step * mixed + step * step * dir_wgt) / sample_total
        ans_w, ans_o = ans_w + step * dir_w, ans_o + step * dir_o
        ans_c = [a + step * d for a, d in zip(ans_c, dir_c)]
    params = N_SITES * HIDDEN_SIZE + HIDDEN_SIZE + N_SITES
    scale = lax.rsqrt(norm / params + EPSILON)
    own_rows = mat_ref.shape[0]
    picks = lax.broadcasted_iota(jnp.int32, (MIN_ROWS, sites), 0) + me * own_rows
    picks = (picks == lax.broadcasted_iota(jnp.int32, (MIN_ROWS, sites), 1)).astype(BF16)
    for i in range(hidden // tile):
        part = slice(i * tile, (i + 1) * tile)
        out = 0.0
        for k in range(ITERS):
            piece = lax.dot_general(
                picks, pulled[k, part, :], (((1,), (1,)), ((), ())), preferred_element_type=F32
            )
            out = out + (ans_c[k] * scale) * piece
        mat_ref[:, part] = out[:own_rows]
    vec = 0.0
    for k in range(ITERS):
        vec = vec + (ans_c[k] * scale) * vecs[k]
    vec_ref[...] = vec


def wide_device(spins, energies, counts, accepted, hidden_bias, weights):
    n_chain = lax.axis_size("chain")
    n_rep = lax.axis_size("rep")
    slots, sites = spins.shape
    hidden = weights.shape[1]
    visible = sites // n_rep
    bits = n_chain.bit_length() - 1
    strands = min(MAX_STRANDS, hidden // 256)
    vec_rows = -(-(hidden // LANES + 1) // 8) * 8
    order = jnp.arange(slots, dtype=jnp.int32)
    names = jnp.where(order < counts[0], accepted[0], -1)
    live = jnp.any(order[:, None] == names[None, :], axis=1).astype(F32)
    vmem = pl.BlockSpec(memory_space=pltpu.VMEM)
    dma = pltpu.SemaphoreType.DMA
    mat, vec = pl.pallas_call(
        functools.partial(wide_kernel, n_chain, n_rep),
        out_shape=(
            jax.ShapeDtypeStruct((sites // n_chain, hidden), F32),
            jax.ShapeDtypeStruct((vec_rows, LANES), F32),
        ),
        in_specs=[vmem] * 6,
        out_specs=(vmem, vmem),
        scratch_shapes=[
            pltpu.VMEM((hidden, slots), BF16),
            pltpu.VMEM((hidden, sites), F32),
            pltpu.VMEM((hidden + strands * MIN_ROWS * bits, sites), BF16),
            pltpu.VMEM((hidden + strands * MIN_ROWS * bits, sites), BF16),
            pltpu.VMEM((ITERS, hidden, sites), BF16),
            pltpu.VMEM((ITERS, vec_rows, LANES), F32),
            pltpu.VMEM((ITERS, bits, vec_rows, LANES), F32),
            pltpu.VMEM((8, slots), F32),
            pltpu.VMEM((ITERS, n_rep, 8, slots), F32),
            pltpu.VMEM((ITERS + 1, n_chain, 8, LANES), F32),
            dma((ITERS, strands * bits)),
            dma((ITERS, strands * bits)),
            dma((ITERS, strands * bits)),
            dma((ITERS, strands * bits)),
            dma((ITERS, bits)),
            dma((ITERS, bits)),
            dma((ITERS, n_rep)),
            dma((ITERS, n_rep)),
            dma((ITERS + 1, n_chain)),
            dma((ITERS + 1, n_chain)),
        ],
        compiler_params=pltpu.CompilerParams(
            collective_id=0, has_side_effects=True, vmem_limit_bytes=60 * 1024 * 1024
        ),
    )(
        spins,
        spins.T,
        weights.T,
        hidden_bias.astype(F32).reshape(hidden // LANES, LANES),
        energies.astype(F32)[None],
        live[None],
    )
    flat = vec.reshape(-1)
    return flat[hidden : hidden + visible], flat[:hidden], mat


VMEM_LIMIT = 60 * 1024 * 1024
TAIL = 16
CORES = 2
PAIR = 2


def line_kernel(
    n_chain, s_ref, w_ref, aux_ref, names_ref, count_ref,
    mat_ref, hid_ref, vis_ref,
    samples, spins_t, acts, acc, hid_acc, bias_col, shift_col, w_t, w_in,
    outbox, inbox, tail_out, tail_in, push_mat, row_weight, partial, part_in, full, energies, tail_sum, flipped, final_in,
    line_send, line_recv, rep_send, rep_recv, sib_send, sib_recv, own_send, own_recv,
    en_send, en_recv, mat_send, mat_recv, tail_send, tail_recv, part_send, part_recv, full_send, full_recv,
    fin_send, fin_recv, load_sem, load_w_sem,
):
    slots, sites = s_ref.shape
    hidden = w_ref.shape[1]
    line = n_chain // (CORES * PAIR)
    blocks = line * CORES
    width = hidden // blocks
    tall = width + TAIL
    half = slots // 2
    half_rows = half // LANES
    tiles = slots // LANES
    piece = min(256, half)
    pieces = half // piece
    members = 2 * blocks
    line_rows = members * 8
    own_sites = mat_ref.shape[0]
    chunks = width // LANES
    sample_total = float(KEEP_DEV * n_chain)
    steps = line - 1
    arrivals = steps * pieces
    long_lag = 2 * pieces - 1

    me = lax.axis_index("chain")
    rep = lax.axis_index("rep")
    core = lax.rem(me, CORES)
    side = lax.rem(me // CORES, PAIR)
    z = me // (CORES * PAIR)
    block = z * CORES + core
    member = block * 2 + rep
    own_tile = side * members + member

    def chain_of(z_, side_, core_):
        return (z_ * PAIR + side_) * CORES + core_

    def device_of(m):
        b = m // 2
        return {"chain": chain_of(b // CORES, side, lax.rem(b, CORES)), "rep": lax.rem(m, 2)}

    everyone = PAIR * members
    load = pltpu.make_async_copy(s_ref, samples.at[block], load_sem)
    load.start()
    columns = pl.ds(pl.multiple_of(block * width, width), width)
    load_w = pltpu.make_async_copy(w_ref.at[:, columns], w_in, load_w_sem)
    load_w.start()
    barrier = pltpu.get_barrier_semaphore()

    def nearest(n):
        below, above = z, line - 1 - z
        near = jnp.minimum(below, above)
        paired = n < 2 * near
        dist = jnp.where(paired, n // 2 + 1, n - near + 1)
        upward = jnp.where(paired, lax.rem(n, 2) == 0, below > above)
        return upward, dist, jnp.where(upward, z - dist, z + dist)

    far_z = [nearest(line - 2 - n)[2] for n in range(line - 1)] + [z]

    def peers():
        for n in range(line):
            for turn in range(8):
                sides, cores, reps = turn < 4, turn % 2 == 0, turn % 4 < 2
                if n == line - 1 and not (sides or cores or reps):
                    continue
                yield (
                    far_z[n],
                    1 - side if sides else side,
                    1 - core if cores else core,
                    1 - rep if reps else rep,
                )

    for at_z, at_side, at_core, at_rep in peers():
        target = {"chain": chain_of(at_z, at_side, at_core), "rep": at_rep}
        pl.semaphore_signal(barrier, inc=1, device_id=target, device_id_type=MESH)

    names = names_ref[...]
    order = lax.broadcasted_iota(jnp.int32, (1, slots), 1)
    names = jnp.where(order < count_ref[0], names, -1)
    tile_no = names // LANES
    row_no = jnp.where(names < 0, -1, tile_no + jnp.where(tile_no >= half_rows, 8 - half_rows, 0))
    row_hot = (lax.broadcasted_iota(jnp.int32, (16, slots), 0) == row_no).astype(F32).astype(BF16)
    low = names - tile_no * LANES
    lane_hot = (lax.broadcasted_iota(jnp.int32, (LANES, slots), 0) == low).astype(F32).astype(BF16)
    live_own = lax.dot_general(
        row_hot, lane_hot, (((1,), (1,)), ((), ())), preferred_element_type=F32
    )
    slot_no = side * blocks + block
    energies[slot_no] = (aux_ref[0:16, :] * live_own).astype(BF16)
    load.wait()
    load_w.wait()
    pl.semaphore_wait(barrier, everyone - 1)

    def batch(place, send, recv):
        return pltpu.make_async_remote_copy(
            src_ref=place,
            dst_ref=place,
            send_sem=send,
            recv_sem=recv,
            device_id={"chain": chain_of(z, side, 1 - core)},
            device_id_type=MESH,
        )

    def part_rows(r, p):
        return pl.ds(pl.multiple_of(r * half + p * piece, piece), piece)

    def line_copy(d, s, p, from_z, to_z):
        place = samples.at[from_z * CORES + core, part_rows(rep, p)]
        return pltpu.make_async_remote_copy(
            src_ref=place,
            dst_ref=place,
            send_sem=line_send.at[d, s, p],
            recv_sem=line_recv.at[d, s, p],
            device_id={"chain": chain_of(to_z, side, core)},
            device_id_type=MESH,
        )

    def own_copy(b):
        return pltpu.make_async_remote_copy(
            src_ref=samples.at[b],
            dst_ref=samples.at[b],
            send_sem=own_send,
            recv_sem=own_recv,
            device_id={"chain": chain_of(z, side, 1 - core)},
            device_id_type=MESH,
        )

    def rep_copy(it, from_z, r, p):
        place = samples.at[from_z * CORES + core, part_rows(r, p)]
        return pltpu.make_async_remote_copy(
            src_ref=place,
            dst_ref=place,
            send_sem=rep_send.at[it],
            recv_sem=rep_recv.at[it],
            device_id={"rep": 1 - rep},
            device_id_type=MESH,
        )

    def sib_copy(kind, it, from_z, c, r, p):
        place = samples.at[from_z * CORES + c, part_rows(r, p)]
        return pltpu.make_async_remote_copy(
            src_ref=place,
            dst_ref=place,
            send_sem=sib_send.at[kind, it],
            recv_sem=sib_recv.at[kind, it],
            device_id={"chain": chain_of(z, side, 1 - core)},
            device_id_type=MESH,
        )

    for at_z, at_side, at_core, at_rep in peers():
        if at_rep is rep:
            pltpu.make_async_remote_copy(
                src_ref=energies.at[slot_no],
                dst_ref=energies.at[slot_no],
                send_sem=en_send,
                recv_sem=en_recv,
                device_id={"chain": chain_of(at_z, at_side, at_core)},
                device_id_type=MESH,
            ).start()

    for p in range(pieces):
        @pl.when(z + 1 < line)
        def _():
            line_copy(0, 0, p, z, z + 1).start()

        @pl.when(z > 0)
        def _():
            line_copy(1, 0, p, z, z - 1).start()
    own_copy(block).start()

    w_t[...] = jnp.transpose(w_in[...])
    for r in range(chunks):
        bias = to_column(aux_ref[pl.ds(16 + block * chunks + r, 1), :])
        bias_col[r * LANES : (r + 1) * LANES, :] = jnp.broadcast_to(bias, (LANES, LANES))
    partial[...] = jnp.zeros_like(partial)
    tail = lax.broadcasted_iota(jnp.int32, (TAIL, slots), 0)
    ones = (tail == 0).astype(F32).astype(BF16)

    @pl.loop(0, blocks)
    def _(j):
        acts[j, width:, :] = ones

    batch(energies.at[pl.ds(0, n_chain - 1)], en_send, en_recv).wait_recv()

    energy = energies[...].astype(F32).reshape(PAIR * line_rows, LANES)
    live = (energy != 0.0).astype(F32)

    def sum_all(values):
        return total(jnp.sum(values, axis=0, keepdims=True))

    centered = (energy - sum_all(energy) / sample_total) * live

    row_weight[...] = centered / sample_total
    acc[...] = jnp.zeros_like(acc)
    hid_acc[...] = jnp.zeros_like(hid_acc)
    tail_lane = lax.broadcasted_iota(jnp.int32, (TAIL, LANES), 0)
    tail_row = lax.broadcasted_iota(jnp.int32, (TAIL, sites), 0)

    def weigh(held, b, r, p, sums):
        parts = []
        for e in range(piece // LANES):
            row = side * line_rows + b * 16 + r * 8 + p * (piece // LANES) + e
            scale = row_weight[pl.ds(row, 1), :]
            scaled = held[:, e * LANES : (e + 1) * LANES].astype(F32) * scale
            sums = sums + scaled
            high = scale.astype(BF16).astype(F32)
            ends = jnp.where(tail_lane == 0, high, jnp.where(tail_lane == 1, scale - high, 0.0))
            parts.append(jnp.concatenate([scaled, ends], axis=0).astype(BF16))
        return parts, sums

    def process(places):
        rows = [samples[b, part_rows(r, p), :] for b, r, p in places]
        got = [jnp.transpose(part) for part in rows]
        bias = jnp.concatenate([bias_col[...]] * (piece // LANES), axis=1)
        found = [
            jnp.tanh(jnp.dot(w_t[...], part, preferred_element_type=F32) + bias).astype(BF16)
            for part in got
        ]
        parts, sums = [], hid_acc[...]
        for (b, r, p), part in zip(places, found):
            more, sums = weigh(part, b, r, p, sums)
            parts += more
        pulled = jnp.dot(
            jnp.concatenate(parts, axis=1),
            jnp.concatenate(rows, axis=0),
            preferred_element_type=F32,
        )
        hid_acc[...] = sums
        acc[...] += pulled
        for (b, r, p), flip, act in zip(places, got, found):
            lanes = pl.ds(pl.multiple_of(r * half + p * piece, piece), piece)
            spins_t[b, :, lanes] = flip
            acts[b, 0:width, lanes] = act

    other = z * CORES + 1 - core
    own_copy(other).wait_recv()

    def arrival(it):
        both = it // pieces < 2 * jnp.minimum(z, line - 1 - z)
        spot = lax.rem(it, 2 * pieces)
        n = jnp.where(both, it // (2 * pieces) * 2 + lax.rem(spot, 2), it // pieces)
        p = jnp.where(both, spot // 2, lax.rem(it, pieces))
        upward, dist, from_z = nearest(n)
        return jnp.where(upward, 0, 1), dist - 1, p, from_z

    lag = jnp.where(jnp.minimum(z, line - 1 - z) > 0, long_lag, pieces - 1)

    @pl.loop(0, arrivals + long_lag + 1)
    def _(it):
        @pl.when(it < arrivals)
        def _():
            d, s, p, from_z = arrival(it)
            line_copy(d, s, p, from_z, z).wait_recv()
            to_z = z + 1 - 2 * d

            @pl.when(jnp.logical_and(to_z >= 0, to_z < line))
            def _():
                line_copy(d, s + 1, p, from_z, to_z).start()

            rep_copy(it, from_z, rep, p).start()
            sib_copy(0, it, from_z, core, rep, p).start()

        fresh = it < pieces
        ripe = jnp.logical_and(it > lag, it <= arrivals + lag)
        last = jnp.clip(it - lag - 1, 0, arrivals - 1)
        _, _, last_p, last_z = arrival(last)
        p = jnp.where(fresh, it, last_p)
        at_z = jnp.where(fresh, z, last_z)
        b = at_z * CORES + core
        other = at_z * CORES + 1 - core

        @pl.when(ripe)
        def _():
            sib_copy(0, last, last_z, 1 - core, rep, p).wait_recv()
            sib_copy(1, last, last_z, 1 - core, 1 - rep, p).wait_recv()

        @pl.when(jnp.logical_or(fresh, ripe))
        def _():
            process([(b, rep, p), (other, rep, p), (b, 1 - rep, p), (other, 1 - rep, p)])

        @pl.when(jnp.logical_and(it >= lag, it < arrivals + lag))
        def _():
            last = it - lag
            _, _, p, from_z = arrival(last)
            rep_copy(last, from_z, 1 - rep, p).wait_recv()
            sib_copy(1, last, from_z, core, 1 - rep, p).start()

    def mat_copy(k):
        return pltpu.make_async_remote_copy(
            src_ref=outbox.at[k],
            dst_ref=inbox.at[k],
            send_sem=mat_send.at[k],
            recv_sem=mat_recv.at[k],
            device_id={"chain": chain_of(z, 1 - side, core)},
            device_id_type=MESH,
        )

    def tail_copy(k):
        return pltpu.make_async_remote_copy(
            src_ref=tail_out.at[k],
            dst_ref=tail_in.at[k],
            send_sem=tail_send.at[k],
            recv_sem=tail_recv.at[k],
            device_id={"chain": chain_of(z, 1 - side, core)},
            device_id_type=MESH,
        )

    def part_copy(k, source, target):
        return pltpu.make_async_remote_copy(
            src_ref=partial.at[k, target],
            dst_ref=part_in.at[k, source],
            send_sem=part_send.at[k],
            recv_sem=part_recv.at[k],
            device_id=device_of(target),
            device_id_type=MESH,
        )

    def part_batch(k):
        return batch(part_in.at[k, pl.ds(0, members - 1)], part_send.at[k], part_recv.at[k])

    def full_batch(k):
        return batch(full.at[k, pl.ds(0, everyone - 1)], full_send.at[k], full_recv.at[k])

    def final_batch(k):
        return batch(final_in.at[k, pl.ds(0, blocks - 1)], fin_send.at[k], fin_recv.at[k])

    def final_start(k):
        for at_z, at_side, at_core, at_rep in peers():
            if at_rep is rep and at_side is side:
                target = chain_of(at_z, side, at_core)
                begin = pl.multiple_of(target * own_sites, own_sites)
                pltpu.make_async_remote_copy(
                    src_ref=flipped.at[k, pl.ds(begin, own_sites)],
                    dst_ref=final_in.at[k, block],
                    send_sem=fin_send.at[k],
                    recv_sem=fin_recv.at[k],
                    device_id={"chain": target},
                    device_id_type=MESH,
                ).start()

    def pull(k, weight):
        row_weight[...] = weight / sample_total
        acc[...] = jnp.zeros_like(acc)
        hid_acc[...] = jnp.zeros_like(hid_acc)

        @pl.loop(0, blocks // 4)
        def _(i):
            sums = hid_acc[...]
            pulled = acc[...]
            for j in (4 * i, 4 * i + 1, 4 * i + 2, 4 * i + 3):
                parts = []
                for r in range(2):
                    for p in range(pieces):
                        begin = r * half + p * piece
                        more, sums = weigh(acts[j, 0:width, begin : begin + piece], j, r, p, sums)
                        parts += more
                pulled = pulled + jnp.dot(
                    jnp.concatenate(parts, axis=1), samples[j], preferred_element_type=F32
                )
            hid_acc[...] = sums
            acc[...] = pulled

    def apply(k, meanwhile):
        sums = jnp.sum(hid_acc[...], axis=1, keepdims=True)
        hid_row = jnp.concatenate(
            [to_row(sums[r * LANES : (r + 1) * LANES]) for r in range(chunks)], axis=1
        )
        if width < sites:
            hid_row = jnp.concatenate([hid_row, jnp.zeros((1, sites - width), F32)], axis=1)
        vis_row = acc[width : width + 1, :] + acc[width + 1 : width + 2, :]
        outbox[k] = acc[0:width, :].astype(BF16)
        tail_out[k] = jnp.concatenate([vis_row, hid_row, jnp.zeros((6, sites), F32)], axis=0)
        tail_copy(k).start()
        mat_copy(k).start()
        meanwhile()
        mat_copy(k).wait()
        tail_copy(k).wait()
        whole = outbox[k].astype(F32) + inbox[k].astype(F32)
        rest = tail_out[k] + tail_in[k]
        tail_sum[k] = rest
        push_mat[0:width, :] = whole.astype(BF16)
        rest = jnp.concatenate([rest, jnp.zeros((TAIL - 8, sites), F32)], axis=0)
        push_mat[width:, :] = jnp.where(tail_row == 0, rest / members, 0.0).astype(BF16)
        for r in range(chunks):
            shift = to_column(rest[1:2, r * LANES : (r + 1) * LANES])
            shift_col[r * LANES : (r + 1) * LANES, :] = jnp.broadcast_to(shift, (LANES, LANES))
        shift_col[width:, :] = jnp.zeros((TAIL, LANES), F32)

        @pl.loop(0, members)
        def _(i):
            turn = lax.rem(i, 4)
            _, _, far_z = nearest(jnp.maximum(line - 2 - i // 4, 0))
            at_z = jnp.where(i // 4 == line - 1, z, far_z)
            at_core = lax.rem(core + jnp.where(lax.rem(turn, 2) == 0, 1, 0), CORES)
            at_rep = lax.rem(rep + jnp.where(turn < 2, 1, 0), 2)
            j = at_z * CORES + at_core
            target = j * 2 + at_rep
            shift = shift_col[...]
            for p in range(pieces):
                begin = at_rep * half + p * piece
                mixture = jnp.dot(
                    push_mat[...],
                    spins_t[j, :, pl.ds(pl.multiple_of(begin, piece), piece)],
                    preferred_element_type=F32,
                )
                for e in range(piece // LANES):
                    lanes = pl.ds(pl.multiple_of(begin + e * LANES, LANES), LANES)
                    mix = mixture[:, e * LANES : (e + 1) * LANES] + shift
                    mix = mix * acts[j, :, lanes].astype(F32)
                    row = p * (piece // LANES) + e
                    partial[k, target, row : row + 1, :] = jnp.sum(mix, axis=0, keepdims=True)

            @pl.when(i < members - 1)
            def _():
                part_copy(k, member, target).start()

        flipped[k] = jnp.transpose(push_mat[0:width, :])

        final_start(k)
        own_begin = pl.multiple_of(me * own_sites, own_sites)
        final_in[k, block] = flipped[k, pl.ds(own_begin, own_sites), :]
        part_in[k, member] = partial[k, member]

        part_batch(k).wait_recv()

        full[k, own_tile] = jnp.sum(part_in[k], axis=0)
        for r in range(chunks):
            full[k, own_tile, half_rows + r : half_rows + r + 1, :] = tail_sum[
                k, 1:2, r * LANES : (r + 1) * LANES
            ]

        for at_z, at_side, at_core, at_rep in peers():
            pltpu.make_async_remote_copy(
                src_ref=full.at[k, own_tile],
                dst_ref=full.at[k, own_tile],
                send_sem=full_send.at[k],
                recv_sem=full_recv.at[k],
                device_id={"chain": chain_of(at_z, at_side, at_core), "rep": at_rep},
                device_id_type=MESH,
            ).start()

        full_batch(k).wait_recv()
        return full[k].reshape(PAIR * line_rows, LANES)

    def center(values):
        return (values - sum_all(values * live) / sample_total) * live

    state = {}

    def nothing():
        pass

    def first():
        resid_sq = sum_all(image * centered)
        state["resid_sq"] = resid_sq
        state["dir"] = centered, image, [1.0, 0.0, 0.0]
        state["res"] = centered, image, [1.0, 0.0, 0.0]
        advance(sum_all(image * image), resid_sq, None)

    def advance(dir_dir, dir_wgt, before):
        step = state["resid_sq"] / (dir_dir + DIAG_SHIFT * dir_wgt)
        dir_w, dir_o, dir_c = state["dir"]
        if before is None:
            ans = step * dir_w, step * dir_o, [step * x for x in dir_c]
        else:
            ans_w, ans_o, ans_c = before
            ans = (
                ans_w + step * dir_w,
                ans_o + step * dir_o,
                [a + step * d for a, d in zip(ans_c, dir_c)],
            )
        state["step"], state["ans"] = step, ans

    def follow():
        dir_w, dir_o, _ = state["dir"]
        advance(sum_all(dir_o * dir_o), sum_all(dir_w * dir_o), state["ans"])

    def turn_to(i, raw):
        step = state["step"]
        dir_w, dir_o, dir_c = state["dir"]
        res_w, res_o, res_c = state["res"]
        unit = [1.0 if j == i else 0.0 for j in range(ITERS)]
        res_w = res_w - step * (dir_o + DIAG_SHIFT * dir_w)
        res_c = [r - step * (u + DIAG_SHIFT * d) for r, u, d in zip(res_c, unit, dir_c)]
        res_o = center(res_o - step * (raw + DIAG_SHIFT * dir_o))
        resid_next = sum_all(res_w * res_o)
        ratio = resid_next / state["resid_sq"]
        state["resid_sq"] = resid_next
        state["res"] = res_w, res_o, res_c
        state["dir"] = (
            res_w + ratio * dir_w,
            res_o + ratio * dir_o,
            [r + ratio * d for r, d in zip(res_c, dir_c)],
        )

    image = center(apply(0, nothing))
    pull(1, image)
    raw = apply(1, first)
    for i in range(1, ITERS):
        turn_to(i, raw)
        if i + 1 < ITERS:
            pull(i + 1, state["dir"][1])
            raw = apply(i + 1, follow)
        else:
            follow()
    ans_w, ans_o, ans_c = state["ans"]
    norm = sum_all(ans_w * ans_o) / sample_total
    params = N_SITES * HIDDEN_SIZE + HIDDEN_SIZE + N_SITES
    scale = lax.rsqrt(norm / params + EPSILON)
    mix_c = [c * scale for c in ans_c]

    for k in range(ITERS):
        final_batch(k).wait_recv()

    answer = 0.0
    for k in range(ITERS):
        answer = answer + mix_c[k] * tail_sum[k]
    for b in range(blocks):
        out = 0.0
        for k in range(ITERS):
            out = out + mix_c[k] * final_in[k, b].astype(F32)
        mat_ref[:, b * width : (b + 1) * width] = out
        out = 0.0
        for k in range(ITERS):
            out = out + mix_c[k] * full[k, side * members + 2 * b + rep]
        hid_ref[b * chunks : (b + 1) * chunks, :] = out[half_rows : half_rows + chunks]
    visible = sites // 2
    vis_row = answer[0:1, :]
    vis_ref[...] = jnp.where(rep == 0, vis_row[:, :visible], vis_row[:, visible:])

    @pl.loop(0, arrivals)
    def _(it):
        _, _, p, from_z = arrival(it)
        rep_copy(it, from_z, rep, p).wait_send()
        sib_copy(0, it, from_z, core, rep, p).wait_send()
        sib_copy(1, it, from_z, core, 1 - rep, p).wait_send()

    for s in range(steps):
        for p in range(pieces):
            @pl.when(jnp.logical_and(z + 1 < line, z - s >= 0))
            def _():
                line_copy(0, s, p, z - s, z + 1).wait_send()

            @pl.when(jnp.logical_and(z > 0, z + s < line))
            def _():
                line_copy(1, s, p, z + s, z - 1).wait_send()
    own_copy(block).wait_send()

    batch(energies.at[pl.ds(0, n_chain - 1)], en_send, en_recv).wait_send()
    for k in range(ITERS):
        final_batch(k).wait_send()
        part_batch(k).wait_send()
        full_batch(k).wait_send()


def line_fits(n_chain, n_rep, slots, sites, hidden):
    blocks = n_chain // PAIR
    if n_rep != 2 or n_chain % (CORES * PAIR) or n_chain < 2 * CORES * PAIR:
        return False
    if blocks % 4 or hidden % (blocks * LANES) or sites != 2 * LANES or hidden // blocks > sites:
        return False
    half = slots // 2
    if slots % (2 * LANES) or half % min(256, half) or sites % (16 * n_chain):
        return False
    if half // LANES + hidden // blocks // LANES > 8:
        return False
    held = 2 * blocks * slots * (2 * sites + hidden // blocks + TAIL)
    return 2 * held < VMEM_LIMIT


def per_device(spins, energies, counts, accepted, hidden_bias, weights):
    n_chain = lax.axis_size("chain")
    n_rep = lax.axis_size("rep")
    slots, sites = spins.shape
    hidden = weights.shape[1]
    if not line_fits(n_chain, n_rep, slots, sites, hidden):
        return wide_device(spins, energies, counts, accepted, hidden_bias, weights)
    blocks = n_chain // PAIR
    line = blocks // CORES
    width = hidden // blocks
    tall = width + TAIL
    half = slots // 2
    pieces = half // min(256, half)
    arrivals = (line - 1) * pieces
    members = 2 * blocks
    rows = PAIR * members
    own_sites = sites // n_chain
    energy = energies.astype(F32).reshape(2, half // LANES, LANES)
    energy = jnp.pad(energy, ((0, 0), (0, 8 - half // LANES), (0, 0))).reshape(16, LANES)
    aux = jnp.concatenate([energy, hidden_bias.astype(F32).reshape(hidden // LANES, LANES)], axis=0)
    vmem = pl.BlockSpec(memory_space=pltpu.VMEM)
    dma = pltpu.SemaphoreType.DMA
    mat, hid, vis = pl.pallas_call(
        functools.partial(line_kernel, n_chain),
        out_shape=(
            jax.ShapeDtypeStruct((own_sites, hidden), F32),
            jax.ShapeDtypeStruct((hidden // LANES, LANES), F32),
            jax.ShapeDtypeStruct((1, sites // 2), F32),
        ),
        in_specs=[pl.BlockSpec(memory_space=pl.ANY)] * 2 + [vmem] * 2 + [pl.BlockSpec(memory_space=pltpu.SMEM)],
        out_specs=(vmem, vmem, vmem),
        scratch_shapes=[
            pltpu.VMEM((blocks, slots, sites), BF16),
            pltpu.VMEM((blocks, sites, slots), BF16),
            pltpu.VMEM((blocks, tall, slots), BF16),
            pltpu.VMEM((tall, sites), F32),
            pltpu.VMEM((width, LANES), F32),
            pltpu.VMEM((width, LANES), F32),
            pltpu.VMEM((tall, LANES), F32),
            pltpu.VMEM((width, sites), BF16),
            pltpu.VMEM((sites, width), BF16),
            pltpu.VMEM((ITERS, width, sites), BF16),
            pltpu.VMEM((ITERS, width, sites), BF16),
            pltpu.VMEM((ITERS, 8, sites), F32),
            pltpu.VMEM((ITERS, 8, sites), F32),
            pltpu.VMEM((tall, sites), BF16),
            pltpu.VMEM((rows * 8, LANES), F32),
            pltpu.VMEM((ITERS, members, 8, LANES), F32),
            pltpu.VMEM((ITERS, members, 8, LANES), F32),
            pltpu.VMEM((ITERS, rows, 8, LANES), F32),
            pltpu.VMEM((n_chain, 16, LANES), BF16),
            pltpu.VMEM((ITERS, 8, sites), F32),
            pltpu.VMEM((ITERS, sites, width), BF16),
            pltpu.VMEM((ITERS, blocks, own_sites, width), BF16),
            dma((2, line - 1, pieces)),
            dma((2, line - 1, pieces)),
            dma((arrivals,)),
            dma((arrivals,)),
            dma((2, arrivals)),
            dma((2, arrivals)),
            dma,
            dma,
            dma,
            dma,
            dma((ITERS,)),
            dma((ITERS,)),
            dma((ITERS,)),
            dma((ITERS,)),
            dma((ITERS,)),
            dma((ITERS,)),
            dma((ITERS,)),
            dma((ITERS,)),
            dma((ITERS,)),
            dma((ITERS,)),
            dma,
            dma,
        ],
        compiler_params=pltpu.CompilerParams(
            collective_id=0, has_side_effects=True, vmem_limit_bytes=VMEM_LIMIT
        ),
    )(spins, weights, aux, accepted, counts)
    return vis.reshape(-1), hid.reshape(-1), mat


def solution(mesh):
    in_specs = (
        P("chain", None),
        P("chain"),
        P("chain"),
        P("chain", None),
        P("rep"),
        P(None, "rep"),
    )
    out_specs = (P("rep"), P("rep"), P("chain", "rep"))
    return jax.shard_map(
        per_device, mesh=mesh, in_specs=in_specs, out_specs=out_specs, check_vma=False
    )
```

```python
import functools

import jax
import jax.numpy as jnp
from jax import lax
from jax.experimental import pallas as pl
from jax.experimental.pallas import tpu as pltpu
from jax.sharding import PartitionSpec as P

N_SITES = 256
HIDDEN_SIZE = 4096
KEEP_DEV = 768
ITERS = 3

DIAG_SHIFT = 0.05
EPSILON = 1e-06
LANES = 128
MAX_STRANDS = 4
MIN_ROWS = 16
MESH = pl.DeviceIdType.MESH
F32 = jnp.float32
BF16 = jnp.bfloat16


def to_row(column):
    return jnp.transpose(jnp.broadcast_to(column, (LANES, LANES)))[:1, :]


def to_column(row):
    return jnp.transpose(jnp.broadcast_to(row, (LANES, LANES)))[:, :1]


def bit_order(strand, bits):
    rest = list(range(1, bits - 1))
    turn = strand % len(rest)
    return [0] + rest[turn:] + rest[:turn] + [bits - 1]


def total(values):
    return jnp.sum(values, axis=1, keepdims=True)


def wide_kernel(
    n_chain, n_rep, s_ref, st_ref, wt_ref, bias_ref, energy_ref, live_ref,
    mat_ref, vec_ref, acts, acc, outbox, inbox, pulled, vecs, vec_in, rowsum, rows, gathered,
    mat_send, mat_recv, back_send, back_recv, vec_send, vec_recv, row_send, row_recv,
    tell_send, tell_recv,
):
    slots, sites = s_ref.shape
    hidden = wt_ref.shape[0]
    visible = sites // n_rep
    sample_total = float(KEEP_DEV * n_chain)
    bits = n_chain.bit_length() - 1
    strands = min(MAX_STRANDS, hidden // 256)
    tile = min(256, hidden // (2 * strands))
    chunks = tile // LANES
    vis_row = hidden // LANES
    me = lax.axis_index("chain")
    rep = lax.axis_index("rep")
    lane = lax.broadcasted_iota(jnp.int32, (1, LANES), 1)

    barrier = pltpu.get_barrier_semaphore()

    @pl.loop(1, n_chain)
    def _(k):
        pl.semaphore_signal(
            barrier, inc=1, device_id={"chain": lax.rem(me + k, n_chain)}, device_id_type=MESH
        )

    for k in range(1, n_rep):
        pl.semaphore_signal(
            barrier, inc=1, device_id={"rep": lax.rem(rep + k, n_rep)}, device_id_type=MESH
        )
    pl.semaphore_wait(barrier, n_chain - 1 + n_rep - 1)

    def tell_copy(sync, source, target):
        return pltpu.make_async_remote_copy(
            src_ref=gathered.at[sync, source],
            dst_ref=gathered.at[sync, source],
            send_sem=tell_send.at[sync, target],
            recv_sem=tell_recv.at[sync, source],
            device_id={"chain": target},
            device_id_type=MESH,
        )

    def tell(sync, values):
        packed = jnp.zeros((1, LANES), F32)
        for j, value in enumerate(values):
            packed = jnp.where(lane == j, value, packed)
        weight = jnp.broadcast_to(values[0], (1, LANES))
        middle = jnp.broadcast_to(values[1], (1, LANES))
        blank = jnp.zeros((5, LANES), F32)
        gathered[sync, me] = jnp.concatenate([packed, weight, middle, blank], axis=0)

        @pl.loop(1, n_chain)
        def _(k):
            tell_copy(sync, me, lax.rem(me + k, n_chain)).start()

    def hear(sync, count):
        @pl.loop(1, n_chain)
        def _(k):
            tell_copy(sync, lax.rem(me + k, n_chain), lax.rem(me + k, n_chain)).wait_recv()

        @pl.loop(1, n_chain)
        def _(k):
            tell_copy(sync, me, lax.rem(me + k, n_chain)).wait_send()

        everyone = [gathered[sync, j] for j in range(n_chain)]
        packed = everyone[0][0:1]
        weighted = everyone[0][1:2] * everyone[0][2:3]
        for one in everyone[1:]:
            packed = packed + one[0:1]
            weighted = weighted + one[1:2] * one[2:3]
        mean = weighted / sample_total
        spread = jnp.zeros((1, LANES), F32)
        for one in everyone:
            spread = spread + one[1:2] * (one[2:3] - mean) * (one[2:3] - mean)
        found = [total(jnp.where(lane == j, packed, 0.0)) for j in range(count)]
        return mean[:, :1], spread[:, :1], found

    vecs[...] = jnp.zeros_like(vecs)
    live = live_ref[...]
    own_count = total(live)
    energy = energy_ref[...]
    tell(0, [own_count, total(energy * live) / own_count])

    @pl.loop(0, hidden // tile)
    def _(i):
        part = pl.ds(pl.multiple_of(i * tile, tile), tile)
        preact = jnp.dot(wt_ref[part, :], st_ref[...], preferred_element_type=F32)
        bias = [to_column(bias_ref[pl.ds(i * chunks + r, 1), :]) for r in range(chunks)]
        acts[part, :] = jnp.tanh(preact + jnp.concatenate(bias, axis=0)).astype(BF16)

    mean_energy, _, _ = hear(0, 0)
    centered = (energy - mean_energy) * live

    own_visible = pl.ds(pl.multiple_of(rep * visible, visible), visible)

    def pull_tiles(k, first, count, row_weight):
        @pl.loop(0, count)
        def _(i):
            begin = first + i * tile
            part = pl.ds(pl.multiple_of(begin, tile), tile)
            weighted = acts[part, :].astype(F32) * row_weight
            sums = jnp.sum(weighted, axis=1, keepdims=True)
            for r in range(chunks):
                row = to_row(sums[r * LANES : (r + 1) * LANES])
                vecs[k, pl.ds(begin // LANES + r, 1), :] = row
            acc[part, :] = jnp.dot(
                weighted.astype(BF16), s_ref[...], preferred_element_type=F32
            )

    def peer(b):
        digit = lax.rem(me // (2**b), 2)
        return digit, me + (1 - 2 * digit) * (2**b)

    def push_tiles(k, first, count):
        @pl.loop(0, count)
        def _(i):
            begin = first + i * tile
            part = pl.ds(pl.multiple_of(begin, tile), tile)
            mixture = jnp.dot(pulled[k, part, :], st_ref[...], preferred_element_type=F32)
            shift = [to_column(vecs[k, pl.ds(begin // LANES + r, 1), :]) for r in range(chunks)]
            mixture = mixture + jnp.concatenate(shift, axis=0)
            product = mixture * acts[part, :].astype(F32)
            rowsum[...] += jnp.sum(product.reshape(tile // 8, 8, slots), axis=0)

    def apply(k, row_weight):
        row_weight = row_weight / sample_total
        sums = jnp.sum(st_ref[own_visible, :].astype(F32) * row_weight, axis=1, keepdims=True)
        if visible < LANES:
            sums = jnp.concatenate([sums, jnp.zeros((LANES - visible, 1), F32)], axis=0)
        vecs[k, vis_row : vis_row + 1, :] = to_row(sums)

        rowsum[...] = jnp.zeros_like(rowsum)

        def mat_copy(source, target, sends, recvs, slot, partner):
            return pltpu.make_async_remote_copy(
                src_ref=source,
                dst_ref=target,
                send_sem=sends.at[k, slot],
                recv_sem=recvs.at[k, slot],
                device_id={"chain": partner},
                device_id_type=MESH,
            )

        def strand(c, order):
            size = hidden // strands
            start, place = c * size, c * (size + MIN_ROWS * bits)
            steps = []
            for b in order:
                digit, partner = peer(b)
                split = size // 2 >= MIN_ROWS
                moved = size // 2 if split else size
                away = start + (1 - digit) * moved if split else start
                keep = start + digit * moved if split else start
                away = pl.multiple_of(away, moved)
                keep = pl.multiple_of(keep, moved)
                if b == order[0]:
                    pull_tiles(k, away, moved // tile, row_weight)
                outbox[pl.ds(place, moved), :] = acc[pl.ds(away, moved), :].astype(BF16)
                box = pl.ds(place, moved)
                send = mat_copy(
                    outbox.at[box], inbox.at[box], mat_send, mat_recv, c * bits + b, partner
                )
                send.start()
                yield
                if b == order[0]:
                    pull_tiles(k, keep, moved // tile, row_weight)
                send.wait()
                own = acc[pl.ds(keep, moved), :]
                if not split:
                    own = own.astype(BF16).astype(F32)
                acc[pl.ds(keep, moved), :] = own + inbox[box, :].astype(F32)
                place += moved
                start, size = keep, moved
                steps.append((b, partner, split, keep, moved))
            pulled[k, pl.ds(start, size), :] = acc[pl.ds(start, size), :].astype(BF16)
            for b, partner, split, keep, moved in reversed(steps):
                if not split:
                    continue
                part = pulled.at[k, pl.ds(pl.multiple_of(keep, moved), moved)]
                send = mat_copy(part, part, back_send, back_recv, c * bits + b, partner)
                send.start()
                yield
                if b == order[0]:
                    push_tiles(k, keep, moved // tile)
                    yield
                send.wait()
                if b == order[0]:
                    other = 2 * c * (hidden // strands) + hidden // strands - moved - keep
                    push_tiles(k, other, moved // tile)

        def vec_strand():
            yield
            for b in range(bits):
                spread = pltpu.make_async_remote_copy(
                    src_ref=vecs.at[k],
                    dst_ref=vec_in.at[k, b],
                    send_sem=vec_send.at[k, b],
                    recv_sem=vec_recv.at[k, b],
                    device_id={"chain": peer(b)[1]},
                    device_id_type=MESH,
                )
                spread.start()
                yield
                spread.wait()
                vecs[k] = vecs[k] + vec_in[k, b]

        active = [strand(c, bit_order(c, bits)) for c in range(strands)] + [vec_strand()]
        while active:
            active = [one for one in active if next(one, active) is not active]
        seen = jnp.sum(rowsum[...], axis=0, keepdims=True)
        effect = to_column(vecs[k, vis_row : vis_row + 1, :])[:visible]
        seen = seen + jnp.sum(st_ref[own_visible, :].astype(F32) * effect, axis=0, keepdims=True)
        rows[k, rep, 0:1, :] = seen

        def row_copy(source, target):
            return pltpu.make_async_remote_copy(
                src_ref=rows.at[k, source, pl.ds(0, 1)],
                dst_ref=rows.at[k, source, pl.ds(0, 1)],
                send_sem=row_send.at[k, target],
                recv_sem=row_recv.at[k, source],
                device_id={"rep": target},
                device_id_type=MESH,
            )

        others = [lax.rem(rep + d, n_rep) for d in range(1, n_rep)]
        for other in others:
            row_copy(rep, other).start()
        for other in others:
            row_copy(other, other).wait_recv()
        for other in others:
            row_copy(rep, other).wait_send()
        whole = rows[k, 0, 0:1, :]
        for j in range(1, n_rep):
            whole = whole + rows[k, j, 0:1, :]
        return whole * live

    raw = apply(0, centered)
    middle = total(raw) / own_count
    local = (raw - middle) * live
    tell(1, [own_count, middle, total(local * local), total(raw * centered)])
    mean, spread, found = hear(1, 4)
    image = (raw - mean) * live
    dir_dir = found[2] + spread
    dir_wgt = found[3]
    resid_sq = dir_wgt
    dir_w, dir_o, dir_c = centered, image, [1.0, 0.0, 0.0]
    res_w, res_o, res_c = centered, image, [1.0, 0.0, 0.0]
    step = resid_sq / (dir_dir + DIAG_SHIFT * dir_wgt)
    ans_w, ans_o = step * dir_w, step * dir_o
    ans_c = [step * x for x in dir_c]
    norm = None
    for i in range(1, ITERS):
        raw = apply(i, dir_o)
        unit = [1.0 if j == i else 0.0 for j in range(ITERS)]
        res_w = res_w - step * (dir_o + DIAG_SHIFT * dir_w)
        res_c = [r - step * (u + DIAG_SHIFT * d) for r, u, d in zip(res_c, unit, dir_c)]
        fresh = res_o - step * (raw + DIAG_SHIFT * dir_o)
        middle = total(fresh * live) / own_count
        local = (fresh - middle) * live
        tell(i + 1, [
            own_count, middle, total(local * local), total(fresh * dir_o), total(fresh * res_w),
            total(fresh * dir_w), total(dir_o * res_w), total(fresh * ans_w),
            total(dir_o * ans_w), total(ans_o * ans_w),
        ])
        mean, spread, found = hear(i + 1, 10)
        res_o = (fresh - mean) * live
        _, _, res_res, res_dir, resid_next, res_dirw, dir_resw, res_ans, dir_ans, ans_ans = found
        res_res = res_res + spread
        ratio = resid_next / resid_sq
        new_dir = res_res + 2.0 * ratio * res_dir + ratio * ratio * dir_dir
        new_wgt = resid_next + ratio * (res_dirw + dir_resw) + ratio * ratio * dir_wgt
        mixed = res_ans + ratio * dir_ans
        dir_w = res_w + ratio * dir_w
        dir_o = res_o + ratio * dir_o
        dir_c = [r + ratio * d for r, d in zip(res_c, dir_c)]
        dir_dir, dir_wgt, resid_sq = new_dir, new_wgt, resid_next
        step = resid_sq / (dir_dir + DIAG_SHIFT * dir_wgt)
        norm = (ans_ans + 2.0 * step * mixed + step * step * dir_wgt) / sample_total
        ans_w, ans_o = ans_w + step * dir_w, ans_o + step * dir_o
        ans_c = [a + step * d for a, d in zip(ans_c, dir_c)]
    params = N_SITES * HIDDEN_SIZE + HIDDEN_SIZE + N_SITES
    scale = lax.rsqrt(norm / params + EPSILON)
    own_rows = mat_ref.shape[0]
    picks = lax.broadcasted_iota(jnp.int32, (MIN_ROWS, sites), 0) + me * own_rows
    picks = (picks == lax.broadcasted_iota(jnp.int32, (MIN_ROWS, sites), 1)).astype(BF16)
    for i in range(hidden // tile):
        part = slice(i * tile, (i + 1) * tile)
        out = 0.0
        for k in range(ITERS):
            piece = lax.dot_general(
                picks, pulled[k, part, :], (((1,), (1,)), ((), ())), preferred_element_type=F32
            )
            out = out + (ans_c[k] * scale) * piece
        mat_ref[:, part] = out[:own_rows]
    vec = 0.0
    for k in range(ITERS):
        vec = vec + (ans_c[k] * scale) * vecs[k]
    vec_ref[...] = vec


def wide_device(spins, energies, counts, accepted, hidden_bias, weights):
    n_chain = lax.axis_size("chain")
    n_rep = lax.axis_size("rep")
    slots, sites = spins.shape
    hidden = weights.shape[1]
    visible = sites // n_rep
    bits = n_chain.bit_length() - 1
    strands = min(MAX_STRANDS, hidden // 256)
    vec_rows = -(-(hidden // LANES + 1) // 8) * 8
    order = jnp.arange(slots, dtype=jnp.int32)
    names = jnp.where(order < counts[0], accepted[0], -1)
    live = jnp.any(order[:, None] == names[None, :], axis=1).astype(F32)
    vmem = pl.BlockSpec(memory_space=pltpu.VMEM)
    dma = pltpu.SemaphoreType.DMA
    mat, vec = pl.pallas_call(
        functools.partial(wide_kernel, n_chain, n_rep),
        out_shape=(
            jax.ShapeDtypeStruct((sites // n_chain, hidden), F32),
            jax.ShapeDtypeStruct((vec_rows, LANES), F32),
        ),
        in_specs=[vmem] * 6,
        out_specs=(vmem, vmem),
        scratch_shapes=[
            pltpu.VMEM((hidden, slots), BF16),
            pltpu.VMEM((hidden, sites), F32),
            pltpu.VMEM((hidden + strands * MIN_ROWS * bits, sites), BF16),
            pltpu.VMEM((hidden + strands * MIN_ROWS * bits, sites), BF16),
            pltpu.VMEM((ITERS, hidden, sites), BF16),
            pltpu.VMEM((ITERS, vec_rows, LANES), F32),
            pltpu.VMEM((ITERS, bits, vec_rows, LANES), F32),
            pltpu.VMEM((8, slots), F32),
            pltpu.VMEM((ITERS, n_rep, 8, slots), F32),
            pltpu.VMEM((ITERS + 1, n_chain, 8, LANES), F32),
            dma((ITERS, strands * bits)),
            dma((ITERS, strands * bits)),
            dma((ITERS, strands * bits)),
            dma((ITERS, strands * bits)),
            dma((ITERS, bits)),
            dma((ITERS, bits)),
            dma((ITERS, n_rep)),
            dma((ITERS, n_rep)),
            dma((ITERS + 1, n_chain)),
            dma((ITERS + 1, n_chain)),
        ],
        compiler_params=pltpu.CompilerParams(
            collective_id=0, has_side_effects=True, vmem_limit_bytes=60 * 1024 * 1024
        ),
    )(
        spins,
        spins.T,
        weights.T,
        hidden_bias.astype(F32).reshape(hidden // LANES, LANES),
        energies.astype(F32)[None],
        live[None],
    )
    flat = vec.reshape(-1)
    return flat[hidden : hidden + visible], flat[:hidden], mat


VMEM_LIMIT = 60 * 1024 * 1024
TAIL = 16
CORES = 2
PAIR = 2


def line_kernel(
    n_chain, s_ref, w_ref, aux_ref, names_ref, count_ref,
    mat_ref, hid_ref, vis_ref,
    samples, spins_t, acts, acc, hid_acc, bias_col, shift_col, w_t, w_in,
    outbox, inbox, tail_out, tail_in, push_mat, row_weight, partial, part_in, full, energies, tail_sum, flipped, final_in,
    line_send, line_recv, rep_send, rep_recv, sib_send, sib_recv, own_send, own_recv,
    en_send, en_recv, mat_send, mat_recv, tail_send, tail_recv, part_send, part_recv, full_send, full_recv,
    fin_send, fin_recv, load_sem, load_w_sem,
):
    slots, sites = s_ref.shape
    hidden = w_ref.shape[1]
    line = n_chain // (CORES * PAIR)
    blocks = line * CORES
    width = hidden // blocks
    tall = width + TAIL
    half = slots // 2
    half_rows = half // LANES
    tiles = slots // LANES
    piece = min(256, half)
    pieces = half // piece
    members = 2 * blocks
    line_rows = members * 8
    own_sites = mat_ref.shape[0]
    chunks = width // LANES
    sample_total = float(KEEP_DEV * n_chain)
    steps = line - 1
    arrivals = steps * pieces
    long_lag = 2 * pieces - 1

    me = lax.axis_index("chain")
    rep = lax.axis_index("rep")
    core = lax.rem(me, CORES)
    side = lax.rem(me // CORES, PAIR)
    z = me // (CORES * PAIR)
    block = z * CORES + core
    member = block * 2 + rep
    own_tile = side * members + member

    def chain_of(z_, side_, core_):
        return (z_ * PAIR + side_) * CORES + core_

    def device_of(m):
        b = m // 2
        return {"chain": chain_of(b // CORES, side, lax.rem(b, CORES)), "rep": lax.rem(m, 2)}

    everyone = PAIR * members
    load = pltpu.make_async_copy(s_ref, samples.at[block], load_sem)
    load.start()
    columns = pl.ds(pl.multiple_of(block * width, width), width)
    load_w = pltpu.make_async_copy(w_ref.at[:, columns], w_in, load_w_sem)
    load_w.start()
    barrier = pltpu.get_barrier_semaphore()

    def nearest(n):
        below, above = z, line - 1 - z
        near = jnp.minimum(below, above)
        paired = n < 2 * near
        dist = jnp.where(paired, n // 2 + 1, n - near + 1)
        upward = jnp.where(paired, lax.rem(n, 2) == 0, below > above)
        return upward, dist, jnp.where(upward, z - dist, z + dist)

    far_z = [nearest(line - 2 - n)[2] for n in range(line - 1)] + [z]

    def peers():
        for n in range(line):
            for turn in range(8):
                sides, cores, reps = turn < 4, turn % 2 == 0, turn % 4 < 2
                if n == line - 1 and not (sides or cores or reps):
                    continue
                yield (
                    far_z[n],
                    1 - side if sides else side,
                    1 - core if cores else core,
                    1 - rep if reps else rep,
                )

    for at_z, at_side, at_core, at_rep in peers():
        target = {"chain": chain_of(at_z, at_side, at_core), "rep": at_rep}
        pl.semaphore_signal(barrier, inc=1, device_id=target, device_id_type=MESH)

    names = names_ref[...]
    order = lax.broadcasted_iota(jnp.int32, (1, slots), 1)
    names = jnp.where(order < count_ref[0], names, -1)
    tile_no = names // LANES
    row_no = jnp.where(names < 0, -1, tile_no + jnp.where(tile_no >= half_rows, 8 - half_rows, 0))
    row_hot = (lax.broadcasted_iota(jnp.int32, (16, slots), 0) == row_no).astype(F32).astype(BF16)
    low = names - tile_no * LANES
    lane_hot = (lax.broadcasted_iota(jnp.int32, (LANES, slots), 0) == low).astype(F32).astype(BF16)
    live_own = lax.dot_general(
        row_hot, lane_hot, (((1,), (1,)), ((), ())), preferred_element_type=F32
    )
    slot_no = side * blocks + block
    energies[slot_no] = (aux_ref[0:16, :] * live_own).astype(BF16)
    load.wait()
    load_w.wait()
    pl.semaphore_wait(barrier, everyone - 1)

    def batch(place, send, recv):
        return pltpu.make_async_remote_copy(
            src_ref=place,
            dst_ref=place,
            send_sem=send,
            recv_sem=recv,
            device_id={"chain": chain_of(z, side, 1 - core)},
            device_id_type=MESH,
        )

    def part_rows(r, p):
        return pl.ds(pl.multiple_of(r * half + p * piece, piece), piece)

    def line_copy(d, s, p, from_z, to_z):
        place = samples.at[from_z * CORES + core, part_rows(rep, p)]
        return pltpu.make_async_remote_copy(
            src_ref=place,
            dst_ref=place,
            send_sem=line_send.at[d, s, p],
            recv_sem=line_recv.at[d, s, p],
            device_id={"chain": chain_of(to_z, side, core)},
            device_id_type=MESH,
        )

    def own_copy(b):
        return pltpu.make_async_remote_copy(
            src_ref=samples.at[b],
            dst_ref=samples.at[b],
            send_sem=own_send,
            recv_sem=own_recv,
            device_id={"chain": chain_of(z, side, 1 - core)},
            device_id_type=MESH,
        )

    def rep_copy(it, from_z, r, p):
        place = samples.at[from_z * CORES + core, part_rows(r, p)]
        return pltpu.make_async_remote_copy(
            src_ref=place,
            dst_ref=place,
            send_sem=rep_send.at[it],
            recv_sem=rep_recv.at[it],
            device_id={"rep": 1 - rep},
            device_id_type=MESH,
        )

    def sib_copy(kind, it, from_z, c, r, p):
        place = samples.at[from_z * CORES + c, part_rows(r, p)]
        return pltpu.make_async_remote_copy(
            src_ref=place,
            dst_ref=place,
            send_sem=sib_send.at[kind, it],
            recv_sem=sib_recv.at[kind, it],
            device_id={"chain": chain_of(z, side, 1 - core)},
            device_id_type=MESH,
        )

    for at_z, at_side, at_core, at_rep in peers():
        if at_rep is rep:
            pltpu.make_async_remote_copy(
                src_ref=energies.at[slot_no],
                dst_ref=energies.at[slot_no],
                send_sem=en_send,
                recv_sem=en_recv,
                device_id={"chain": chain_of(at_z, at_side, at_core)},
                device_id_type=MESH,
            ).start()

    for p in range(pieces):
        @pl.when(z + 1 < line)
        def _():
            line_copy(0, 0, p, z, z + 1).start()

        @pl.when(z > 0)
        def _():
            line_copy(1, 0, p, z, z - 1).start()
    own_copy(block).start()

    w_t[...] = jnp.transpose(w_in[...])
    for r in range(chunks):
        bias = to_column(aux_ref[pl.ds(16 + block * chunks + r, 1), :])
        bias_col[r * LANES : (r + 1) * LANES, :] = jnp.broadcast_to(bias, (LANES, LANES))
    partial[...] = jnp.zeros_like(partial)
    tail = lax.broadcasted_iota(jnp.int32, (TAIL, slots), 0)
    ones = (tail == 0).astype(F32).astype(BF16)

    @pl.loop(0, blocks)
    def _(j):
        acts[j, width:, :] = ones

    batch(energies.at[pl.ds(0, n_chain - 1)], en_send, en_recv).wait_recv()

    energy = energies[...].astype(F32).reshape(PAIR * line_rows, LANES)
    live = (energy != 0.0).astype(F32)

    def sum_all(values):
        return total(jnp.sum(values, axis=0, keepdims=True))

    centered = (energy - sum_all(energy) / sample_total) * live

    row_weight[...] = centered / sample_total
    acc[...] = jnp.zeros_like(acc)
    hid_acc[...] = jnp.zeros_like(hid_acc)
    tail_lane = lax.broadcasted_iota(jnp.int32, (TAIL, LANES), 0)
    tail_row = lax.broadcasted_iota(jnp.int32, (TAIL, sites), 0)

    def weigh(held, b, r, p, sums):
        parts = []
        for e in range(piece // LANES):
            row = side * line_rows + b * 16 + r * 8 + p * (piece // LANES) + e
            scale = row_weight[pl.ds(row, 1), :]
            scaled = held[:, e * LANES : (e + 1) * LANES].astype(F32) * scale
            sums = sums + scaled
            high = scale.astype(BF16).astype(F32)
            ends = jnp.where(tail_lane == 0, high, jnp.where(tail_lane == 1, scale - high, 0.0))
            parts.append(jnp.concatenate([scaled, ends], axis=0).astype(BF16))
        return parts, sums

    def process(places):
        rows = [samples[b, part_rows(r, p), :] for b, r, p in places]
        got = [jnp.transpose(part) for part in rows]
        bias = jnp.concatenate([bias_col[...]] * (piece // LANES), axis=1)
        found = [
            jnp.tanh(jnp.dot(w_t[...], part, preferred_element_type=F32) + bias).astype(BF16)
            for part in got
        ]
        parts, sums = [], hid_acc[...]
        for (b, r, p), part in zip(places, found):
            more, sums = weigh(part, b, r, p, sums)
            parts += more
        pulled = jnp.dot(
            jnp.concatenate(parts, axis=1),
            jnp.concatenate(rows, axis=0),
            preferred_element_type=F32,
        )
        hid_acc[...] = sums
        acc[...] += pulled
        for (b, r, p), flip, act in zip(places, got, found):
            lanes = pl.ds(pl.multiple_of(r * half + p * piece, piece), piece)
            spins_t[b, :, lanes] = flip
            acts[b, 0:width, lanes] = act

    other = z * CORES + 1 - core
    own_copy(other).wait_recv()

    def arrival(it):
        both = it // pieces < 2 * jnp.minimum(z, line - 1 - z)
        spot = lax.rem(it, 2 * pieces)
        n = jnp.where(both, it // (2 * pieces) * 2 + lax.rem(spot, 2), it // pieces)
        p = jnp.where(both, spot // 2, lax.rem(it, pieces))
        upward, dist, from_z = nearest(n)
        return jnp.where(upward, 0, 1), dist - 1, p, from_z

    lag = jnp.where(jnp.minimum(z, line - 1 - z) > 0, long_lag, pieces - 1)

    @pl.loop(0, arrivals + long_lag + 1)
    def _(it):
        @pl.when(it < arrivals)
        def _():
            d, s, p, from_z = arrival(it)
            line_copy(d, s, p, from_z, z).wait_recv()
            to_z = z + 1 - 2 * d

            @pl.when(jnp.logical_and(to_z >= 0, to_z < line))
            def _():
                line_copy(d, s + 1, p, from_z, to_z).start()

            rep_copy(it, from_z, rep, p).start()
            sib_copy(0, it, from_z, core, rep, p).start()

        fresh = it < pieces
        ripe = jnp.logical_and(it > lag, it <= arrivals + lag)
        last = jnp.clip(it - lag - 1, 0, arrivals - 1)
        _, _, last_p, last_z = arrival(last)
        p = jnp.where(fresh, it, last_p)
        at_z = jnp.where(fresh, z, last_z)
        b = at_z * CORES + core
        other = at_z * CORES + 1 - core

        @pl.when(ripe)
        def _():
            sib_copy(0, last, last_z, 1 - core, rep, p).wait_recv()
            sib_copy(1, last, last_z, 1 - core, 1 - rep, p).wait_recv()

        @pl.when(jnp.logical_or(fresh, ripe))
        def _():
            process([(b, rep, p), (other, rep, p), (b, 1 - rep, p), (other, 1 - rep, p)])

        @pl.when(jnp.logical_and(it >= lag, it < arrivals + lag))
        def _():
            last = it - lag
            _, _, p, from_z = arrival(last)
            rep_copy(last, from_z, 1 - rep, p).wait_recv()
            sib_copy(1, last, from_z, core, 1 - rep, p).start()

    def mat_copy(k):
        return pltpu.make_async_remote_copy(
            src_ref=outbox.at[k],
            dst_ref=inbox.at[k],
            send_sem=mat_send.at[k],
            recv_sem=mat_recv.at[k],
            device_id={"chain": chain_of(z, 1 - side, core)},
            device_id_type=MESH,
        )

    def tail_copy(k):
        return pltpu.make_async_remote_copy(
            src_ref=tail_out.at[k],
            dst_ref=tail_in.at[k],
            send_sem=tail_send.at[k],
            recv_sem=tail_recv.at[k],
            device_id={"chain": chain_of(z, 1 - side, core)},
            device_id_type=MESH,
        )

    def part_copy(k, source, target):
        return pltpu.make_async_remote_copy(
            src_ref=partial.at[k, target],
            dst_ref=part_in.at[k, source],
            send_sem=part_send.at[k],
            recv_sem=part_recv.at[k],
            device_id=device_of(target),
            device_id_type=MESH,
        )

    def part_batch(k):
        return batch(part_in.at[k, pl.ds(0, members - 1)], part_send.at[k], part_recv.at[k])

    def full_batch(k):
        return batch(full.at[k, pl.ds(0, everyone - 1)], full_send.at[k], full_recv.at[k])

    def final_batch(k):
        return batch(final_in.at[k, pl.ds(0, blocks - 1)], fin_send.at[k], fin_recv.at[k])

    def final_start(k):
        for at_z, at_side, at_core, at_rep in peers():
            if at_rep is rep and at_side is side:
                target = chain_of(at_z, side, at_core)
                begin = pl.multiple_of(target * own_sites, own_sites)
                pltpu.make_async_remote_copy(
                    src_ref=flipped.at[k, pl.ds(begin, own_sites)],
                    dst_ref=final_in.at[k, block],
                    send_sem=fin_send.at[k],
                    recv_sem=fin_recv.at[k],
                    device_id={"chain": target},
                    device_id_type=MESH,
                ).start()

    def pull(k, weight):
        row_weight[...] = weight / sample_total

        sums = jnp.zeros((width, LANES), F32)
        pulled = jnp.zeros((tall, sites), F32)
        for j in range(blocks):
            parts = []
            for r in range(2):
                for p in range(pieces):
                    begin = r * half + p * piece
                    more, sums = weigh(acts[j, 0:width, begin : begin + piece], j, r, p, sums)
                    parts += more
            pulled = pulled + jnp.dot(
                jnp.concatenate(parts, axis=1), samples[j], preferred_element_type=F32
            )
        hid_acc[...] = sums
        acc[...] = pulled

    def apply(k, meanwhile):
        outbox[k] = acc[0:width, :].astype(BF16)
        mat_copy(k).start()
        sums = jnp.sum(hid_acc[...], axis=1, keepdims=True)
        hid_row = jnp.concatenate(
            [to_row(sums[r * LANES : (r + 1) * LANES]) for r in range(chunks)], axis=1
        )
        if width < sites:
            hid_row = jnp.concatenate([hid_row, jnp.zeros((1, sites - width), F32)], axis=1)
        vis_row = acc[width : width + 1, :] + acc[width + 1 : width + 2, :]
        tail_out[k] = jnp.concatenate([vis_row, hid_row, jnp.zeros((6, sites), F32)], axis=0)
        tail_copy(k).start()
        meanwhile()
        mat_copy(k).wait()
        tail_copy(k).wait()
        whole = outbox[k].astype(F32) + inbox[k].astype(F32)
        rest = tail_out[k] + tail_in[k]
        tail_sum[k] = rest
        push_mat[0:width, :] = whole.astype(BF16)
        rest = jnp.concatenate([rest, jnp.zeros((TAIL - 8, sites), F32)], axis=0)
        push_mat[width:, :] = jnp.where(tail_row == 0, rest / members, 0.0).astype(BF16)
        for r in range(chunks):
            shift = to_column(rest[1:2, r * LANES : (r + 1) * LANES])
            shift_col[r * LANES : (r + 1) * LANES, :] = jnp.broadcast_to(shift, (LANES, LANES))
        shift_col[width:, :] = jnp.zeros((TAIL, LANES), F32)

        @pl.loop(0, members)
        def _(i):
            turn = lax.rem(i, 4)
            _, _, far_z = nearest(jnp.maximum(line - 2 - i // 4, 0))
            at_z = jnp.where(i // 4 == line - 1, z, far_z)
            at_core = lax.rem(core + jnp.where(lax.rem(turn, 2) == 0, 1, 0), CORES)
            at_rep = lax.rem(rep + jnp.where(turn < 2, 1, 0), 2)
            j = at_z * CORES + at_core
            target = j * 2 + at_rep
            shift = shift_col[...]
            begin = at_rep * half
            mixture = jnp.dot(
                push_mat[...],
                spins_t[j, :, pl.ds(pl.multiple_of(begin, half), half)],
                preferred_element_type=F32,
            )
            for row in range(half_rows):
                lanes = pl.ds(pl.multiple_of(begin + row * LANES, LANES), LANES)
                mix = mixture[:, row * LANES : (row + 1) * LANES] + shift
                mix = mix * acts[j, :, lanes].astype(F32)
                partial[k, target, row : row + 1, :] = jnp.sum(mix, axis=0, keepdims=True)

            @pl.when(i < members - 1)
            def _():
                part_copy(k, member, target).start()

        flipped[k] = jnp.transpose(push_mat[0:width, :])

        final_start(k)
        own_begin = pl.multiple_of(me * own_sites, own_sites)
        final_in[k, block] = flipped[k, pl.ds(own_begin, own_sites), :]
        part_in[k, member] = partial[k, member]

        part_batch(k).wait_recv()

        full[k, own_tile] = jnp.sum(part_in[k], axis=0)
        for r in range(chunks):
            full[k, own_tile, half_rows + r : half_rows + r + 1, :] = tail_sum[
                k, 1:2, r * LANES : (r + 1) * LANES
            ]

        for at_z, at_side, at_core, at_rep in peers():
            pltpu.make_async_remote_copy(
                src_ref=full.at[k, own_tile],
                dst_ref=full.at[k, own_tile],
                send_sem=full_send.at[k],
                recv_sem=full_recv.at[k],
                device_id={"chain": chain_of(at_z, at_side, at_core), "rep": at_rep},
                device_id_type=MESH,
            ).start()

        full_batch(k).wait_recv()
        return full[k].reshape(PAIR * line_rows, LANES)

    def center(values):
        return (values - sum_all(values * live) / sample_total) * live

    state = {}

    def nothing():
        pass

    def first():
        resid_sq = sum_all(image * centered)
        state["resid_sq"] = resid_sq
        state["dir"] = centered, image, [1.0, 0.0, 0.0]
        state["res"] = centered, image, [1.0, 0.0, 0.0]
        advance(sum_all(image * image), resid_sq, None)

    def advance(dir_dir, dir_wgt, before):
        step = state["resid_sq"] / (dir_dir + DIAG_SHIFT * dir_wgt)
        dir_w, dir_o, dir_c = state["dir"]
        if before is None:
            ans = step * dir_w, step * dir_o, [step * x for x in dir_c]
        else:
            ans_w, ans_o, ans_c = before
            ans = (
                ans_w + step * dir_w,
                ans_o + step * dir_o,
                [a + step * d for a, d in zip(ans_c, dir_c)],
            )
        state["step"], state["ans"] = step, ans

    def follow():
        dir_w, dir_o, _ = state["dir"]
        advance(sum_all(dir_o * dir_o), sum_all(dir_w * dir_o), state["ans"])

    def turn_to(i, raw):
        step = state["step"]
        dir_w, dir_o, dir_c = state["dir"]
        res_w, res_o, res_c = state["res"]
        unit = [1.0 if j == i else 0.0 for j in range(ITERS)]
        res_w = res_w - step * (dir_o + DIAG_SHIFT * dir_w)
        res_c = [r - step * (u + DIAG_SHIFT * d) for r, u, d in zip(res_c, unit, dir_c)]
        res_o = center(res_o - step * (raw + DIAG_SHIFT * dir_o))
        resid_next = sum_all(res_w * res_o)
        ratio = resid_next / state["resid_sq"]
        state["resid_sq"] = resid_next
        state["res"] = res_w, res_o, res_c
        state["dir"] = (
            res_w + ratio * dir_w,
            res_o + ratio * dir_o,
            [r + ratio * d for r, d in zip(res_c, dir_c)],
        )

    image = center(apply(0, nothing))
    pull(1, image)
    raw = apply(1, first)
    for i in range(1, ITERS):
        turn_to(i, raw)
        if i + 1 < ITERS:
            pull(i + 1, state["dir"][1])
            raw = apply(i + 1, follow)
        else:
            follow()
    ans_w, ans_o, ans_c = state["ans"]
    norm = sum_all(ans_w * ans_o) / sample_total
    params = N_SITES * HIDDEN_SIZE + HIDDEN_SIZE + N_SITES
    scale = lax.rsqrt(norm / params + EPSILON)
    mix_c = [c * scale for c in ans_c]

    for k in range(ITERS):
        final_batch(k).wait_recv()

    answer = 0.0
    for k in range(ITERS):
        answer = answer + mix_c[k] * tail_sum[k]
    for b in range(blocks):
        out = 0.0
        for k in range(ITERS):
            out = out + mix_c[k] * final_in[k, b].astype(F32)
        mat_ref[:, b * width : (b + 1) * width] = out
        out = 0.0
        for k in range(ITERS):
            out = out + mix_c[k] * full[k, side * members + 2 * b + rep]
        hid_ref[b * chunks : (b + 1) * chunks, :] = out[half_rows : half_rows + chunks]
    visible = sites // 2
    vis_row = answer[0:1, :]
    vis_ref[...] = jnp.where(rep == 0, vis_row[:, :visible], vis_row[:, visible:])

    @pl.loop(0, arrivals)
    def _(it):
        _, _, p, from_z = arrival(it)
        rep_copy(it, from_z, rep, p).wait_send()
        sib_copy(0, it, from_z, core, rep, p).wait_send()
        sib_copy(1, it, from_z, core, 1 - rep, p).wait_send()

    for s in range(steps):
        for p in range(pieces):
            @pl.when(jnp.logical_and(z + 1 < line, z - s >= 0))
            def _():
                line_copy(0, s, p, z - s, z + 1).wait_send()

            @pl.when(jnp.logical_and(z > 0, z + s < line))
            def _():
                line_copy(1, s, p, z + s, z - 1).wait_send()
    own_copy(block).wait_send()

    batch(energies.at[pl.ds(0, n_chain - 1)], en_send, en_recv).wait_send()
    for k in range(ITERS):
        final_batch(k).wait_send()
        part_batch(k).wait_send()
        full_batch(k).wait_send()


def line_fits(n_chain, n_rep, slots, sites, hidden):
    blocks = n_chain // PAIR
    if n_rep != 2 or n_chain % (CORES * PAIR) or n_chain < 2 * CORES * PAIR:
        return False
    if blocks % 4 or hidden % (blocks * LANES) or sites != 2 * LANES or hidden // blocks > sites:
        return False
    half = slots // 2
    if slots % (2 * LANES) or half % min(256, half) or sites % (16 * n_chain):
        return False
    if half // LANES + hidden // blocks // LANES > 8:
        return False
    held = 2 * blocks * slots * (2 * sites + hidden // blocks + TAIL)
    return 2 * held < VMEM_LIMIT


def per_device(spins, energies, counts, accepted, hidden_bias, weights):
    n_chain = lax.axis_size("chain")
    n_rep = lax.axis_size("rep")
    slots, sites = spins.shape
    hidden = weights.shape[1]
    if not line_fits(n_chain, n_rep, slots, sites, hidden):
        return wide_device(spins, energies, counts, accepted, hidden_bias, weights)
    blocks = n_chain // PAIR
    line = blocks // CORES
    width = hidden // blocks
    tall = width + TAIL
    half = slots // 2
    pieces = half // min(256, half)
    arrivals = (line - 1) * pieces
    members = 2 * blocks
    rows = PAIR * members
    own_sites = sites // n_chain
    energy = energies.astype(F32).reshape(2, half // LANES, LANES)
    energy = jnp.pad(energy, ((0, 0), (0, 8 - half // LANES), (0, 0))).reshape(16, LANES)
    aux = jnp.concatenate([energy, hidden_bias.astype(F32).reshape(hidden // LANES, LANES)], axis=0)
    vmem = pl.BlockSpec(memory_space=pltpu.VMEM)
    dma = pltpu.SemaphoreType.DMA
    mat, hid, vis = pl.pallas_call(
        functools.partial(line_kernel, n_chain),
        out_shape=(
            jax.ShapeDtypeStruct((own_sites, hidden), F32),
            jax.ShapeDtypeStruct((hidden // LANES, LANES), F32),
            jax.ShapeDtypeStruct((1, sites // 2), F32),
        ),
        in_specs=[pl.BlockSpec(memory_space=pl.ANY)] * 2 + [vmem] * 2 + [pl.BlockSpec(memory_space=pltpu.SMEM)],
        out_specs=(vmem, vmem, vmem),
        scratch_shapes=[
            pltpu.VMEM((blocks, slots, sites), BF16),
            pltpu.VMEM((blocks, sites, slots), BF16),
            pltpu.VMEM((blocks, tall, slots), BF16),
            pltpu.VMEM((tall, sites), F32),
            pltpu.VMEM((width, LANES), F32),
            pltpu.VMEM((width, LANES), F32),
            pltpu.VMEM((tall, LANES), F32),
            pltpu.VMEM((width, sites), BF16),
            pltpu.VMEM((sites, width), BF16),
            pltpu.VMEM((ITERS, width, sites), BF16),
            pltpu.VMEM((ITERS, width, sites), BF16),
            pltpu.VMEM((ITERS, 8, sites), F32),
            pltpu.VMEM((ITERS, 8, sites), F32),
            pltpu.VMEM((tall, sites), BF16),
            pltpu.VMEM((rows * 8, LANES), F32),
            pltpu.VMEM((ITERS, members, 8, LANES), F32),
            pltpu.VMEM((ITERS, members, 8, LANES), F32),
            pltpu.VMEM((ITERS, rows, 8, LANES), F32),
            pltpu.VMEM((n_chain, 16, LANES), BF16),
            pltpu.VMEM((ITERS, 8, sites), F32),
            pltpu.VMEM((ITERS, sites, width), BF16),
            pltpu.VMEM((ITERS, blocks, own_sites, width), BF16),
            dma((2, line - 1, pieces)),
            dma((2, line - 1, pieces)),
            dma((arrivals,)),
            dma((arrivals,)),
            dma((2, arrivals)),
            dma((2, arrivals)),
            dma,
            dma,
            dma,
            dma,
            dma((ITERS,)),
            dma((ITERS,)),
            dma((ITERS,)),
            dma((ITERS,)),
            dma((ITERS,)),
            dma((ITERS,)),
            dma((ITERS,)),
            dma((ITERS,)),
            dma((ITERS,)),
            dma((ITERS,)),
            dma,
            dma,
        ],
        compiler_params=pltpu.CompilerParams(
            collective_id=0, has_side_effects=True, vmem_limit_bytes=VMEM_LIMIT
        ),
    )(spins, weights, aux, accepted, counts)
    return vis.reshape(-1), hid.reshape(-1), mat


def solution(mesh):
    in_specs = (
        P("chain", None),
        P("chain"),
        P("chain"),
        P("chain", None),
        P("rep"),
        P(None, "rep"),
    )
    out_specs = (P("rep"), P("rep"), P("chain", "rep"))
    return jax.shard_map(
        per_device, mesh=mesh, in_specs=in_specs, out_specs=out_specs, check_vma=False
    )
```
